256 devices in a mesh: seq: 32 (over x, z), tensor: 8 (over y, core).
Axes of the slice: x: 4, y: 4, z: 8, core: 2. Of those that a mesh axis runs over, the one named last changes fastest.
Arguments:
- hidden_in: bfloat16 [8192, 4096], P(('seq', 'tensor')), may hold values from -30 to 30
- prev_amax: float32 [], replicated, may hold values from 5 to 9
- w_x: bfloat16 [4096, 8192], P('seq', 'tensor'), may hold values from -0.09375 to 0.09375
- w_bc: bfloat16 [4096, 8, 2, 128], P('seq', 'tensor'), may hold values from -0.046875 to 0.046875
- w_dt: bfloat16 [4096, 128], P('seq', 'tensor'), may hold values from -0.09375 to 0.09375
- conv_x: float32 [4, 8192], P(None, 'tensor'), may hold values from -4 to 4
- conv_bc: float32 [4, 8, 2, 128], P(None, 'tensor'), may hold values from -4 to 4
- conv_state_x: bfloat16 [3, 8192], P(None, 'tensor'), may hold values from -6 to 6
- conv_state_bc: bfloat16 [3, 8, 2, 128], P(None, 'tensor'), may hold values from -3 to 3
- dt_bias: float32 [128], P('tensor'), may hold values from -2 to 1
- decay_rate: float32 [128], P('tensor'), may hold values from 1.2207031e-05 to 0.12
- skip: float32 [128], P('tensor'), may hold values from 0.5 to 4
- init_state: float32 [128, 64, 128], P('tensor'), may hold values from -48 to 48
- norm_gain: float32 [8192], P('tensor'), may hold values from 0.1 to 1.9
- w_out: bfloat16 [8192, 4096], P('tensor', 'seq'), may hold values from -0.0625 to 0.0625
Outputs:
- layer_out: bfloat16 [8192, 4096], P(('seq', 'tensor'))
- abs_max: float32 [], replicated
The draws below stay inside these ranges and needn't reach their ends.
All inputs are finite; a program needn't handle non-finite values.
Results may differ from the reference program's by a relative error of at most 0.019.
Values may be sent and summed in bfloat16 or wider, within the bound.
A program may use at most 64 MiB of HBM per device.

```python
import math
import jax
import jax.numpy as jnp
from jax import lax

D = 4096
HEADS = 128
HEAD_DIM = 64
STATE = 128
GROUPS = 8
KERNEL = 4
SPAN = 128
TOKENS = 8192
N_TENSOR = 8


def draw_hidden_in(key, part):
    noise_key, scale_key = jax.random.split(key)
    position = jnp.arange(TOKENS, dtype=jnp.float32) / TOKENS
    rising = jnp.exp(jnp.log(3.0) * position)
    roughness = jnp.exp(jax.random.uniform(scale_key, (TOKENS, 1), minval=0.0, maxval=jnp.log(10.0)))
    values = jax.random.truncated_normal(noise_key, -4.0, 4.0, (TOKENS, D))
    return (values * rising[:, None] * roughness * 0.25).astype(jnp.bfloat16)


def draw_decay_rate(key, part):
    pick_key, slow_key, fast_key = jax.random.split(key, 3)
    share = 0.5
    slow_side = jax.random.uniform(pick_key, (HEADS,)) < share
    slow_rate = jnp.exp(jax.random.uniform(slow_key, (HEADS,), minval=jnp.log(0.1 / TOKENS), maxval=jnp.log(1.0 / TOKENS)))
    fast_rate = jnp.exp(jax.random.uniform(fast_key, (HEADS,), minval=jnp.log(0.03), maxval=jnp.log(0.12)))
    return jnp.where(slow_side, slow_rate, fast_rate).astype(jnp.float32)


def level_of(own_key, extent, cuts, smallest, high):
    loudness, own = 1.0, jax.random.fold_in(own_key, 6)
    for dim, shards_of in cuts:
        steps = jnp.exp(jax.random.uniform(jax.random.fold_in(own, dim), (shards_of,), jnp.float32, smallest / len(cuts), high / len(cuts)))
        loudness = loudness * jnp.repeat(steps, extent[dim] // shards_of).reshape([-1 if axis == dim else 1 for axis in range(len(extent))])
    return loudness


def scatter_about(key, shape, deviation, bound, cuts=(), held_as=jnp.bfloat16):
    result = jax.random.normal(key, shape, jnp.float32) * deviation
    if len(cuts) > 0:
        result = level_of(key, shape, cuts, -0.22, 0.18) * result
    return jnp.clip(result, min=-bound, max=bound).astype(held_as)


def setup_inputs(seed: int = 0) -> dict:
    keys = jax.random.split(jax.random.key(seed), 16)
    hidden_in = draw_hidden_in(jax.random.fold_in(keys[15], 71), 0)
    prev_amax = jnp.clip(jax.random.uniform(keys[1], (), jnp.float32, 5.0, 9.0), 5.0, 9.0)
    w_x = scatter_about(keys[2], (D, HEADS * HEAD_DIM), D ** -0.5, 0.09375, ((0, 32), (1, 8)))
    w_bc = scatter_about(keys[3], (D, GROUPS, 2, STATE), (4 * D) ** -0.5, 0.046875, ((0, 32), (1, 8)))
    w_dt = scatter_about(keys[4], (D, HEADS), D ** -0.5, 0.09375, ((0, 32), (1, 8)))
    conv_x = scatter_about(keys[5], (KERNEL, HEADS * HEAD_DIM), 2 ** -0.5, 4.0, ((1, 8),), jnp.float32)
    conv_bc = scatter_about(keys[6], (KERNEL, GROUPS, 2, STATE), 2 ** -0.5, 4.0, ((1, 8),), jnp.float32)
    conv_state_x = scatter_about(keys[7], (KERNEL - 1, HEADS * HEAD_DIM), 1.0, 6.0, ((1, 8),))
    conv_state_bc = scatter_about(keys[8], (KERNEL - 1, GROUPS, 2, STATE), 0.5, 3.0, ((1, 8),))
    dt_bias = jnp.clip(-2.0 + 3.0 * jax.random.uniform(keys[9], (HEADS,), jnp.float32) ** level_of(keys[9], (HEADS,), ((0, 8),), -0.2, 0.2), -2.0, 1.0)
    decay_rate = draw_decay_rate(jax.random.fold_in(keys[15], 71), 0)
    skip = jnp.clip(jnp.exp(math.log(4.0) - 2.0794415 * jax.random.uniform(keys[11], (HEADS,), jnp.float32) ** level_of(keys[11], (HEADS,), ((0, 8),), -0.2, 0.2)), 0.5, 4.0)
    init_state = scatter_about(keys[12], (HEADS, HEAD_DIM, STATE), 8.0, 48.0, ((0, 8),), jnp.float32)
    norm_gain = jnp.clip(1.0 + 0.18 * jax.random.normal(keys[13], (HEADS * HEAD_DIM,), jnp.float32), 0.1, 1.9)
    w_out = scatter_about(keys[14], (HEADS * HEAD_DIM, D), (HEADS * HEAD_DIM) ** -0.5, 0.0625, ((0, 8), (1, 32)))
    return {"hidden_in": hidden_in, "prev_amax": prev_amax, "w_x": w_x, "w_bc": w_bc, "w_dt": w_dt, "conv_x": conv_x, "conv_bc": conv_bc, "conv_state_x": conv_state_x, "conv_state_bc": conv_state_bc, "dt_bias": dt_bias, "decay_rate": decay_rate, "skip": skip, "init_state": init_state, "norm_gain": norm_gain, "w_out": w_out}


epsilon = 1e-05
quant_range = 448.0

def depthwise(before, projected, conv_taps, length):
    extended = jnp.concatenate([before, projected], axis=0)
    summed = conv_taps[0] * extended[0:length]
    for offset in range(1, KERNEL):
        summed = summed + conv_taps[offset] * extended[offset:offset + length]
    return jax.nn.silu(summed).astype(jnp.bfloat16)

def reference(hidden_in, prev_amax, w_x, w_bc, w_dt, conv_x, conv_bc, conv_state_x, conv_state_bc, dt_bias, decay_rate, skip, init_state, norm_gain, w_out):
    abs_max = jnp.max(jnp.abs(hidden_in.astype(jnp.float32)))
    in_scale = prev_amax / quant_range
    scaled = hidden_in.astype(jnp.float32) * (quant_range / prev_amax)
    quant = jnp.clip(scaled, -quant_range, quant_range).astype(jnp.bfloat16)
    bc_width = GROUPS * 2 * STATE
    x_pre = (jnp.dot(quant, w_x, preferred_element_type=jnp.float32) * in_scale).astype(jnp.bfloat16)
    bc_pre = (jnp.dot(quant, w_bc.reshape(D, bc_width), preferred_element_type=jnp.float32) * in_scale).astype(jnp.bfloat16)
    dt_raw = jnp.dot(quant, w_dt, preferred_element_type=jnp.float32) * in_scale
    x_act = depthwise(conv_state_x, x_pre, conv_x, TOKENS)
    bc_act = depthwise(conv_state_bc.reshape(KERNEL - 1, bc_width), bc_pre, conv_bc.reshape(KERNEL, bc_width), TOKENS)
    step_size = jax.nn.softplus(dt_raw + dt_bias)
    blocks = TOKENS // SPAN
    per_group = HEADS // GROUPS
    x_blocks = x_act.reshape(blocks, SPAN, HEADS, HEAD_DIM)
    bc_blocks = bc_act.reshape(blocks, SPAN, GROUPS, 2, STATE)
    step_blocks = step_size.reshape(blocks, SPAN, HEADS)
    cum_blocks = jnp.cumsum(-step_blocks * decay_rate, axis=1)
    index_row = jnp.arange(SPAN, dtype=jnp.int32)
    lower_mask = index_row[:, None] >= index_row[None, :]

    def advance(carried, element):
        x_block, in_map, out_map, step_block, cum_block = element
        in_heads = jnp.repeat(in_map, per_group, axis=1).astype(jnp.float32)
        out_heads = jnp.repeat(out_map, per_group, axis=1).astype(jnp.float32)
        intersection = jnp.einsum('tgn,ugn->gtu', out_map.astype(jnp.float32), in_map.astype(jnp.float32))
        intersection = jnp.repeat(intersection, per_group, axis=0)
        cum_heads = cum_block.T
        log_gap = cum_heads[:, :, None] - cum_heads[:, None, :]
        decay = jnp.exp(jnp.where(lower_mask[None], log_gap, -1e+30))
        weights = (intersection * decay * step_block.T[:, None, :]).astype(jnp.bfloat16)
        x_float = x_block.astype(jnp.float32)
        local_part = jnp.einsum('htu,uhp->thp', weights.astype(jnp.float32), x_float)
        carried_part = jnp.einsum('thn,hpn->thp', out_heads, carried, precision=lax.Precision.HIGHEST) * jnp.exp(cum_block)[:, :, None]
        ssm_out = local_part + carried_part + skip[None, :, None] * x_float
        x_weighted = (x_float * (step_block * jnp.exp(cum_block[-1] - cum_block))[:, :, None]).astype(jnp.bfloat16)
        added = jnp.einsum('uhp,uhn->hpn', x_weighted.astype(jnp.float32), in_heads)
        carried = jnp.exp(cum_block[-1])[:, None, None] * carried + added
        return (carried, ssm_out)
    inputs = (x_blocks, bc_blocks[:, :, :, 0], bc_blocks[:, :, :, 1], step_blocks, cum_blocks)
    unused, outputs = lax.scan(advance, init_state.astype(jnp.float32), inputs)
    ssm_out = outputs.reshape(TOKENS, HEADS * HEAD_DIM)
    mean_sq = lax.optimization_barrier(jnp.mean(ssm_out * ssm_out, axis=1))
    normed = (ssm_out * lax.rsqrt(mean_sq + epsilon)[:, None] * norm_gain).astype(jnp.bfloat16)
    run_width = HEADS * HEAD_DIM // N_TENSOR
    summed = jnp.zeros((TOKENS, D), jnp.float32)
    for run_index in range(N_TENSOR):
        partial_out = jnp.dot(normed[:, run_index * run_width:(run_index + 1) * run_width], w_out[run_index * run_width:(run_index + 1) * run_width], preferred_element_type=jnp.float32)
        summed = summed + partial_out.astype(jnp.bfloat16).astype(jnp.float32)
    return (summed.astype(jnp.bfloat16), abs_max)
```

```python
import jax
import jax.numpy as jnp
from jax import lax
from jax.sharding import Mesh
from jax.sharding import PartitionSpec as P
from jax.experimental import pallas as pl
from jax.experimental.pallas import tpu as pltpu

HEADS = 128
HEAD_DIM = 64
STATE = 128
GROUPS = 8
KERNEL = 4
SPAN = 128
SEQ = ("x", "z")
TENSOR = ("y", "c")
SEQ_TENSOR = SEQ + TENSOR


epsilon = 1e-05
quant_range = 448.0


def in_order(parts, dim):
    dims = list(parts.shape[1:])
    dims[dim] *= parts.shape[0]
    return jnp.moveaxis(parts, 0, dim).reshape(dims)


def sent_to_all(shard, axis):
    count = lax.axis_size(axis)
    return lax.all_to_all(
        jnp.broadcast_to(shard[None], (count, *shard.shape)), axis, 0, 0, tiled=True
    )


def gather_directly(shard, axis, dim):
    return in_order(sent_to_all(shard, axis), dim)


def over_copies(shard, axis):
    everything = sent_to_all(shard, axis)
    return jnp.max(everything, axis=0)


def sent_together(arrays, axis, dim, along):
    ends, at = ([], 0)
    for a in arrays[:-1]:
        at += a.shape[along]
        ends.append(at)
    both = jnp.concatenate(arrays, axis=along)
    return tuple(jnp.split(lax.all_gather(both, axis, axis=dim, tiled=True), ends, axis=along))


def from_behind(value, axis, steps):
    count = lax.axis_size(axis)
    first, last = (max(0, -steps), min(count, count - steps))
    return lax.ppermute(value, axis, [(source, source + steps) for source in range(first, last)])


def neutral_like(shard, identity):
    return jax.tree.map(
        lambda a, e: jnp.broadcast_to(jnp.asarray(e, a.dtype), a.shape), shard, identity
    )


def prefix_by_axis(shard, axes, combine, identity):
    before = start = neutral_like(shard, identity)
    total = shard
    for axis in reversed(axes):
        count, here = (lax.axis_size(axis), lax.axis_index(axis))
        pieces = jax.tree.map(
            lambda part, kind: lax.all_gather(part.astype(kind), axis),
            total,
            (jnp.bfloat16, jnp.bfloat16),
        )
        inside, total = (start, start)
        for k in range(count):
            passed = k < here
            total = combine(
                total, jax.tree.map(lambda part, own: part[k].astype(own.dtype), pieces, shard)
            )
            inside = jax.tree.map(lambda new, old: jnp.where(passed, new, old), total, inside)
        before = combine(inside, before)
    return before


def taken_together(shard, axis):
    return sent_to_all(shard, axis).sum(axis=0)


def cut_along(shard, dim, count):
    before, after = (shard.shape[:dim], shard.shape[dim + 1 :])
    return jnp.moveaxis(shard.reshape(*before, count, -1, *after), dim, 0)


def sent_and_summed(shard, axis, dim):
    parts = cut_along(shard, dim, lax.axis_size(axis))
    arrived = lax.all_to_all(parts, axis, split_axis=0, concat_axis=0, tiled=True)
    return arrived.astype(jnp.float32).sum(axis=0)


def depthwise(before, projected, conv_taps, length):
    extended = jnp.concatenate([before, projected], axis=0)
    summed = conv_taps[0] * extended[0:length]
    for offset in range(1, KERNEL):
        summed = summed + conv_taps[offset] * extended[offset : offset + length]
    return jax.nn.silu(summed).astype(jnp.bfloat16)


def combine(earlier, later):
    return (earlier[0] * later[0], later[0][:, None, None] * earlier[1] + later[1])


MESH_ID = pl.DeviceIdType.MESH
NX, NZ, NY, NC = (4, 8, 4, 2)
CHUNKS = (384, 256, 256, 256, 256)
X_ROWS = 1024


def remote(src, dst, send_sem, recv_sem, where):
    return pltpu.make_async_remote_copy(
        src_ref=src,
        dst_ref=dst,
        send_sem=send_sem,
        recv_sem=recv_sem,
        device_id=where,
        device_id_type=MESH_ID,
    )


def greet(peers):
    barrier = pltpu.get_barrier_semaphore()
    for peer in peers:
        pl.semaphore_signal(barrier, inc=1, device_id=peer, device_id_type=MESH_ID)
    pl.semaphore_wait(barrier, len(peers))


def in_projection(
    amax_ref,
    hid_ref,
    wx_ref,
    wbd_ref,
    x_out,
    bc_out,
    dt_out,
    max_out,
    rows,
    quant,
    w0,
    w1,
    w2,
    w3,
    w4,
    stage,
    r1,
    r2,
    own,
    plus,
    minus,
    local_sem,
    hx_send,
    hx_recv,
    hy_send,
    hy_recv,
    z_send,
    z_recv,
    rs_send,
    rs_recv,
):
    x, z, y, c = (lax.axis_index(name) for name in ("x", "z", "y", "c"))
    wbuf = (w0, w1, w2, w3, w4)

    def at(dx=0, dz=0, dy=0, dc=0):
        return (
            lax.rem(x + dx + NX, NX),
            lax.rem(z + dz + NZ, NZ),
            lax.rem(y + dy + NY, NY),
            lax.rem(c + dc, NC),
        )

    def z_rows(dz, low=0, count=128):
        block = lax.rem(z + dz + NZ, NZ)
        return pl.ds(pl.multiple_of(block * 128 + low, count), count)

    def t_rows(dy, dc=0):
        index = lax.rem(y + dy + NY, NY) * NC + lax.rem(c + dc, NC)
        return pl.ds(pl.multiple_of(index * 32, 32), 32)

    def x_of(r):
        return lax.rem(x + r, NX)

    local = []
    for j in range(5):
        src = wbd_ref if j == 0 else wx_ref.at[:, pl.ds(256 * (j - 1), 256)]
        local.append(pltpu.make_async_copy(src, wbuf[j].at[z_rows(0)], local_sem.at[j]))
    local.append(
        pltpu.make_async_copy(
            hid_ref.at[:, pl.ds(pl.multiple_of(x * X_ROWS, X_ROWS), X_ROWS)],
            rows.at[x, t_rows(0)],
            local_sem.at[5],
        )
    )
    for copy in local:
        copy.start()

    greet(
        [
            at(dx=1),
            at(dx=-1),
            at(dx=2),
            at(dz=1),
            at(dz=-1),
            at(dy=1),
            at(dy=-1),
            at(dc=1),
        ]
    )
    for copy in local:
        copy.wait()

    sends = []

    def go(copy):
        copy.start()
        sends.append(copy)

    def z_copy(j, k, d):
        sign = 1 if d == 0 else -1
        if k < 3:
            piece = z_rows(-sign * k)
        else:
            piece = z_rows(-sign * k, 64 * d, 64)
        ref = wbuf[j].at[piece]
        return remote(ref, ref, z_send.at[d, j, k], z_recv.at[d, j, k], at(dz=sign))

    def z_arrived(j, k, d):
        sign = 1 if d == 0 else -1
        if k < 3:
            piece = z_rows(-sign * (k + 1))
        else:
            piece = z_rows(-sign * (k + 1), 64 * d, 64)
        ref = wbuf[j].at[piece]
        remote(ref, ref, z_send.at[d, j, k], z_recv.at[d, j, k], at(dz=sign)).wait_recv()

    def z_step(j, k):
        for d in range(2):
            if k > 0:
                z_arrived(j, k - 1, d)
            if k < 4:
                go(z_copy(j, k, d))

    def hx_copy(r):
        dest = lax.rem(x + NX - r, NX)
        src = hid_ref.at[:, pl.ds(pl.multiple_of(dest * X_ROWS, X_ROWS), X_ROWS)]
        return remote(src, rows.at[x, t_rows(0)], hx_send.at[r], hx_recv.at[r], at(dx=-r))

    def hx_arrived(r):
        ref = rows.at[x_of(r), t_rows(0)]
        remote(ref, ref, hx_send.at[r], hx_recv.at[r], at(dx=r)).wait_recv()

    kind_place = {0: (-1, 0), 1: (1, 0), 2: (2, 0), 3: (0, 1), 4: (-1, 1), 5: (1, 1), 6: (2, 1)}

    def hy_copy(r, kind, src_dy, where):
        ref = rows.at[x_of(r), t_rows(src_dy)]
        return remote(ref, ref, hy_send.at[r, kind], hy_recv.at[r, kind], where)

    def hy_arrived(r, kind):
        dy, dc = kind_place[kind]
        ref = rows.at[x_of(r), t_rows(dy, dc)]
        remote(ref, ref, hy_send.at[r, kind], hy_recv.at[r, kind], at(dc=1)).wait_recv()

    def hy_first(r):
        go(hy_copy(r, 0, 0, at(dy=1)))
        go(hy_copy(r, 1, 0, at(dy=-1)))
        go(hy_copy(r, 3, 0, at(dc=1)))

    def hy_relay(r):
        hy_arrived(r, 0)
        if r in (0, 3):
            go(hy_copy(r, 2, -1, at(dy=1)))
        go(hy_copy(r, 4, -1, at(dc=1)))
        hy_arrived(r, 1)
        if r in (1, 2):
            go(hy_copy(r, 2, 1, at(dy=-1)))
        go(hy_copy(r, 5, 1, at(dc=1)))

    def hy_last(r):
        hy_arrived(r, 2)
        go(hy_copy(r, 6, 2, at(dc=1)))

    largest = jnp.zeros((8, 128), jnp.float32)
    amax = jnp.full((8, 128), amax_ref[0], jnp.float32)
    factor = (quant_range / amax)[0:1, 0:1]
    in_scale = (amax / quant_range)[0:1, 0:1]
    max_out[...] = largest

    def quantized(r):
        for kind in (3, 4, 5, 6):
            hy_arrived(r, kind)
        where = x_of(r)

        def tile(i, carry):
            part = pl.ds(pl.multiple_of(i * 32, 32), 32)
            value = rows[where, part, :].astype(jnp.float32)
            quant[where, part, :] = jnp.clip(
                value * factor, -quant_range, quant_range
            ).astype(jnp.bfloat16)
            top = jnp.max(jnp.abs(value).reshape(4, 8, 1024), axis=0)
            best = top[:, 0:128]
            for lane in range(128, 1024, 128):
                best = jnp.maximum(best, top[:, lane : lane + 128])
            max_out[...] = jnp.maximum(max_out[...], best)
            return carry

        lax.fori_loop(0, 8, tile, 0)

    starts = [0]
    for width in CHUNKS:
        starts.append(starts[-1] + width)

    def cols(j):
        return pl.ds(starts[j], CHUNKS[j])

    def rs_copy(j, name):
        slot, low, dst, dst_low, sign = {
            "two_up": (0, 0, r1, 0, 1),
            "two_down": (0, 128, r1, 128, -1),
            "one_up_b": (1, 128, r2, 128, 1),
            "one_down_a": (2, 0, r2, 256, -1),
            "one_up_a": (1, 0, r2, 0, 1),
            "one_down_b": (2, 128, r2, 384, -1),
        }[name]
        index = RS_NAMES.index(name)
        return remote(
            stage.at[slot, pl.ds(low, 128), cols(j)],
            dst.at[pl.ds(dst_low, 128), cols(j)],
            rs_send.at[j, index],
            rs_recv.at[j, index],
            at(dx=sign),
        )

    def product(j, r):
        return jnp.dot(quant[x_of(r)], wbuf[j][...], preferred_element_type=jnp.float32)

    def rs_multiply(j):
        z_step(j, 4)
        stage[0, :, cols(j)] = product(j, 2).astype(jnp.bfloat16)
        value = product(j, 1)
        plus[:, cols(j)] = value[0:128]
        stage[1, 128:256, cols(j)] = value[128:256].astype(jnp.bfloat16)
        go(rs_copy(j, "two_up"))
        go(rs_copy(j, "two_down"))
        value = product(j, 3)
        minus[:, cols(j)] = value[128:256]
        stage[2, 0:128, cols(j)] = value[0:128].astype(jnp.bfloat16)
        go(rs_copy(j, "one_up_b"))
        own[:, cols(j)] = product(j, 0)
        go(rs_copy(j, "one_down_a"))

    def rs_add(j):
        rs_copy(j, "two_up").wait_recv()
        stage[1, 0:128, cols(j)] = (
            plus[:, cols(j)] + r1[0:128, cols(j)].astype(jnp.float32)
        ).astype(jnp.bfloat16)
        rs_copy(j, "two_down").wait_recv()
        stage[2, 128:256, cols(j)] = (
            minus[:, cols(j)] + r1[128:256, cols(j)].astype(jnp.float32)
        ).astype(jnp.bfloat16)
        go(rs_copy(j, "one_up_a"))
        go(rs_copy(j, "one_down_b"))

    def rs_final(j):
        for name in ("one_up_b", "one_down_a", "one_up_a", "one_down_b"):
            rs_copy(j, name).wait_recv()
        total = (
            own[:, cols(j)]
            + r2[0:256, cols(j)].astype(jnp.float32)
            + r2[256:512, cols(j)].astype(jnp.float32)
        ) * in_scale
        if j == 0:
            bc_out[...] = total[:, 0:256].astype(jnp.bfloat16)
            dt_out[...] = total[:, 256:384]
        else:
            x_out[:, 256 * (j - 1) : 256 * j] = total.astype(jnp.bfloat16)

    z_step(0, 0)
    for r in (1, 3, 2):
        go(hx_copy(r))
    hy_first(0)
    z_step(1, 0)
    for r in (1, 3):
        hx_arrived(r)
        hy_first(r)
    z_step(0, 1)
    hx_arrived(2)
    hy_first(2)
    z_step(2, 0)
    hy_relay(0)
    z_step(1, 1)
    hy_relay(1)
    z_step(0, 2)
    z_step(3, 0)
    hy_relay(3)
    hy_relay(2)
    hy_last(0)
    hy_last(1)
    z_step(2, 1)
    z_step(1, 2)
    hy_last(3)
    hy_last(2)
    z_step(0, 3)
    z_step(4, 0)
    z_step(3, 1)
    for r in (0, 1, 3, 2):
        quantized(r)
    z_step(2, 2)
    z_step(1, 3)
    rs_multiply(0)
    z_step(4, 1)
    z_step(3, 2)
    z_step(2, 3)
    rs_multiply(1)
    rs_add(0)
    z_step(4, 2)
    z_step(3, 3)
    rs_multiply(2)
    rs_add(1)
    z_step(4, 3)
    rs_final(0)
    rs_multiply(3)
    rs_add(2)
    rs_final(1)
    rs_multiply(4)
    rs_add(3)
    rs_final(2)
    rs_add(4)
    rs_final(3)
    rs_final(4)
    for copy in sends:
        copy.wait_send()


RS_NAMES = ("two_up", "two_down", "one_up_b", "one_down_a", "one_up_a", "one_down_b")


def project_in(prev_amax, hidden_in, w_x, w_bc_dt):
    total = sum(CHUNKS)
    any_place = pl.BlockSpec(memory_space=pl.ANY)
    vmem = pl.BlockSpec(memory_space=pltpu.VMEM)
    dma = pltpu.SemaphoreType.DMA
    return pl.pallas_call(
        in_projection,
        name="in_projection",
        out_shape=(
            jax.ShapeDtypeStruct((256, 1024), jnp.bfloat16),
            jax.ShapeDtypeStruct((256, 256), jnp.bfloat16),
            jax.ShapeDtypeStruct((256, 128), jnp.float32),
            jax.ShapeDtypeStruct((8, 128), jnp.float32),
        ),
        in_specs=[pl.BlockSpec(memory_space=pltpu.SMEM), any_place, any_place, any_place],
        out_specs=(vmem, vmem, vmem, vmem),
        scratch_shapes=[
            pltpu.VMEM((4, 256, X_ROWS), jnp.bfloat16),
            pltpu.VMEM((4, 256, X_ROWS), jnp.bfloat16),
            *[pltpu.VMEM((X_ROWS, width), jnp.bfloat16) for width in CHUNKS],
            pltpu.VMEM((3, 256, total), jnp.bfloat16),
            pltpu.VMEM((256, total), jnp.bfloat16),
            pltpu.VMEM((512, total), jnp.bfloat16),
            pltpu.VMEM((256, total), jnp.float32),
            pltpu.VMEM((128, total), jnp.float32),
            pltpu.VMEM((128, total), jnp.float32),
            dma((6,)),
            dma((4,)),
            dma((4,)),
            dma((4, 7)),
            dma((4, 7)),
            dma((2, 5, 4)),
            dma((2, 5, 4)),
            dma((5, 6)),
            dma((5, 6)),
        ],
        compiler_params=pltpu.CompilerParams(
            collective_id=0, has_side_effects=True, vmem_limit_bytes=48 * 2**20
        ),
    )(jnp.reshape(prev_amax, (1,)), hidden_in, w_x, w_bc_dt)


def local(
    hidden_in,
    prev_amax,
    w_x,
    w_bc,
    w_dt,
    conv_x,
    conv_bc,
    conv_state_x,
    conv_state_bc,
    dt_bias,
    decay_rate,
    skip,
    init_state,
    norm_gain,
    w_out,
):
    margin = KERNEL - 1
    leading = lax.axis_index(SEQ) == 0
    row_count = hidden_in.shape[0] * 8
    bc_width = w_bc.shape[1] * w_bc.shape[2] * w_bc.shape[3]
    heads = w_dt.shape[1]
    w_bc_dt = jnp.concatenate(
        [
            jnp.reshape(w_bc, (w_bc.shape[0], bc_width)),
            w_dt,
            jnp.zeros((w_dt.shape[0], 128 - heads), w_dt.dtype),
        ],
        axis=1,
    )
    x_whole, bc_whole, dt_raw, top = project_in(prev_amax, hidden_in, w_x, w_bc_dt)
    dt_raw = dt_raw[:, :heads]
    abs_max = over_copies(jnp.max(top), SEQ)
    state_bc = jnp.reshape(conv_state_bc, (margin, bc_width))
    received = from_behind((x_whole[row_count - margin :], bc_whole[row_count - margin :]), SEQ, 1)
    x_edge = jnp.where(leading, conv_state_x, received[0])
    bc_edge = jnp.where(leading, state_bc, received[1])
    x_act = depthwise(x_edge, x_whole, conv_x, row_count)
    bc_act = depthwise(bc_edge, bc_whole, jnp.reshape(conv_bc, (KERNEL, bc_width)), row_count)
    step_size = jax.nn.softplus(dt_raw + dt_bias)
    heads_here = step_size.shape[1]
    groups_here = w_bc.shape[1]
    per_group = HEADS // GROUPS
    blocks = row_count // SPAN
    x_blocks = x_act.reshape(blocks, SPAN, heads_here, HEAD_DIM)
    bc_blocks = bc_act.reshape(blocks, SPAN, groups_here, 2, STATE)
    in_map = bc_blocks[:, :, :, 0]
    out_map = bc_blocks[:, :, :, 1]
    step_blocks = step_size.reshape(blocks, SPAN, heads_here)
    cum_blocks = jnp.cumsum(-step_blocks * decay_rate, axis=1)
    index_row = jnp.arange(SPAN, dtype=jnp.int32)
    lower_mask = index_row[:, None] >= index_row[None, :]
    intersection = jnp.einsum(
        "ctgn,cugn->cgtu", out_map, in_map, preferred_element_type=jnp.float32
    )
    intersection = jnp.repeat(intersection, per_group, axis=1)
    cum_heads = jnp.transpose(cum_blocks, (0, 2, 1))
    log_gap = cum_heads[:, :, :, None] - cum_heads[:, :, None, :]
    decay = jnp.exp(jnp.where(lower_mask[None, None], log_gap, -1e30))
    step_heads = jnp.transpose(step_blocks, (0, 2, 1))
    weights = (intersection * decay * step_heads[:, :, None, :]).astype(jnp.bfloat16)
    local_part = jnp.einsum(
        "chtu,cuhp->cthp", weights, x_blocks, preferred_element_type=jnp.float32
    )
    last_cum = cum_blocks[:, SPAN - 1, :]
    x_weighted = (
        x_blocks.astype(jnp.float32)
        * (step_blocks * jnp.exp(last_cum[:, None, :] - cum_blocks))[:, :, :, None]
    ).astype(jnp.bfloat16)
    in_heads = jnp.repeat(in_map, per_group, axis=2)
    added = jnp.einsum("cuhp,cuhn->chpn", x_weighted, in_heads, preferred_element_type=jnp.float32)

    def carry_on(carried, element):
        block_decay, block_added = element
        return (block_decay[:, None, None] * carried + block_added, carried)

    empty_state = jnp.zeros((heads_here, HEAD_DIM, STATE), jnp.float32)
    device_state, entering = lax.scan(carry_on, empty_state, (jnp.exp(last_cum), added))
    device_decay = jnp.exp(jnp.sum(last_cum, axis=0))
    seeded = device_state + jnp.where(leading, device_decay[:, None, None] * init_state, 0.0)
    identity = (jnp.ones_like(device_decay), jnp.zeros_like(device_state))
    scanned = prefix_by_axis((device_decay, seeded), SEQ, combine, identity)
    incoming = jnp.where(leading, init_state, scanned[1])
    prefix = jnp.exp(jnp.cumsum(last_cum, axis=0) - last_cum)
    states_in = entering + prefix[:, :, None, None] * incoming[None]
    out_heads = jnp.repeat(out_map, per_group, axis=2).astype(jnp.float32)
    carried_part = (
        jnp.einsum("cthn,chpn->cthp", out_heads, states_in, precision=lax.Precision.HIGHEST)
        * jnp.exp(cum_blocks)[:, :, :, None]
    )
    ssm_out = local_part + carried_part + skip[None, None, :, None] * x_blocks.astype(jnp.float32)
    ssm_out = ssm_out.reshape(row_count, heads_here * HEAD_DIM)
    squares = taken_together(jnp.sum(ssm_out * ssm_out, axis=1), TENSOR)
    mean_sq = squares / (HEADS * HEAD_DIM)
    normed = (ssm_out * lax.rsqrt(mean_sq + epsilon)[:, None] * norm_gain).astype(jnp.bfloat16)
    partial_out = jnp.dot(
        normed, lax.all_gather(w_out, SEQ, axis=1, tiled=True), preferred_element_type=jnp.float32
    )
    layer_out = sent_and_summed(partial_out.astype(jnp.bfloat16), TENSOR, 0).astype(jnp.bfloat16)
    return (layer_out, abs_max)


def solution(mesh):
    finer = Mesh(mesh.devices.reshape(NX, NZ, NY, NC), SEQ_TENSOR)
    return jax.shard_map(
        local,
        mesh=finer,
        in_specs=(
            P(SEQ_TENSOR, None),
            P(),
            P(SEQ, TENSOR),
            P(SEQ, TENSOR, None, None),
            P(SEQ, TENSOR),
            P(None, TENSOR),
            P(None, TENSOR, None, None),
            P(None, TENSOR),
            P(None, TENSOR, None, None),
            P(TENSOR),
            P(TENSOR),
            P(TENSOR),
            P(TENSOR, None, None),
            P(TENSOR),
            P(TENSOR, SEQ),
        ),
        out_specs=(P(SEQ_TENSOR, None), P()),
        check_vma=False,
    )
```

```python
import jax
import jax.numpy as jnp
from jax import lax
from jax.sharding import Mesh
from jax.sharding import PartitionSpec as P
from jax.experimental import pallas as pl
from jax.experimental.pallas import tpu as pltpu

HEADS = 128
HEAD_DIM = 64
STATE = 128
GROUPS = 8
KERNEL = 4
SPAN = 128
SEQ = ("x", "z")
TENSOR = ("y", "c")
SEQ_TENSOR = SEQ + TENSOR


epsilon = 1e-05
quant_range = 448.0


def in_order(parts, dim):
    dims = list(parts.shape[1:])
    dims[dim] *= parts.shape[0]
    return jnp.moveaxis(parts, 0, dim).reshape(dims)


def sent_to_all(shard, axis):
    count = lax.axis_size(axis)
    return lax.all_to_all(
        jnp.broadcast_to(shard[None], (count, *shard.shape)), axis, 0, 0, tiled=True
    )


def gather_directly(shard, axis, dim):
    return in_order(sent_to_all(shard, axis), dim)


def over_copies(shard, axis):
    everything = sent_to_all(shard, axis)
    return jnp.max(everything, axis=0)


def sent_together(arrays, axis, dim, along):
    ends, at = ([], 0)
    for a in arrays[:-1]:
        at += a.shape[along]
        ends.append(at)
    both = jnp.concatenate(arrays, axis=along)
    return tuple(jnp.split(lax.all_gather(both, axis, axis=dim, tiled=True), ends, axis=along))


def from_behind(value, axis, steps):
    count = lax.axis_size(axis)
    first, last = (max(0, -steps), min(count, count - steps))
    return lax.ppermute(value, axis, [(source, source + steps) for source in range(first, last)])


def neutral_like(shard, identity):
    return jax.tree.map(
        lambda a, e: jnp.broadcast_to(jnp.asarray(e, a.dtype), a.shape), shard, identity
    )


def prefix_by_axis(shard, axes, combine, identity):
    before = start = neutral_like(shard, identity)
    total = shard
    for axis in reversed(axes):
        count, here = (lax.axis_size(axis), lax.axis_index(axis))
        pieces = jax.tree.map(
            lambda part, kind: lax.all_gather(part.astype(kind), axis),
            total,
            (jnp.bfloat16, jnp.bfloat16),
        )
        inside, total = (start, start)
        for k in range(count):
            passed = k < here
            total = combine(
                total, jax.tree.map(lambda part, own: part[k].astype(own.dtype), pieces, shard)
            )
            inside = jax.tree.map(lambda new, old: jnp.where(passed, new, old), total, inside)
        before = combine(inside, before)
    return before


def taken_together(shard, axis):
    return sent_to_all(shard, axis).sum(axis=0)


def cut_along(shard, dim, count):
    before, after = (shard.shape[:dim], shard.shape[dim + 1 :])
    return jnp.moveaxis(shard.reshape(*before, count, -1, *after), dim, 0)


def sent_and_summed(shard, axis, dim):
    parts = cut_along(shard, dim, lax.axis_size(axis))
    arrived = lax.all_to_all(parts, axis, split_axis=0, concat_axis=0, tiled=True)
    return arrived.astype(jnp.float32).sum(axis=0)


def depthwise(before, projected, conv_taps, length):
    extended = jnp.concatenate([before, projected], axis=0)
    summed = conv_taps[0] * extended[0:length]
    for offset in range(1, KERNEL):
        summed = summed + conv_taps[offset] * extended[offset : offset + length]
    return jax.nn.silu(summed).astype(jnp.bfloat16)


def combine(earlier, later):
    return (earlier[0] * later[0], later[0][:, None, None] * earlier[1] + later[1])


MESH_ID = pl.DeviceIdType.MESH
NX, NZ, NY, NC = (4, 8, 4, 2)
CHUNKS = (384, 256, 256, 256, 256)
X_ROWS = 1024


def remote(src, dst, send_sem, recv_sem, where):
    return pltpu.make_async_remote_copy(
        src_ref=src,
        dst_ref=dst,
        send_sem=send_sem,
        recv_sem=recv_sem,
        device_id=where,
        device_id_type=MESH_ID,
    )


def greet(peers):
    barrier = pltpu.get_barrier_semaphore()
    for peer in peers:
        pl.semaphore_signal(barrier, inc=1, device_id=peer, device_id_type=MESH_ID)
    pl.semaphore_wait(barrier, len(peers))


def in_projection(
    amax_ref,
    hid_ref,
    wx_ref,
    wbd_ref,
    x_out,
    bc_out,
    dt_out,
    max_out,
    rows,
    quant,
    w0,
    w1,
    w2,
    w3,
    w4,
    stage,
    r1,
    r2,
    own,
    plus,
    minus,
    local_sem,
    hx_send,
    hx_recv,
    hy_send,
    hy_recv,
    z_send,
    z_recv,
    rs_send,
    rs_recv,
):
    x, z, y, c = (lax.axis_index(name) for name in ("x", "z", "y", "c"))
    wbuf = (w0, w1, w2, w3, w4)

    def at(dx=0, dz=0, dy=0, dc=0):
        return (
            lax.rem(x + dx + NX, NX),
            lax.rem(z + dz + NZ, NZ),
            lax.rem(y + dy + NY, NY),
            lax.rem(c + dc, NC),
        )

    def z_rows(dz, low=0, count=128):
        block = lax.rem(z + dz + NZ, NZ)
        return pl.ds(pl.multiple_of(block * 128 + low, count), count)

    def t_rows(dy, dc=0):
        index = lax.rem(y + dy + NY, NY) * NC + lax.rem(c + dc, NC)
        return pl.ds(pl.multiple_of(index * 32, 32), 32)

    def x_of(r):
        return lax.rem(x + r, NX)

    local = []
    for j in range(5):
        src = wbd_ref if j == 0 else wx_ref.at[:, pl.ds(256 * (j - 1), 256)]
        local.append(pltpu.make_async_copy(src, wbuf[j].at[z_rows(0)], local_sem.at[j]))
    local.append(
        pltpu.make_async_copy(
            hid_ref.at[:, pl.ds(pl.multiple_of(x * X_ROWS, X_ROWS), X_ROWS)],
            rows.at[x, t_rows(0)],
            local_sem.at[5],
        )
    )
    for copy in local:
        copy.start()

    greet(
        [
            at(dx=1),
            at(dx=-1),
            at(dx=2),
            at(dz=1),
            at(dz=-1),
            at(dy=1),
            at(dy=-1),
            at(dc=1),
        ]
    )
    for copy in local:
        copy.wait()

    sends = []

    def go(copy):
        copy.start()
        sends.append(copy)

    def z_copy(j, k, d):
        sign = 1 if d == 0 else -1
        if k < 3:
            piece = z_rows(-sign * k)
        else:
            piece = z_rows(-sign * k, 64 * d, 64)
        ref = wbuf[j].at[piece]
        return remote(ref, ref, z_send.at[d, j, k], z_recv.at[d, j, k], at(dz=sign))

    def z_arrived(j, k, d):
        sign = 1 if d == 0 else -1
        if k < 3:
            piece = z_rows(-sign * (k + 1))
        else:
            piece = z_rows(-sign * (k + 1), 64 * d, 64)
        ref = wbuf[j].at[piece]
        remote(ref, ref, z_send.at[d, j, k], z_recv.at[d, j, k], at(dz=sign)).wait_recv()

    def z_step(j, k):
        for d in range(2):
            if k > 0:
                z_arrived(j, k - 1, d)
            if k < 4:
                go(z_copy(j, k, d))

    def hx_copy(r):
        dest = lax.rem(x + NX - r, NX)
        src = hid_ref.at[:, pl.ds(pl.multiple_of(dest * X_ROWS, X_ROWS), X_ROWS)]
        return remote(src, rows.at[x, t_rows(0)], hx_send.at[r], hx_recv.at[r], at(dx=-r))

    def hx_arrived(r):
        ref = rows.at[x_of(r), t_rows(0)]
        remote(ref, ref, hx_send.at[r], hx_recv.at[r], at(dx=r)).wait_recv()

    kind_place = {0: (-1, 0), 1: (1, 0), 2: (2, 0), 3: (0, 1), 4: (-1, 1), 5: (1, 1), 6: (2, 1)}

    def hy_copy(r, kind, src_dy, where):
        ref = rows.at[x_of(r), t_rows(src_dy)]
        return remote(ref, ref, hy_send.at[r, kind], hy_recv.at[r, kind], where)

    def hy_arrived(r, kind):
        dy, dc = kind_place[kind]
        ref = rows.at[x_of(r), t_rows(dy, dc)]
        remote(ref, ref, hy_send.at[r, kind], hy_recv.at[r, kind], at(dc=1)).wait_recv()

    def hy_first(r):
        go(hy_copy(r, 0, 0, at(dy=1)))
        go(hy_copy(r, 1, 0, at(dy=-1)))
        go(hy_copy(r, 3, 0, at(dc=1)))

    def hy_relay(r):
        hy_arrived(r, 0)
        if r in (0, 3):
            go(hy_copy(r, 2, -1, at(dy=1)))
        go(hy_copy(r, 4, -1, at(dc=1)))
        hy_arrived(r, 1)
        if r in (1, 2):
            go(hy_copy(r, 2, 1, at(dy=-1)))
        go(hy_copy(r, 5, 1, at(dc=1)))

    def hy_last(r):
        hy_arrived(r, 2)
        go(hy_copy(r, 6, 2, at(dc=1)))

    largest = jnp.zeros((8, 128), jnp.float32)
    amax = jnp.full((8, 128), amax_ref[0], jnp.float32)
    factor = (quant_range / amax)[0:1, 0:1]
    in_scale = (amax / quant_range)[0:1, 0:1]
    max_out[...] = largest

    def quantized(r):
        for kind in (3, 4, 5, 6):
            hy_arrived(r, kind)
        where = x_of(r)

        def tile(i, carry):
            part = pl.ds(pl.multiple_of(i * 32, 32), 32)
            value = rows[where, part, :].astype(jnp.float32)
            quant[where, part, :] = jnp.clip(
                value * factor, -quant_range, quant_range
            ).astype(jnp.bfloat16)
            top = jnp.max(jnp.abs(value).reshape(4, 8, 1024), axis=0)
            best = top[:, 0:128]
            for lane in range(128, 1024, 128):
                best = jnp.maximum(best, top[:, lane : lane + 128])
            max_out[...] = jnp.maximum(max_out[...], best)
            return carry

        lax.fori_loop(0, 8, tile, 0)

    starts = [0]
    for width in CHUNKS:
        starts.append(starts[-1] + width)

    def cols(j):
        return pl.ds(starts[j], CHUNKS[j])

    def rs_copy(j, name):
        slot, low, dst, dst_low, sign = {
            "two_up": (0, 0, r1, 0, 1),
            "two_down": (0, 128, r1, 128, -1),
            "one_up_b": (1, 128, r2, 128, 1),
            "one_down_a": (2, 0, r2, 256, -1),
            "one_up_a": (1, 0, r2, 0, 1),
            "one_down_b": (2, 128, r2, 384, -1),
        }[name]
        index = RS_NAMES.index(name)
        return remote(
            stage.at[slot, pl.ds(low, 128), cols(j)],
            dst.at[pl.ds(dst_low, 128), cols(j)],
            rs_send.at[j, index],
            rs_recv.at[j, index],
            at(dx=sign),
        )

    def product(j, r):
        return jnp.dot(quant[x_of(r)], wbuf[j][...], preferred_element_type=jnp.float32)

    def rs_multiply(j):
        z_step(j, 4)
        stage[0, :, cols(j)] = product(j, 2).astype(jnp.bfloat16)
        value = product(j, 1)
        plus[:, cols(j)] = value[0:128]
        stage[1, 128:256, cols(j)] = value[128:256].astype(jnp.bfloat16)
        go(rs_copy(j, "two_up"))
        go(rs_copy(j, "two_down"))
        value = product(j, 3)
        minus[:, cols(j)] = value[128:256]
        stage[2, 0:128, cols(j)] = value[0:128].astype(jnp.bfloat16)
        go(rs_copy(j, "one_up_b"))
        own[:, cols(j)] = product(j, 0)
        go(rs_copy(j, "one_down_a"))

    def rs_add(j):
        rs_copy(j, "two_up").wait_recv()
        stage[1, 0:128, cols(j)] = (
            plus[:, cols(j)] + r1[0:128, cols(j)].astype(jnp.float32)
        ).astype(jnp.bfloat16)
        rs_copy(j, "two_down").wait_recv()
        stage[2, 128:256, cols(j)] = (
            minus[:, cols(j)] + r1[128:256, cols(j)].astype(jnp.float32)
        ).astype(jnp.bfloat16)
        go(rs_copy(j, "one_up_a"))
        go(rs_copy(j, "one_down_b"))

    def rs_final(j):
        for name in ("one_up_b", "one_down_a", "one_up_a", "one_down_b"):
            rs_copy(j, name).wait_recv()
        total = (
            own[:, cols(j)]
            + r2[0:256, cols(j)].astype(jnp.float32)
            + r2[256:512, cols(j)].astype(jnp.float32)
        ) * in_scale
        if j == 0:
            bc_out[...] = total[:, 0:256].astype(jnp.bfloat16)
            dt_out[...] = total[:, 256:384]
        else:
            x_out[:, 256 * (j - 1) : 256 * j] = total.astype(jnp.bfloat16)

    z_step(0, 0)
    for r in (1, 3, 2):
        go(hx_copy(r))
    hy_first(0)
    z_step(1, 0)
    for r in (1, 3):
        hx_arrived(r)
        hy_first(r)
    z_step(0, 1)
    hx_arrived(2)
    hy_first(2)
    z_step(2, 0)
    hy_relay(0)
    z_step(1, 1)
    hy_relay(1)
    z_step(0, 2)
    z_step(3, 0)
    hy_relay(3)
    hy_relay(2)
    hy_last(0)
    hy_last(1)
    z_step(2, 1)
    z_step(1, 2)
    hy_last(3)
    hy_last(2)
    z_step(0, 3)
    z_step(4, 0)
    z_step(3, 1)
    for r in (0, 1, 3, 2):
        quantized(r)
    z_step(2, 2)
    z_step(1, 3)
    rs_multiply(0)
    z_step(4, 1)
    z_step(3, 2)
    z_step(2, 3)
    rs_multiply(1)
    rs_add(0)
    z_step(4, 2)
    z_step(3, 3)
    rs_multiply(2)
    rs_add(1)
    z_step(4, 3)
    rs_final(0)
    rs_multiply(3)
    rs_add(2)
    rs_final(1)
    rs_multiply(4)
    rs_add(3)
    rs_final(2)
    rs_add(4)
    rs_final(3)
    rs_final(4)
    for copy in sends:
        copy.wait_send()


RS_NAMES = ("two_up", "two_down", "one_up_b", "one_down_a", "one_up_a", "one_down_b")


def project_in(prev_amax, hidden_in, w_x, w_bc_dt):
    total = sum(CHUNKS)
    any_place = pl.BlockSpec(memory_space=pl.ANY)
    vmem = pl.BlockSpec(memory_space=pltpu.VMEM)
    dma = pltpu.SemaphoreType.DMA
    return pl.pallas_call(
        in_projection,
        name="in_projection",
        out_shape=(
            jax.ShapeDtypeStruct((256, 1024), jnp.bfloat16),
            jax.ShapeDtypeStruct((256, 256), jnp.bfloat16),
            jax.ShapeDtypeStruct((256, 128), jnp.float32),
            jax.ShapeDtypeStruct((8, 128), jnp.float32),
        ),
        in_specs=[pl.BlockSpec(memory_space=pltpu.SMEM), any_place, any_place, any_place],
        out_specs=(vmem, vmem, vmem, vmem),
        scratch_shapes=[
            pltpu.VMEM((4, 256, X_ROWS), jnp.bfloat16),
            pltpu.VMEM((4, 256, X_ROWS), jnp.bfloat16),
            *[pltpu.VMEM((X_ROWS, width), jnp.bfloat16) for width in CHUNKS],
            pltpu.VMEM((3, 256, total), jnp.bfloat16),
            pltpu.VMEM((256, total), jnp.bfloat16),
            pltpu.VMEM((512, total), jnp.bfloat16),
            pltpu.VMEM((256, total), jnp.float32),
            pltpu.VMEM((128, total), jnp.float32),
            pltpu.VMEM((128, total), jnp.float32),
            dma((6,)),
            dma((4,)),
            dma((4,)),
            dma((4, 7)),
            dma((4, 7)),
            dma((2, 5, 4)),
            dma((2, 5, 4)),
            dma((5, 6)),
            dma((5, 6)),
        ],
        compiler_params=pltpu.CompilerParams(
            collective_id=0, has_side_effects=True, vmem_limit_bytes=48 * 2**20
        ),
    )(jnp.reshape(prev_amax, (1,)), hidden_in, w_x, w_bc_dt)


GROUP_SLOTS = ((0, 4), (-1, 1), (-2, 2), (-3, 3))
GROUP_ORDER = (1, 2, 3, 0)
Y_NAMES = ("two_up", "two_down", "one_up_b", "one_down_a", "one_up_a", "one_down_b")


def out_projection(
    u_ref,
    sq_ref,
    w_ref,
    out_ref,
    tokens,
    weights,
    partial,
    from_core,
    ystage,
    ry1,
    ry2,
    yown,
    yup,
    ydown,
    fstage,
    landed,
    squares,
    local_sem,
    x_send,
    x_recv,
    z_send,
    z_recv,
    sq_send,
    sq_recv,
    c_send,
    c_recv,
    y_send,
    y_recv,
    f_send,
    f_recv,
):
    x, z, y, c = (lax.axis_index(name) for name in ("x", "z", "y", "c"))

    def at(dx=0, dz=0, dy=0, dc=0):
        return (
            lax.rem(x + dx + NX, NX),
            lax.rem(z + dz + NZ, NZ),
            lax.rem(y + dy + NY, NY),
            lax.rem(c + dc, NC),
        )

    def x_of(dx):
        return lax.rem(x + dx + NX, NX)

    def y_of(dy):
        return lax.rem(y + dy + NY, NY)

    def z_cols(slot):
        for g, pair in enumerate(GROUP_SLOTS):
            if slot in pair:
                return pl.ds(256 * g + 128 * pair.index(slot), 128)

    mine = pltpu.make_async_copy(w_ref, weights.at[:, z_cols(0)], local_sem.at[0])
    mine.start()
    mine_u = pltpu.make_async_copy(u_ref, tokens.at[x], local_sem.at[1])
    mine_u.start()
    greet(
        [at(dx=1), at(dx=-1), at(dx=2), at(dz=1), at(dz=-1)]
        + [at(dy=dy, dc=dc) for dy in range(4) for dc in range(2) if (dy, dc) != (0, 0)]
    )
    mine.wait()
    mine_u.wait()

    sends = []

    def go(copy):
        copy.start()
        sends.append(copy)

    def x_copy(p, kind, source, where):
        ref = tokens.at[x_of(source), pl.ds(64 * p, 64)]
        return remote(ref, ref, x_send.at[p, kind], x_recv.at[p, kind], where)

    def x_arrived(p, kind):
        x_copy(p, kind, {0: -1, 1: 1, 2: 2}[kind], at(dx=1)).wait_recv()

    def x_relay_up(p):
        x_arrived(p, 0)
        go(x_copy(p, 2, -1, at(dx=1)))

    def x_relay_down(p):
        x_arrived(p, 1)
        go(x_copy(p, 2, 1, at(dx=-1)))

    def z_copy(j, k, d):
        sign = 1 if d == 0 else -1
        rows = pl.ds(256 * j, 256)
        arrives = -sign * (k + 1)
        if k == 3:
            arrives = 4
        return remote(
            weights.at[rows, z_cols(-sign * k)],
            weights.at[rows, z_cols(arrives)],
            z_send.at[d, j, k],
            z_recv.at[d, j, k],
            at(dz=sign),
        )

    def z_step(j, k, d):
        if k > 0:
            z_copy(j, k - 1, d).wait_recv()
        if k < 3 or j // 2 == d:
            go(z_copy(j, k, d))

    others = [(dy, dc) for dy in range(4) for dc in range(2) if (dy, dc) != (0, 0)]

    def t_index(dy, dc):
        return y_of(dy) * NC + lax.rem(c + dc, NC)

    def sq_copy(n):
        dy, dc = others[n]
        there = pl.ds(pl.multiple_of(t_index(dy, dc) * 32, 32), 32)
        return remote(
            sq_ref.at[there], squares.at[n], sq_send.at[n], sq_recv.at[n], at(dy=dy, dc=dc)
        )

    for p in (0, 1, 2, 3):
        go(x_copy(p, 0, 0, at(dx=1)))
        go(x_copy((p + 2) % 4, 1, 0, at(dx=-1)))
        for d in range(2):
            z_step(p, 0, d)
    for n in range(7):
        go(sq_copy(n))
    z_step(0, 1, 0), z_step(0, 1, 1), z_step(1, 1, 0), z_step(1, 1, 1)
    x_relay_up(0), x_relay_down(2)
    z_step(2, 1, 0), z_step(2, 1, 1), z_step(3, 1, 0), z_step(3, 1, 1)
    x_relay_up(1), x_relay_down(3)
    for j in range(4):
        z_step(j, 2, 0), z_step(j, 2, 1)
    for p in (2, 3):
        x_arrived(p, 0), x_arrived((p + 2) % 4, 1)
    for p in range(4):
        x_arrived(p, 2)

    def cols(g):
        return pl.ds(256 * g, 256)

    def multiply(g):
        def one(slot, carry):
            value = jnp.dot(
                tokens[slot], weights[:, cols(g)], preferred_element_type=jnp.float32
            ).astype(jnp.bfloat16)
            value = value.reshape(NY, NC, 32, 256)
            for core in range(NC):
                partial[g, core, :, slot] = value[:, core]
            return carry

        lax.fori_loop(0, NX, one, 0)

    def c_copy(g):
        other = lax.rem(c + 1, NC)
        return remote(
            partial.at[g, other], from_core.at[g], c_send.at[g], c_recv.at[g], at(dc=1)
        )

    def y_copy(g, name):
        slot, low, dst, sign = {
            "two_up": (2, 0, ry1.at[g], 1),
            "two_down": (2, 2, ry1.at[g], -1),
            "one_up_b": (1, 2, ry2.at[g, 0], 1),
            "one_down_a": (3, 0, ry2.at[g, 1], -1),
            "one_up_a": (1, 0, ry2.at[g, 0], 1),
            "one_down_b": (3, 2, ry2.at[g, 1], -1),
        }[name]
        index = Y_NAMES.index(name)
        return remote(
            ystage.at[g, slot, pl.ds(low, 2)],
            dst.at[pl.ds(low, 2)],
            y_send.at[g, index],
            y_recv.at[g, index],
            at(dy=sign),
        )

    def both_cores(g, dy):
        where = y_of(dy)
        return partial[g, c, where].astype(jnp.float32) + from_core[g, where].astype(jnp.float32)

    def y_first(g):
        c_copy(g).wait_recv()
        ystage[g, 2] = both_cores(g, 2).astype(jnp.bfloat16)
        value = both_cores(g, 1)
        yup[g] = value[0:2]
        ystage[g, 1, 2:4] = value[2:4].astype(jnp.bfloat16)
        go(y_copy(g, "two_up"))
        go(y_copy(g, "two_down"))
        value = both_cores(g, 3)
        ydown[g] = value[2:4]
        ystage[g, 3, 0:2] = value[0:2].astype(jnp.bfloat16)
        go(y_copy(g, "one_up_b"))
        yown[g] = both_cores(g, 0)
        go(y_copy(g, "one_down_a"))

    def y_add(g):
        y_copy(g, "two_up").wait_recv()
        ystage[g, 1, 0:2] = (yup[g] + ry1[g, 0:2].astype(jnp.float32)).astype(jnp.bfloat16)
        y_copy(g, "two_down").wait_recv()
        ystage[g, 3, 2:4] = (ydown[g] + ry1[g, 2:4].astype(jnp.float32)).astype(jnp.bfloat16)
        go(y_copy(g, "one_up_a"))
        go(y_copy(g, "one_down_b"))

    def out_cols(x_slot, g, side):
        block = lax.rem(z + GROUP_SLOTS[g][side] + NZ, NZ)
        return pl.ds(pl.multiple_of(x_slot * 1024 + block * 128, 128), 128)

    def f_copy(g, side, dx):
        return remote(
            fstage.at[g, x_of(dx), :, pl.ds(128 * side, 128)],
            landed.at[:, out_cols(x, g, side)],
            f_send.at[g, side, dx],
            f_recv.at[g, side, dx],
            at(dx=dx),
        )

    def f_arrived(g, side, dx):
        ref = landed.at[:, out_cols(x_of(-dx), g, side)]
        remote(
            ref, ref, f_send.at[g, side, dx], f_recv.at[g, side, dx], at(dx=-dx)
        ).wait_recv()

    def y_final(g):
        for name in ("one_up_b", "one_down_a", "one_up_a", "one_down_b"):
            y_copy(g, name).wait_recv()
        fstage[g] = (
            yown[g] + ry2[g, 0].astype(jnp.float32) + ry2[g, 1].astype(jnp.float32)
        ).astype(jnp.bfloat16)
        here = fstage[g, x]
        for side in range(2):
            landed[:, out_cols(x, g, side)] = here[:, 128 * side : 128 * side + 128]
        for dx in (2, 1, 3):
            for side in range(2):
                go(f_copy(g, side, dx))

    multiply(1)
    go(c_copy(1))
    for j in range(4):
        z_step(j, 3, 0), z_step(j, 3, 1)
    multiply(2)
    go(c_copy(2))
    y_first(1)
    multiply(3)
    go(c_copy(3))
    y_first(2)
    y_add(1)
    for j in range(4):
        z_copy(j, 3, j // 2).wait_recv()
    multiply(0)
    go(c_copy(0))
    y_first(3)
    y_add(2)
    y_final(1)
    y_first(0)
    y_add(3)
    y_final(2)
    y_add(0)
    y_final(3)

    total = sq_ref[pl.ds(pl.multiple_of(t_index(0, 0) * 32, 32), 32), :]
    for n in range(7):
        sq_copy(n).wait_recv()
        total = total + squares[n]
    mean_sq = jnp.sum(total, axis=1, keepdims=True) / (HEADS * HEAD_DIM)
    scale = lax.rsqrt(mean_sq + epsilon)

    y_final(0)
    for g in GROUP_ORDER:
        for dx in (1, 2, 3):
            for side in range(2):
                f_arrived(g, side, dx)
    out_ref[...] = (landed[...].astype(jnp.float32) * scale).astype(jnp.bfloat16)
    for copy in sends:
        copy.wait_send()


def project_out(u, squares, w_out):
    any_place = pl.BlockSpec(memory_space=pl.ANY)
    vmem = pl.BlockSpec(memory_space=pltpu.VMEM)
    dma = pltpu.SemaphoreType.DMA
    bf16, f32 = (jnp.bfloat16, jnp.float32)
    return pl.pallas_call(
        out_projection,
        name="out_projection",
        out_shape=jax.ShapeDtypeStruct((32, 4096), bf16),
        in_specs=[any_place, vmem, any_place],
        out_specs=vmem,
        scratch_shapes=[
            pltpu.VMEM((4, 256, 1024), bf16),
            pltpu.VMEM((1024, 1024), bf16),
            pltpu.VMEM((4, 2, 4, 4, 32, 256), bf16),
            pltpu.VMEM((4, 4, 4, 32, 256), bf16),
            pltpu.VMEM((4, 4, 4, 32, 256), bf16),
            pltpu.VMEM((4, 4, 32, 256), bf16),
            pltpu.VMEM((4, 2, 4, 32, 256), bf16),
            pltpu.VMEM((4, 4, 32, 256), f32),
            pltpu.VMEM((4, 2, 32, 256), f32),
            pltpu.VMEM((4, 2, 32, 256), f32),
            pltpu.VMEM((4, 4, 32, 256), bf16),
            pltpu.VMEM((32, 4096), bf16),
            pltpu.VMEM((7, 32, 128), f32),
            dma((2,)),
            dma((4, 3)),
            dma((4, 3)),
            dma((2, 4, 4)),
            dma((2, 4, 4)),
            dma((7,)),
            dma((7,)),
            dma((4,)),
            dma((4,)),
            dma((4, 6)),
            dma((4, 6)),
            dma((4, 2, 4)),
            dma((4, 2, 4)),
        ],
        compiler_params=pltpu.CompilerParams(
            collective_id=1, has_side_effects=True, vmem_limit_bytes=48 * 2**20
        ),
    )(u, squares, w_out)


def local(
    hidden_in,
    prev_amax,
    w_x,
    w_bc,
    w_dt,
    conv_x,
    conv_bc,
    conv_state_x,
    conv_state_bc,
    dt_bias,
    decay_rate,
    skip,
    init_state,
    norm_gain,
    w_out,
):
    margin = KERNEL - 1
    leading = lax.axis_index(SEQ) == 0
    row_count = hidden_in.shape[0] * 8
    bc_width = w_bc.shape[1] * w_bc.shape[2] * w_bc.shape[3]
    heads = w_dt.shape[1]
    w_bc_dt = jnp.concatenate(
        [
            jnp.reshape(w_bc, (w_bc.shape[0], bc_width)),
            w_dt,
            jnp.zeros((w_dt.shape[0], 128 - heads), w_dt.dtype),
        ],
        axis=1,
    )
    x_whole, bc_whole, dt_raw, top = project_in(prev_amax, hidden_in, w_x, w_bc_dt)
    dt_raw = dt_raw[:, :heads]
    abs_max = over_copies(jnp.max(top), SEQ)
    state_bc = jnp.reshape(conv_state_bc, (margin, bc_width))
    received = from_behind((x_whole[row_count - margin :], bc_whole[row_count - margin :]), SEQ, 1)
    x_edge = jnp.where(leading, conv_state_x, received[0])
    bc_edge = jnp.where(leading, state_bc, received[1])
    x_act = depthwise(x_edge, x_whole, conv_x, row_count)
    bc_act = depthwise(bc_edge, bc_whole, jnp.reshape(conv_bc, (KERNEL, bc_width)), row_count)
    step_size = jax.nn.softplus(dt_raw + dt_bias)
    heads_here = step_size.shape[1]
    groups_here = w_bc.shape[1]
    per_group = HEADS // GROUPS
    blocks = row_count // SPAN
    x_blocks = x_act.reshape(blocks, SPAN, heads_here, HEAD_DIM)
    bc_blocks = bc_act.reshape(blocks, SPAN, groups_here, 2, STATE)
    in_map = bc_blocks[:, :, :, 0]
    out_map = bc_blocks[:, :, :, 1]
    step_blocks = step_size.reshape(blocks, SPAN, heads_here)
    cum_blocks = jnp.cumsum(-step_blocks * decay_rate, axis=1)
    index_row = jnp.arange(SPAN, dtype=jnp.int32)
    lower_mask = index_row[:, None] >= index_row[None, :]
    intersection = jnp.einsum(
        "ctgn,cugn->cgtu", out_map, in_map, preferred_element_type=jnp.float32
    )
    intersection = jnp.repeat(intersection, per_group, axis=1)
    cum_heads = jnp.transpose(cum_blocks, (0, 2, 1))
    log_gap = cum_heads[:, :, :, None] - cum_heads[:, :, None, :]
    decay = jnp.exp(jnp.where(lower_mask[None, None], log_gap, -1e30))
    step_heads = jnp.transpose(step_blocks, (0, 2, 1))
    weights = (intersection * decay * step_heads[:, :, None, :]).astype(jnp.bfloat16)
    local_part = jnp.einsum(
        "chtu,cuhp->cthp", weights, x_blocks, preferred_element_type=jnp.float32
    )
    last_cum = cum_blocks[:, SPAN - 1, :]
    x_weighted = (
        x_blocks.astype(jnp.float32)
        * (step_blocks * jnp.exp(last_cum[:, None, :] - cum_blocks))[:, :, :, None]
    ).astype(jnp.bfloat16)
    in_heads = jnp.repeat(in_map, per_group, axis=2)
    added = jnp.einsum("cuhp,cuhn->chpn", x_weighted, in_heads, preferred_element_type=jnp.float32)

    def carry_on(carried, element):
        block_decay, block_added = element
        return (block_decay[:, None, None] * carried + block_added, carried)

    empty_state = jnp.zeros((heads_here, HEAD_DIM, STATE), jnp.float32)
    device_state, entering = lax.scan(carry_on, empty_state, (jnp.exp(last_cum), added))
    device_decay = jnp.exp(jnp.sum(last_cum, axis=0))
    seeded = device_state + jnp.where(leading, device_decay[:, None, None] * init_state, 0.0)
    identity = (jnp.ones_like(device_decay), jnp.zeros_like(device_state))
    scanned = prefix_by_axis((device_decay, seeded), SEQ, combine, identity)
    incoming = jnp.where(leading, init_state, scanned[1])
    prefix = jnp.exp(jnp.cumsum(last_cum, axis=0) - last_cum)
    states_in = entering + prefix[:, :, None, None] * incoming[None]
    out_heads = jnp.repeat(out_map, per_group, axis=2).astype(jnp.float32)
    carried_part = (
        jnp.einsum("cthn,chpn->cthp", out_heads, states_in, precision=lax.Precision.HIGHEST)
        * jnp.exp(cum_blocks)[:, :, :, None]
    )
    ssm_out = local_part + carried_part + skip[None, None, :, None] * x_blocks.astype(jnp.float32)
    ssm_out = ssm_out.reshape(row_count, heads_here * HEAD_DIM)
    squares = jnp.sum((ssm_out * ssm_out).reshape(row_count, -1, 128), axis=1)
    scaled_out = (ssm_out * norm_gain).astype(jnp.bfloat16)
    layer_out = project_out(scaled_out, squares, w_out)
    return (layer_out, abs_max)


def solution(mesh):
    finer = Mesh(mesh.devices.reshape(NX, NZ, NY, NC), SEQ_TENSOR)
    return jax.shard_map(
        local,
        mesh=finer,
        in_specs=(
            P(SEQ_TENSOR, None),
            P(),
            P(SEQ, TENSOR),
            P(SEQ, TENSOR, None, None),
            P(SEQ, TENSOR),
            P(None, TENSOR),
            P(None, TENSOR, None, None),
            P(None, TENSOR),
            P(None, TENSOR, None, None),
            P(TENSOR),
            P(TENSOR),
            P(TENSOR),
            P(TENSOR, None, None),
            P(TENSOR),
            P(TENSOR, SEQ),
        ),
        out_specs=(P(SEQ_TENSOR, None), P()),
        check_vma=False,
    )
```

```python
import jax
import jax.numpy as jnp
from jax import lax
from jax.experimental import pallas as pl
from jax.experimental.pallas import tpu as pltpu
from jax.sharding import Mesh
from jax.sharding import PartitionSpec as P

HEADS = 128
HEAD_DIM = 64
STATE = 128
GROUPS = 8
KERNEL = 4
SPAN = 128
SEQ = ("x", "z")
TENSOR = ("y", "c")
SEQ_TENSOR = SEQ + TENSOR


epsilon = 1e-05
quant_range = 448.0


MESH_ID = pl.DeviceIdType.MESH
NX, NZ, NY, NC = (4, 8, 4, 2)
CHUNKS = (384, 256, 256, 256, 256)
X_ROWS = 1024


def remote(src, dst, send_sem, recv_sem, where):
    return pltpu.make_async_remote_copy(
        src_ref=src,
        dst_ref=dst,
        send_sem=send_sem,
        recv_sem=recv_sem,
        device_id=where,
        device_id_type=MESH_ID,
    )


def greet(peers):
    barrier = pltpu.get_barrier_semaphore()
    for peer in peers:
        pl.semaphore_signal(barrier, inc=1, device_id=peer, device_id_type=MESH_ID)
    pl.semaphore_wait(barrier, len(peers))


def in_projection(
    amax_ref,
    hid_ref,
    wx_ref,
    wbd_ref,
    x_out,
    bc_out,
    dt_out,
    max_out,
    rows,
    quant,
    w0,
    w1,
    w2,
    w3,
    w4,
    stage,
    r1,
    r2,
    own,
    plus,
    minus,
    local_sem,
    hx_send,
    hx_recv,
    hy_send,
    hy_recv,
    z_send,
    z_recv,
    rs_send,
    rs_recv,
):
    x, z, y, c = (lax.axis_index(name) for name in ("x", "z", "y", "c"))
    wbuf = (w0, w1, w2, w3, w4)

    def at(dx=0, dz=0, dy=0, dc=0):
        return (
            lax.rem(x + dx + NX, NX),
            lax.rem(z + dz + NZ, NZ),
            lax.rem(y + dy + NY, NY),
            lax.rem(c + dc, NC),
        )

    def z_rows(dz, low=0, count=128):
        block = lax.rem(z + dz + NZ, NZ)
        return pl.ds(pl.multiple_of(block * 128 + low, count), count)

    def t_rows(dy, dc=0):
        index = lax.rem(y + dy + NY, NY) * NC + lax.rem(c + dc, NC)
        return pl.ds(pl.multiple_of(index * 32, 32), 32)

    def x_of(r):
        return lax.rem(x + r, NX)

    local = []
    for j in range(5):
        src = wbd_ref if j == 0 else wx_ref.at[:, pl.ds(256 * (j - 1), 256)]
        local.append(pltpu.make_async_copy(src, wbuf[j].at[z_rows(0)], local_sem.at[j]))
    local.append(
        pltpu.make_async_copy(
            hid_ref.at[:, pl.ds(pl.multiple_of(x * X_ROWS, X_ROWS), X_ROWS)],
            rows.at[x, t_rows(0)],
            local_sem.at[5],
        )
    )
    for copy in local:
        copy.start()

    greet(
        [
            at(dx=1),
            at(dx=-1),
            at(dx=2),
            at(dz=1),
            at(dz=-1),
            at(dy=1),
            at(dy=-1),
            at(dc=1),
        ]
    )
    for copy in local:
        copy.wait()

    sends = []

    def go(copy):
        copy.start()
        sends.append(copy)

    def z_copy(j, k, d):
        sign = 1 if d == 0 else -1
        if k < 3:
            piece = z_rows(-sign * k)
        else:
            piece = z_rows(-sign * k, 64 * d, 64)
        ref = wbuf[j].at[piece]
        return remote(ref, ref, z_send.at[d, j, k], z_recv.at[d, j, k], at(dz=sign))

    def z_arrived(j, k, d):
        sign = 1 if d == 0 else -1
        if k < 3:
            piece = z_rows(-sign * (k + 1))
        else:
            piece = z_rows(-sign * (k + 1), 64 * d, 64)
        ref = wbuf[j].at[piece]
        remote(ref, ref, z_send.at[d, j, k], z_recv.at[d, j, k], at(dz=sign)).wait_recv()

    def z_step(j, k):
        for d in range(2):
            if k > 0:
                z_arrived(j, k - 1, d)
            if k < 4:
                go(z_copy(j, k, d))

    def hx_copy(r):
        dest = lax.rem(x + NX - r, NX)
        src = hid_ref.at[:, pl.ds(pl.multiple_of(dest * X_ROWS, X_ROWS), X_ROWS)]
        return remote(src, rows.at[x, t_rows(0)], hx_send.at[r], hx_recv.at[r], at(dx=-r))

    def hx_arrived(r):
        ref = rows.at[x_of(r), t_rows(0)]
        remote(ref, ref, hx_send.at[r], hx_recv.at[r], at(dx=r)).wait_recv()

    kind_place = {0: (-1, 0), 1: (1, 0), 2: (2, 0), 3: (0, 1), 4: (-1, 1), 5: (1, 1), 6: (2, 1)}

    def hy_copy(r, kind, src_dy, where):
        ref = rows.at[x_of(r), t_rows(src_dy)]
        return remote(ref, ref, hy_send.at[r, kind], hy_recv.at[r, kind], where)

    def hy_arrived(r, kind):
        dy, dc = kind_place[kind]
        ref = rows.at[x_of(r), t_rows(dy, dc)]
        remote(ref, ref, hy_send.at[r, kind], hy_recv.at[r, kind], at(dc=1)).wait_recv()

    def hy_first(r):
        go(hy_copy(r, 0, 0, at(dy=1)))
        go(hy_copy(r, 1, 0, at(dy=-1)))
        go(hy_copy(r, 3, 0, at(dc=1)))

    def hy_relay(r):
        hy_arrived(r, 0)
        if r in (0, 3):
            go(hy_copy(r, 2, -1, at(dy=1)))
        go(hy_copy(r, 4, -1, at(dc=1)))
        hy_arrived(r, 1)
        if r in (1, 2):
            go(hy_copy(r, 2, 1, at(dy=-1)))
        go(hy_copy(r, 5, 1, at(dc=1)))

    def hy_last(r):
        hy_arrived(r, 2)
        go(hy_copy(r, 6, 2, at(dc=1)))

    largest = jnp.zeros((8, 128), jnp.float32)
    amax = jnp.full((8, 128), amax_ref[0], jnp.float32)
    factor = (quant_range / amax)[0:1, 0:1]
    in_scale = (amax / quant_range)[0:1, 0:1]
    max_out[...] = largest

    def quantized(r):
        for kind in (3, 4, 5, 6):
            hy_arrived(r, kind)
        where = x_of(r)

        def tile(i, carry):
            part = pl.ds(pl.multiple_of(i * 32, 32), 32)
            value = rows[where, part, :].astype(jnp.float32)
            quant[where, part, :] = jnp.clip(
                value * factor, -quant_range, quant_range
            ).astype(jnp.bfloat16)
            top = jnp.max(jnp.abs(value).reshape(4, 8, 1024), axis=0)
            best = top[:, 0:128]
            for lane in range(128, 1024, 128):
                best = jnp.maximum(best, top[:, lane : lane + 128])
            max_out[...] = jnp.maximum(max_out[...], best)
            return carry

        lax.fori_loop(0, 8, tile, 0)

    starts = [0]
    for width in CHUNKS:
        starts.append(starts[-1] + width)

    def cols(j):
        return pl.ds(starts[j], CHUNKS[j])

    def rs_copy(j, name):
        slot, low, dst, dst_low, sign = {
            "two_up": (0, 0, r1, 0, 1),
            "two_down": (0, 128, r1, 128, -1),
            "one_up_b": (1, 128, r2, 128, 1),
            "one_down_a": (2, 0, r2, 256, -1),
            "one_up_a": (1, 0, r2, 0, 1),
            "one_down_b": (2, 128, r2, 384, -1),
        }[name]
        index = RS_NAMES.index(name)
        return remote(
            stage.at[slot, pl.ds(low, 128), cols(j)],
            dst.at[pl.ds(dst_low, 128), cols(j)],
            rs_send.at[j, index],
            rs_recv.at[j, index],
            at(dx=sign),
        )

    def product(j, r):
        return jnp.dot(quant[x_of(r)], wbuf[j][...], preferred_element_type=jnp.float32)

    def rs_multiply(j):
        z_step(j, 4)
        stage[0, :, cols(j)] = product(j, 2).astype(jnp.bfloat16)
        value = product(j, 1)
        plus[:, cols(j)] = value[0:128]
        stage[1, 128:256, cols(j)] = value[128:256].astype(jnp.bfloat16)
        go(rs_copy(j, "two_up"))
        go(rs_copy(j, "two_down"))
        value = product(j, 3)
        minus[:, cols(j)] = value[128:256]
        stage[2, 0:128, cols(j)] = value[0:128].astype(jnp.bfloat16)
        go(rs_copy(j, "one_up_b"))
        own[:, cols(j)] = product(j, 0)
        go(rs_copy(j, "one_down_a"))

    def rs_add(j):
        rs_copy(j, "two_up").wait_recv()
        stage[1, 0:128, cols(j)] = (
            plus[:, cols(j)] + r1[0:128, cols(j)].astype(jnp.float32)
        ).astype(jnp.bfloat16)
        rs_copy(j, "two_down").wait_recv()
        stage[2, 128:256, cols(j)] = (
            minus[:, cols(j)] + r1[128:256, cols(j)].astype(jnp.float32)
        ).astype(jnp.bfloat16)
        go(rs_copy(j, "one_up_a"))
        go(rs_copy(j, "one_down_b"))

    def rs_final(j):
        for name in ("one_up_b", "one_down_a", "one_up_a", "one_down_b"):
            rs_copy(j, name).wait_recv()
        total = (
            own[:, cols(j)]
            + r2[0:256, cols(j)].astype(jnp.float32)
            + r2[256:512, cols(j)].astype(jnp.float32)
        ) * in_scale
        if j == 0:
            bc_out[...] = total[:, 0:256].astype(jnp.bfloat16)
            dt_out[...] = total[:, 256:384]
        else:
            x_out[:, 256 * (j - 1) : 256 * j] = total.astype(jnp.bfloat16)

    z_step(0, 0)
    for r in (1, 3, 2):
        go(hx_copy(r))
    hy_first(0)
    z_step(1, 0)
    for r in (1, 3):
        hx_arrived(r)
        hy_first(r)
    z_step(0, 1)
    hx_arrived(2)
    hy_first(2)
    z_step(2, 0)
    hy_relay(0)
    z_step(1, 1)
    hy_relay(1)
    z_step(0, 2)
    z_step(3, 0)
    hy_relay(3)
    hy_relay(2)
    hy_last(0)
    hy_last(1)
    z_step(2, 1)
    z_step(1, 2)
    hy_last(3)
    hy_last(2)
    z_step(0, 3)
    z_step(4, 0)
    z_step(3, 1)
    for r in (0, 1, 3, 2):
        quantized(r)
    z_step(2, 2)
    z_step(1, 3)
    rs_multiply(0)
    z_step(4, 1)
    z_step(3, 2)
    z_step(2, 3)
    rs_multiply(1)
    rs_add(0)
    z_step(4, 2)
    z_step(3, 3)
    rs_multiply(2)
    rs_add(1)
    z_step(4, 3)
    rs_final(0)
    rs_multiply(3)
    rs_add(2)
    rs_final(1)
    rs_multiply(4)
    rs_add(3)
    rs_final(2)
    rs_add(4)
    rs_final(3)
    rs_final(4)
    for copy in sends:
        copy.wait_send()


RS_NAMES = ("two_up", "two_down", "one_up_b", "one_down_a", "one_up_a", "one_down_b")


def project_in(prev_amax, hidden_in, w_x, w_bc_dt):
    total = sum(CHUNKS)
    any_place = pl.BlockSpec(memory_space=pl.ANY)
    vmem = pl.BlockSpec(memory_space=pltpu.VMEM)
    dma = pltpu.SemaphoreType.DMA
    return pl.pallas_call(
        in_projection,
        name="in_projection",
        out_shape=(
            jax.ShapeDtypeStruct((256, 1024), jnp.bfloat16),
            jax.ShapeDtypeStruct((256, 256), jnp.bfloat16),
            jax.ShapeDtypeStruct((256, 128), jnp.float32),
            jax.ShapeDtypeStruct((8, 128), jnp.float32),
        ),
        in_specs=[pl.BlockSpec(memory_space=pltpu.SMEM), any_place, any_place, any_place],
        out_specs=(vmem, vmem, vmem, vmem),
        scratch_shapes=[
            pltpu.VMEM((4, 256, X_ROWS), jnp.bfloat16),
            pltpu.VMEM((4, 256, X_ROWS), jnp.bfloat16),
            *[pltpu.VMEM((X_ROWS, width), jnp.bfloat16) for width in CHUNKS],
            pltpu.VMEM((3, 256, total), jnp.bfloat16),
            pltpu.VMEM((256, total), jnp.bfloat16),
            pltpu.VMEM((512, total), jnp.bfloat16),
            pltpu.VMEM((256, total), jnp.float32),
            pltpu.VMEM((128, total), jnp.float32),
            pltpu.VMEM((128, total), jnp.float32),
            dma((6,)),
            dma((4,)),
            dma((4,)),
            dma((4, 7)),
            dma((4, 7)),
            dma((2, 5, 4)),
            dma((2, 5, 4)),
            dma((5, 6)),
            dma((5, 6)),
        ],
        compiler_params=pltpu.CompilerParams(
            collective_id=0, has_side_effects=True, vmem_limit_bytes=48 * 2**20
        ),
    )(jnp.reshape(prev_amax, (1,)), hidden_in, w_x, w_bc_dt)


def scan_blocks(
    x_ref,
    bc_ref,
    dt_ref,
    top_ref,
    conv_x_ref,
    conv_bc_ref,
    state_x_ref,
    state_bc_ref,
    par_ref,
    init_ref,
    gain_ref,
    u_out,
    sq_out,
    max_out,
    halo_x,
    halo_bc,
    ext,
    x_act,
    bc_act,
    cum_s,
    cum_t,
    step_t,
    expand,
    added0,
    device_state,
    tiles,
    arrived,
    carried,
    incoming,
    init_t,
    grown,
    acc,
    halo_send,
    halo_recv,
    tile_send,
    tile_recv,
    st_send,
    st_recv,
    back_send,
    back_recv,
):
    x, z, y, c = (lax.axis_index(name) for name in ("x", "z", "y", "c"))
    here = x * NZ + z
    f32, bf16 = (jnp.float32, jnp.bfloat16)
    count = NX * NZ

    def at(rel):
        dx, dz = (rel // NZ, rel % NZ)
        return (lax.rem(x + dx, NX), lax.rem(z + dz, NZ), y, c)

    def source(rel):
        dx, dz = (rel // NZ, rel % NZ)
        return (lax.rem(x + NX - dx, NX), lax.rem(z + NZ - dz, NZ))

    def exact_dot(a, b):
        return jnp.dot(a, b, precision=lax.Precision.HIGHEST, preferred_element_type=f32)

    barrier = pltpu.get_barrier_semaphore()

    def greet_one(rel, carry):
        pl.semaphore_signal(barrier, inc=1, device_id=at(rel), device_id_type=MESH_ID)
        return carry

    lax.fori_loop(1, count, greet_one, 0)

    lane = lax.broadcasted_iota(jnp.int32, (128, 1024), 1)
    head = lax.broadcasted_iota(jnp.int32, (128, 1024), 0)
    expand[...] = jnp.where((lane >= head * 64) & (lane < head * 64 + 64), 1.0, 0.0).astype(f32)
    row_at = lax.broadcasted_iota(jnp.int32, (128, 128), 0)
    col_at = lax.broadcasted_iota(jnp.int32, (128, 128), 1)
    lower = row_at >= col_at
    ones_lower = jnp.where(lower, 1.0, 0.0).astype(f32)
    raw = dt_ref[...] + par_ref[0:1, :]
    step = jnp.maximum(raw, 0.0) + jnp.log1p(jnp.exp(-jnp.abs(raw)))
    lasts = []
    shares = []
    for b in range(2):
        part = step[128 * b : 128 * b + 128]
        cum = exact_dot(ones_lower, -part * par_ref[1:2, :])
        cum_s[128 * b : 128 * b + 128, :] = cum
        cum_t[b] = jnp.transpose(cum)[0:16]
        step_t[b] = jnp.transpose(part)[0:16]
        last = cum[127:128]
        lasts.append(last)
        shares.append(part * jnp.exp(last - cum))
    top = jnp.max(top_ref[...], axis=0, keepdims=True)
    first_row = lax.broadcasted_iota(jnp.int32, (8, 128), 0) == 0
    tiles[here] = jnp.where(first_row, lasts[0] + lasts[1], top)

    pl.semaphore_wait(barrier, count - 1)

    next_z = lax.rem(z + 1, NZ)
    next_x = lax.rem(x + (z + 1) // NZ, NX)
    halo_copies = [
        remote(ref.at[pl.ds(240, 16)], dst, halo_send.at[i], halo_recv.at[i], (next_x, next_z, y, c))
        for i, (ref, dst) in enumerate(((x_ref, halo_x), (bc_ref, halo_bc)))
    ]
    for copy in halo_copies:
        copy.start()

    def tile_copy(rel):
        return remote(
            tiles.at[here], tiles.at[here], tile_send.at[rel], tile_recv.at[rel], at(rel)
        )

    def send_tile(rel, carry):
        tile_copy(rel).start()
        return carry

    lax.fori_loop(1, count, send_tile, 0)

    init_t[...] = jnp.transpose(
        init_ref[pl.ds(pl.multiple_of(x * 256, 256), 256), :]
    )

    for b in range(2):
        rows = slice(128 * b, 128 * b + 128)
        ext[8 + 128 * b : 136 + 128 * b, 0:1024] = x_ref[rows, :].astype(f32)
        ext[8 + 128 * b : 136 + 128 * b, 1024:1280] = bc_ref[rows, :].astype(f32)
    for copy in halo_copies:
        copy.wait_recv()
    leading = here == 0
    ext[5:8, 0:1024] = jnp.where(
        leading, state_x_ref[...].astype(f32), halo_x[...].astype(f32)[13:16]
    )
    ext[5:8, 1024:1280] = jnp.where(
        leading, state_bc_ref[...].astype(f32), halo_bc[...].astype(f32)[13:16]
    )
    for b in range(2):
        for col in range(0, 1280, 256):
            cols = slice(col, col + 256)
            taps = conv_bc_ref[...] if col == 1024 else conv_x_ref[:, cols]
            total = taps[0:1] * ext[5 + 128 * b : 133 + 128 * b, cols]
            for k in range(1, KERNEL):
                total = total + taps[k : k + 1] * ext[5 + k + 128 * b : 133 + k + 128 * b, cols]
            value = (total / (1.0 + jnp.exp(-total))).astype(bf16)
            if col == 1024:
                bc_act[128 * b : 128 * b + 128, :] = value
            else:
                x_act[128 * b : 128 * b + 128, cols] = value

    growth1 = exact_dot(jnp.exp(jnp.broadcast_to(lasts[1], (8, 128))), expand[...])[0:1]
    for b in range(2):
        rows = slice(128 * b, 128 * b + 128)
        weighted = (x_act[rows, :].astype(f32) * exact_dot(shares[b], expand[...])).astype(bf16)
        added = lax.dot_general(
            bc_act[rows, 0:128], weighted, (((0,), (0,)), ((), ())), preferred_element_type=f32
        )
        if b == 0:
            added0[...] = added
        else:
            device_state[...] = (growth1 * added0[...] + added).astype(bf16)

    def slice_of(xs, zs):
        return (
            pl.ds(pl.multiple_of(zs * 16, 16), 16),
            pl.ds(pl.multiple_of(xs * 256, 256), 256),
        )

    def state_copy(rel):
        tx, tz, _, _ = at(rel)
        return remote(
            device_state.at[slice_of(tx, tz)],
            arrived.at[here],
            st_send.at[rel],
            st_recv.at[rel],
            at(rel),
        )

    growth0 = exact_dot(jnp.exp(jnp.broadcast_to(lasts[0], (8, 128))), expand[...])[0:1]
    skips = exact_dot(jnp.broadcast_to(par_ref[2:3, :], (8, 128)), expand[...])[0:1]
    grown[...] = jnp.concatenate([growth0, skips], axis=0)

    def send_state(rel, carry):
        state_copy(rel).start()
        return carry

    lax.fori_loop(1, count, send_state, 0)
    arrived[here] = device_state[slice_of(x, z)]

    half_lane = lax.broadcasted_iota(jnp.int32, (128, 128), 1) < 64

    def block(b, carry):
        rows = pl.ds(pl.multiple_of(b * 128, 128), 128)
        meet = lax.dot_general(
            bc_act[rows, 128:256],
            bc_act[rows, 0:128],
            (((1,), (1,)), ((), ())),
            preferred_element_type=f32,
        )
        for pair in range(8):
            cols = slice(128 * pair, 128 * pair + 128)
            weights = []
            for h in (2 * pair, 2 * pair + 1):
                gap = cum_s[rows, h : h + 1] - cum_t[b, h : h + 1, :]
                decay = jnp.exp(jnp.where(lower, gap, -1e30))
                weights.append((meet * decay * step_t[b, h : h + 1, :]).astype(bf16))
            values = x_act[rows, cols].astype(f32)
            both = jnp.concatenate(
                [jnp.where(half_lane, values, 0.0), jnp.where(half_lane, 0.0, values)], axis=0
            ).astype(bf16)
            part = jnp.dot(jnp.concatenate(weights, axis=1), both, preferred_element_type=f32)
            acc[rows, cols] = part + grown[1:2, cols] * values
        return carry

    lax.fori_loop(0, 2, block, 0)

    def tile_done(rel, carry):
        sx, sz = source(rel)
        ref = tiles.at[sx * NZ + sz]
        remote(ref, ref, tile_send.at[rel], tile_recv.at[rel], at(rel)).wait_recv()
        return carry

    def state_done(rel, carry):
        sx, sz = source(rel)
        ref = arrived.at[sx * NZ + sz]
        remote(ref, ref, st_send.at[rel], st_recv.at[rel], at(rel)).wait_recv()
        return carry

    lax.fori_loop(1, count, tile_done, 0)
    everything = tiles[...]
    logs = everything[:, 0, :]
    max_out[...] = jnp.broadcast_to(
        jnp.max(jnp.max(everything[:, 1, :], axis=0, keepdims=True), axis=1, keepdims=True), (8, 128)
    )
    decays = exact_dot(
        jnp.exp(logs), expand[:, pl.ds(pl.multiple_of(x * 256, 256), 256)]
    )
    lax.fori_loop(1, count, state_done, 0)
    state = init_t[pl.ds(pl.multiple_of(z * 16, 16), 16), :]
    for s in range(count):
        carried[s] = state.astype(bf16)
        if s < count - 1:
            state = decays[s : s + 1] * state + arrived[s].astype(f32)

    def back_copy(rel):
        tx, tz, _, _ = at(rel)
        return remote(
            carried.at[tx * NZ + tz],
            incoming.at[slice_of(x, z)],
            back_send.at[rel],
            back_recv.at[rel],
            at(rel),
        )

    def send_back(rel, carry):
        back_copy(rel).start()
        return carry

    lax.fori_loop(1, count, send_back, 0)
    incoming[slice_of(x, z)] = carried[here]

    def back_done(rel, carry):
        sx, sz = source(rel)
        ref = incoming.at[slice_of(sx, sz)]
        remote(ref, ref, back_send.at[rel], back_recv.at[rel], at(rel)).wait_recv()
        return carry

    lax.fori_loop(1, count, back_done, 0)

    for b in range(2):
        rows = slice(128 * b, 128 * b + 128)
        entering = incoming[...]
        if b == 1:
            entering = (grown[0:1, :] * entering.astype(f32) + added0[...]).astype(bf16)
        seen = jnp.dot(bc_act[rows, 128:256], entering, preferred_element_type=f32)
        total = acc[rows, :] + exact_dot(jnp.exp(cum_s[rows, :]), expand[...]) * seen
        u_out[rows, :] = (total * gain_ref[...]).astype(bf16)
        squared = total * total
        best = squared[:, 0:128]
        for col in range(128, 1024, 128):
            best = best + squared[:, col : col + 128]
        sq_out[rows, :] = best

    for copy in halo_copies:
        copy.wait_send()

    def sent(rel, carry):
        tile_copy(rel).wait_send()
        state_copy(rel).wait_send()
        back_copy(rel).wait_send()
        return carry

    lax.fori_loop(1, count, sent, 0)


def scan_all(x_whole, bc_whole, dt_raw, top, conv_x, conv_bc, state_x, state_bc, par, init, gain):
    vmem = pl.BlockSpec(memory_space=pltpu.VMEM)
    dma = pltpu.SemaphoreType.DMA
    bf16, f32 = (jnp.bfloat16, jnp.float32)
    count = NX * NZ
    return pl.pallas_call(
        scan_blocks,
        name="scan_blocks",
        out_shape=(
            jax.ShapeDtypeStruct((256, 1024), bf16),
            jax.ShapeDtypeStruct((256, 128), f32),
            jax.ShapeDtypeStruct((8, 128), f32),
        ),
        in_specs=[vmem] * 11,
        out_specs=(vmem, vmem, vmem),
        scratch_shapes=[
            pltpu.VMEM((16, 1024), bf16),
            pltpu.VMEM((16, 256), bf16),
            pltpu.VMEM((264, 1280), f32),
            pltpu.VMEM((256, 1024), bf16),
            pltpu.VMEM((256, 256), bf16),
            pltpu.VMEM((256, 128), f32),
            pltpu.VMEM((2, 16, 128), f32),
            pltpu.VMEM((2, 16, 128), f32),
            pltpu.VMEM((128, 1024), f32),
            pltpu.VMEM((128, 1024), f32),
            pltpu.VMEM((128, 1024), bf16),
            pltpu.VMEM((count, 8, 128), f32),
            pltpu.VMEM((count, 16, 256), bf16),
            pltpu.VMEM((count, 16, 256), bf16),
            pltpu.VMEM((128, 1024), bf16),
            pltpu.VMEM((128, 256), f32),
            pltpu.VMEM((2, 1024), f32),
            pltpu.VMEM((256, 1024), f32),
            dma((2,)),
            dma((2,)),
            dma((count,)),
            dma((count,)),
            dma((count,)),
            dma((count,)),
            dma((count,)),
            dma((count,)),
        ],
        compiler_params=pltpu.CompilerParams(
            collective_id=2, has_side_effects=True, vmem_limit_bytes=48 * 2**20
        ),
    )(x_whole, bc_whole, dt_raw, top, conv_x, conv_bc, state_x, state_bc, par, init, gain)


GROUP_SLOTS = ((0, 4), (-1, 1), (-2, 2), (-3, 3))
GROUP_ORDER = (1, 2, 3, 0)
Y_NAMES = ("two_up", "two_down", "one_up_b", "one_down_a", "one_up_a", "one_down_b")


def out_projection(
    u_ref,
    sq_ref,
    w_ref,
    out_ref,
    tokens,
    weights,
    partial,
    from_core,
    ystage,
    ry1,
    ry2,
    yown,
    yup,
    ydown,
    fstage,
    landed,
    squares,
    local_sem,
    x_send,
    x_recv,
    z_send,
    z_recv,
    sq_send,
    sq_recv,
    c_send,
    c_recv,
    y_send,
    y_recv,
    f_send,
    f_recv,
):
    x, z, y, c = (lax.axis_index(name) for name in ("x", "z", "y", "c"))

    def at(dx=0, dz=0, dy=0, dc=0):
        return (
            lax.rem(x + dx + NX, NX),
            lax.rem(z + dz + NZ, NZ),
            lax.rem(y + dy + NY, NY),
            lax.rem(c + dc, NC),
        )

    def x_of(dx):
        return lax.rem(x + dx + NX, NX)

    def y_of(dy):
        return lax.rem(y + dy + NY, NY)

    def z_cols(slot):
        for g, pair in enumerate(GROUP_SLOTS):
            if slot in pair:
                return pl.ds(256 * g + 128 * pair.index(slot), 128)

    mine = pltpu.make_async_copy(w_ref, weights.at[:, z_cols(0)], local_sem.at[0])
    mine.start()
    mine_u = pltpu.make_async_copy(u_ref, tokens.at[x], local_sem.at[1])
    mine_u.start()
    greet(
        [at(dx=1), at(dx=-1), at(dx=2), at(dz=1), at(dz=-1)]
        + [at(dy=dy, dc=dc) for dy in range(4) for dc in range(2) if (dy, dc) != (0, 0)]
    )
    mine.wait()
    mine_u.wait()

    sends = []

    def go(copy):
        copy.start()
        sends.append(copy)

    def x_copy(p, kind, source, where):
        ref = tokens.at[x_of(source), pl.ds(64 * p, 64)]
        return remote(ref, ref, x_send.at[p, kind], x_recv.at[p, kind], where)

    def x_arrived(p, kind):
        x_copy(p, kind, {0: -1, 1: 1, 2: 2}[kind], at(dx=1)).wait_recv()

    def x_relay_up(p):
        x_arrived(p, 0)
        go(x_copy(p, 2, -1, at(dx=1)))

    def x_relay_down(p):
        x_arrived(p, 1)
        go(x_copy(p, 2, 1, at(dx=-1)))

    def z_copy(j, k, d):
        sign = 1 if d == 0 else -1
        rows = pl.ds(256 * j, 256)
        arrives = -sign * (k + 1)
        if k == 3:
            arrives = 4
        return remote(
            weights.at[rows, z_cols(-sign * k)],
            weights.at[rows, z_cols(arrives)],
            z_send.at[d, j, k],
            z_recv.at[d, j, k],
            at(dz=sign),
        )

    def z_step(j, k, d):
        if k > 0:
            z_copy(j, k - 1, d).wait_recv()
        if k < 3 or j // 2 == d:
            go(z_copy(j, k, d))

    others = [(dy, dc) for dy in range(4) for dc in range(2) if (dy, dc) != (0, 0)]

    def t_index(dy, dc):
        return y_of(dy) * NC + lax.rem(c + dc, NC)

    def sq_copy(n):
        dy, dc = others[n]
        there = pl.ds(pl.multiple_of(t_index(dy, dc) * 32, 32), 32)
        return remote(
            sq_ref.at[there], squares.at[n], sq_send.at[n], sq_recv.at[n], at(dy=dy, dc=dc)
        )

    for p in (0, 1, 2, 3):
        go(x_copy(p, 0, 0, at(dx=1)))
        go(x_copy((p + 2) % 4, 1, 0, at(dx=-1)))
        for d in range(2):
            z_step(p, 0, d)
    for n in range(7):
        go(sq_copy(n))
    z_step(0, 1, 0), z_step(0, 1, 1), z_step(1, 1, 0), z_step(1, 1, 1)
    x_relay_up(0), x_relay_down(2)
    z_step(2, 1, 0), z_step(2, 1, 1), z_step(3, 1, 0), z_step(3, 1, 1)
    x_relay_up(1), x_relay_down(3)
    for j in range(4):
        z_step(j, 2, 0), z_step(j, 2, 1)
    for p in (2, 3):
        x_arrived(p, 0), x_arrived((p + 2) % 4, 1)
    for p in range(4):
        x_arrived(p, 2)

    def cols(g):
        return pl.ds(256 * g, 256)

    def multiply(g):
        def one(slot, carry):
            value = jnp.dot(
                tokens[slot], weights[:, cols(g)], preferred_element_type=jnp.float32
            ).astype(jnp.bfloat16)
            value = value.reshape(NY, NC, 32, 256)
            for core in range(NC):
                partial[g, core, :, slot] = value[:, core]
            return carry

        lax.fori_loop(0, NX, one, 0)

    def c_copy(g):
        other = lax.rem(c + 1, NC)
        return remote(
            partial.at[g, other], from_core.at[g], c_send.at[g], c_recv.at[g], at(dc=1)
        )

    def y_copy(g, name):
        slot, low, dst, sign = {
            "two_up": (2, 0, ry1.at[g], 1),
            "two_down": (2, 2, ry1.at[g], -1),
            "one_up_b": (1, 2, ry2.at[g, 0], 1),
            "one_down_a": (3, 0, ry2.at[g, 1], -1),
            "one_up_a": (1, 0, ry2.at[g, 0], 1),
            "one_down_b": (3, 2, ry2.at[g, 1], -1),
        }[name]
        index = Y_NAMES.index(name)
        return remote(
            ystage.at[g, slot, pl.ds(low, 2)],
            dst.at[pl.ds(low, 2)],
            y_send.at[g, index],
            y_recv.at[g, index],
            at(dy=sign),
        )

    def both_cores(g, dy):
        where = y_of(dy)
        return partial[g, c, where].astype(jnp.float32) + from_core[g, where].astype(jnp.float32)

    def y_first(g):
        c_copy(g).wait_recv()
        ystage[g, 2] = both_cores(g, 2).astype(jnp.bfloat16)
        value = both_cores(g, 1)
        yup[g] = value[0:2]
        ystage[g, 1, 2:4] = value[2:4].astype(jnp.bfloat16)
        go(y_copy(g, "two_up"))
        go(y_copy(g, "two_down"))
        value = both_cores(g, 3)
        ydown[g] = value[2:4]
        ystage[g, 3, 0:2] = value[0:2].astype(jnp.bfloat16)
        go(y_copy(g, "one_up_b"))
        yown[g] = both_cores(g, 0)
        go(y_copy(g, "one_down_a"))

    def y_add(g):
        y_copy(g, "two_up").wait_recv()
        ystage[g, 1, 0:2] = (yup[g] + ry1[g, 0:2].astype(jnp.float32)).astype(jnp.bfloat16)
        y_copy(g, "two_down").wait_recv()
        ystage[g, 3, 2:4] = (ydown[g] + ry1[g, 2:4].astype(jnp.float32)).astype(jnp.bfloat16)
        go(y_copy(g, "one_up_a"))
        go(y_copy(g, "one_down_b"))

    def out_cols(x_slot, g, side):
        block = lax.rem(z + GROUP_SLOTS[g][side] + NZ, NZ)
        return pl.ds(pl.multiple_of(x_slot * 1024 + block * 128, 128), 128)

    def f_copy(g, side, dx):
        return remote(
            fstage.at[g, x_of(dx), :, pl.ds(128 * side, 128)],
            landed.at[:, out_cols(x, g, side)],
            f_send.at[g, side, dx],
            f_recv.at[g, side, dx],
            at(dx=dx),
        )

    def f_arrived(g, side, dx):
        ref = landed.at[:, out_cols(x_of(-dx), g, side)]
        remote(
            ref, ref, f_send.at[g, side, dx], f_recv.at[g, side, dx], at(dx=-dx)
        ).wait_recv()

    def y_final(g):
        for name in ("one_up_b", "one_down_a", "one_up_a", "one_down_b"):
            y_copy(g, name).wait_recv()
        fstage[g] = (
            yown[g] + ry2[g, 0].astype(jnp.float32) + ry2[g, 1].astype(jnp.float32)
        ).astype(jnp.bfloat16)
        here = fstage[g, x]
        for side in range(2):
            landed[:, out_cols(x, g, side)] = here[:, 128 * side : 128 * side + 128]
        for dx in (2, 1, 3):
            for side in range(2):
                go(f_copy(g, side, dx))

    multiply(1)
    go(c_copy(1))
    for j in range(4):
        z_step(j, 3, 0), z_step(j, 3, 1)
    multiply(2)
    go(c_copy(2))
    y_first(1)
    multiply(3)
    go(c_copy(3))
    y_first(2)
    y_add(1)
    for j in range(4):
        z_copy(j, 3, j // 2).wait_recv()
    multiply(0)
    go(c_copy(0))
    y_first(3)
    y_add(2)
    y_final(1)
    y_first(0)
    y_add(3)
    y_final(2)
    y_add(0)
    y_final(3)

    total = sq_ref[pl.ds(pl.multiple_of(t_index(0, 0) * 32, 32), 32), :]
    for n in range(7):
        sq_copy(n).wait_recv()
        total = total + squares[n]
    mean_sq = jnp.sum(total, axis=1, keepdims=True) / (HEADS * HEAD_DIM)
    scale = lax.rsqrt(mean_sq + epsilon)

    y_final(0)
    for g in GROUP_ORDER:
        for dx in (1, 2, 3):
            for side in range(2):
                f_arrived(g, side, dx)
    out_ref[...] = (landed[...].astype(jnp.float32) * scale).astype(jnp.bfloat16)
    for copy in sends:
        copy.wait_send()


def project_out(u, squares, w_out):
    any_place = pl.BlockSpec(memory_space=pl.ANY)
    vmem = pl.BlockSpec(memory_space=pltpu.VMEM)
    dma = pltpu.SemaphoreType.DMA
    bf16, f32 = (jnp.bfloat16, jnp.float32)
    return pl.pallas_call(
        out_projection,
        name="out_projection",
        out_shape=jax.ShapeDtypeStruct((32, 4096), bf16),
        in_specs=[any_place, vmem, any_place],
        out_specs=vmem,
        scratch_shapes=[
            pltpu.VMEM((4, 256, 1024), bf16),
            pltpu.VMEM((1024, 1024), bf16),
            pltpu.VMEM((4, 2, 4, 4, 32, 256), bf16),
            pltpu.VMEM((4, 4, 4, 32, 256), bf16),
            pltpu.VMEM((4, 4, 4, 32, 256), bf16),
            pltpu.VMEM((4, 4, 32, 256), bf16),
            pltpu.VMEM((4, 2, 4, 32, 256), bf16),
            pltpu.VMEM((4, 4, 32, 256), f32),
            pltpu.VMEM((4, 2, 32, 256), f32),
            pltpu.VMEM((4, 2, 32, 256), f32),
            pltpu.VMEM((4, 4, 32, 256), bf16),
            pltpu.VMEM((32, 4096), bf16),
            pltpu.VMEM((7, 32, 128), f32),
            dma((2,)),
            dma((4, 3)),
            dma((4, 3)),
            dma((2, 4, 4)),
            dma((2, 4, 4)),
            dma((7,)),
            dma((7,)),
            dma((4,)),
            dma((4,)),
            dma((4, 6)),
            dma((4, 6)),
            dma((4, 2, 4)),
            dma((4, 2, 4)),
        ],
        compiler_params=pltpu.CompilerParams(
            collective_id=1, has_side_effects=True, vmem_limit_bytes=48 * 2**20
        ),
    )(u, squares, w_out)


def local(
    hidden_in,
    prev_amax,
    w_x,
    w_bc,
    w_dt,
    conv_x,
    conv_bc,
    conv_state_x,
    conv_state_bc,
    dt_bias,
    decay_rate,
    skip,
    init_state,
    norm_gain,
    w_out,
):
    bc_width = w_bc.shape[1] * w_bc.shape[2] * w_bc.shape[3]
    heads = w_dt.shape[1]
    w_bc_dt = jnp.concatenate(
        [
            jnp.reshape(w_bc, (w_bc.shape[0], bc_width)),
            w_dt,
            jnp.zeros((w_dt.shape[0], 128 - heads), w_dt.dtype),
        ],
        axis=1,
    )
    par = jnp.pad(jnp.stack([dt_bias, decay_rate, skip]), ((0, 5), (0, 128 - heads)))
    x_whole, bc_whole, dt_raw, top = project_in(prev_amax, hidden_in, w_x, w_bc_dt)
    u, squares, largest = scan_all(
        x_whole,
        bc_whole,
        dt_raw,
        top,
        conv_x,
        jnp.reshape(conv_bc, (KERNEL, bc_width)),
        conv_state_x,
        jnp.reshape(conv_state_bc, (KERNEL - 1, bc_width)),
        par,
        jnp.reshape(init_state, (heads * HEAD_DIM, STATE)),
        jnp.reshape(norm_gain, (1, -1)),
    )
    layer_out = project_out(u, squares, w_out)
    return (layer_out, largest[0, 0])


def solution(mesh):
    finer = Mesh(mesh.devices.reshape(NX, NZ, NY, NC), SEQ_TENSOR)
    return jax.shard_map(
        local,
        mesh=finer,
        in_specs=(
            P(SEQ_TENSOR, None),
            P(),
            P(SEQ, TENSOR),
            P(SEQ, TENSOR, None, None),
            P(SEQ, TENSOR),
            P(None, TENSOR),
            P(None, TENSOR, None, None),
            P(None, TENSOR),
            P(None, TENSOR, None, None),
            P(TENSOR),
            P(TENSOR),
            P(TENSOR),
            P(TENSOR, None, None),
            P(TENSOR),
            P(TENSOR, SEQ),
        ),
        out_specs=(P(SEQ_TENSOR, None), P()),
        check_vma=False,
    )
```

```python
import jax
import jax.numpy as jnp
from jax import lax
from jax.experimental import pallas as pl
from jax.experimental.pallas import tpu as pltpu
from jax.sharding import Mesh
from jax.sharding import PartitionSpec as P

HEADS = 128
HEAD_DIM = 64
STATE = 128
GROUPS = 8
KERNEL = 4
SPAN = 128
SEQ = ("x", "z")
TENSOR = ("y", "c")
SEQ_TENSOR = SEQ + TENSOR


epsilon = 1e-05
quant_range = 448.0


MESH_ID = pl.DeviceIdType.MESH
NX, NZ, NY, NC = (4, 8, 4, 2)
COUNT = NX * NZ
CHUNKS = (384, 256, 256, 256, 256)
STARTS = (0, 384, 640, 896, 1152)
WIDE = 1408
X_ROWS = 1024
TWO_UP, TWO_DOWN, ONE_UP_B, ONE_DOWN_A, ONE_UP_A, ONE_DOWN_B = range(6)
SLOTS = (0, 4, -1, 1, -2, 2, -3, 3)
(S_HX, S_HY, S_SIB, S_RS, S_HALO, S_TILE, S_ST, S_BACK, S_U, S_O, S_SQ, S_C, S_Y, S_F) = range(14)
S_Z = 14
OTHERS = tuple((dy, dc) for dy in range(NY) for dc in range(NC) if (dy, dc) != (0, 0))


def scratch():
    bf16, f32 = (jnp.bfloat16, jnp.float32)
    v, dma = (pltpu.VMEM, pltpu.SemaphoreType.DMA)
    return [
        v((4, NC, NY, 32, X_ROWS), bf16),
        v((4, 256, X_ROWS), bf16),
        v((X_ROWS, CHUNKS[0]), bf16),
        v((X_ROWS, CHUNKS[1]), bf16),
        v((X_ROWS, CHUNKS[2]), bf16),
        v((X_ROWS, CHUNKS[3]), bf16),
        v((X_ROWS, CHUNKS[4]), bf16),
        v((3, 256, WIDE), bf16),
        v((256, WIDE), bf16),
        v((512, WIDE), bf16),
        v((256, WIDE), f32),
        v((128, WIDE), f32),
        v((128, WIDE), f32),
        v((8, 128), f32),
        v((16, 1280), bf16),
        v((16, 1280), bf16),
        v((264, 1280), f32),
        v((256, 1024), bf16),
        v((256, 256), bf16),
        v((256, 128), f32),
        v((256, 128), f32),
        v((256, 128), f32),
        v((2, 16, 128), f32),
        v((2, 16, 128), f32),
        v((2, 128, 128), f32),
        v((8, 128), f32),
        v((4, 8, 256), f32),
        v((128, 1024), f32),
        v((128, 1024), f32),
        v((128, 1024), bf16),
        v((COUNT, 8, 128), f32),
        v((COUNT, 16, 256), bf16),
        v((COUNT, 16, 256), bf16),
        v((128, 1024), bf16),
        v((128, 256), f32),
        v((256, 1024), f32),
        v((256, 128), f32),
        v((4, 256, 1024), bf16),
        v((1024, 1024), bf16),
        v((4, NC, NY, 32, 1024), bf16),
        v((4, NY, 32, 1024), bf16),
        v((4, NY, 32, 1024), bf16),
        v((4, 32, 1024), bf16),
        v((4, 2, 32, 1024), bf16),
        v((4, 32, 1024), f32),
        v((4, 16, 1024), f32),
        v((4, 16, 1024), f32),
        v((4, 32, 1024), bf16),
        v((4, 32, 1024), bf16),
        v((7, 32, 128), f32),
        dma((8,)),
        dma((19,)),
        dma((4,)),
        dma((4,)),
        dma((4,)),
        dma((2, 5, 3)),
        dma((5,)),
        dma((5, 2)),
        dma((5,)),
        dma((5,)),
        dma((1,)),
        dma((1,)),
        dma((4,)),
        dma((4, 2)),
        dma((3,)),
        dma((2, 4, 3)),
        dma((1,)),
        dma((1,)),
        dma((4,)),
        dma((4, 2)),
        dma((4,)),
        dma((1,)),
    ]


def remote(src, dst, send_sem, recv_sem, where):
    return pltpu.make_async_remote_copy(
        src_ref=src,
        dst_ref=dst,
        send_sem=send_sem,
        recv_sem=recv_sem,
        device_id=where,
        device_id_type=MESH_ID,
    )


def layer(
    amax_ref,
    hid_ref,
    wx_ref,
    wbd_ref,
    conv_x_ref,
    conv_bc_ref,
    state_x_ref,
    state_bc_ref,
    par_ref,
    init_ref,
    gain_ref,
    w_ref,
    out_ref,
    max_out,
    rows,
    quant,
    w0,
    w1,
    w2,
    w3,
    w4,
    stage,
    r1,
    r2,
    own,
    plus,
    minus,
    top,
    tail_out,
    tail_in,
    ext,
    x_act,
    bc_act,
    dt_s,
    cum_s,
    share_s,
    cum_t,
    step_t,
    meet,
    rates,
    grown,
    expand,
    added0,
    device_state,
    tiles,
    arrived,
    carried,
    incoming,
    init_t,
    acc,
    sq,
    tokens,
    weights,
    partial,
    from_core,
    ystage,
    ry1,
    ry2,
    yown,
    yup,
    ydown,
    fstage,
    landed,
    squares,
    local_sem,
    sent_sem,
    hx_recv,
    hy_recv,
    sib_recv,
    z_recv,
    z_last,
    rs_recv,
    rs_last,
    halo_recv,
    tile_recv,
    st_recv,
    back_recv,
    u_recv,
    u_last,
    o_recv,
    o_last,
    sq_recv,
    c_recv,
    y_recv,
    y_last,
    f_recv,
):
    x, z, y, c = (lax.axis_index(name) for name in ("x", "z", "y", "c"))
    here = x * NZ + z
    f32, bf16 = (jnp.float32, jnp.bfloat16)
    wbuf = (w0, w1, w2, w3, w4)

    def at(dx=0, dz=0, dy=0, dc=0):
        return (
            lax.rem(x + dx + NX, NX),
            lax.rem(z + dz + NZ, NZ),
            lax.rem(y + dy + NY, NY),
            lax.rem(c + dc, NC),
        )

    def at_rel(rel):
        return (lax.rem(x + rel // NZ, NX), lax.rem(z + rel % NZ, NZ), y, c)

    def x_of(r):
        return lax.rem(x + r + NX, NX)

    def y_of(dy):
        return lax.rem(y + dy + NY, NY)

    def t_index(dy, dc):
        return y_of(dy) * NC + lax.rem(c + dc, NC)

    def exact_dot(a, b):
        return jnp.dot(a, b, precision=lax.Precision.HIGHEST, preferred_element_type=f32)

    def go(copy):
        copy.start()

    def take(ref, sem):
        remote(ref, ref, sent_sem.at[0], sem, at(dz=1)).wait_recv()

    def drain(ref, index):
        remote(ref, ref, sent_sem.at[index], hx_recv.at[0], at(dz=1)).wait_send()

    def z_rows(dz, low=0, count=128):
        block = lax.rem(z + dz + NZ, NZ)
        return pl.ds(pl.multiple_of(block * 128 + low, count), count)

    def z_cols(slot):
        return pl.ds(128 * SLOTS.index(slot), 128)

    local = []
    for j in range(5):
        src = wbd_ref if j == 0 else wx_ref.at[:, pl.ds(256 * (j - 1), 256)]
        local.append(pltpu.make_async_copy(src, wbuf[j].at[z_rows(0)], local_sem.at[j]))
    local.append(
        pltpu.make_async_copy(
            hid_ref.at[:, pl.ds(pl.multiple_of(x * X_ROWS, X_ROWS), X_ROWS)],
            rows.at[x, c, y],
            local_sem.at[5],
        )
    )
    local.append(pltpu.make_async_copy(w_ref, weights.at[:, z_cols(0)], local_sem.at[6]))
    for copy in local:
        copy.start()

    barrier = pltpu.get_barrier_semaphore()

    def greet(rel, carry):
        pl.semaphore_signal(barrier, inc=1, device_id=at_rel(rel), device_id_type=MESH_ID)
        return carry

    lax.fori_loop(1, COUNT, greet, 0)
    for dy, dc in OTHERS:
        pl.semaphore_signal(barrier, inc=1, device_id=at(dy=dy, dc=dc), device_id_type=MESH_ID)

    lane = lax.broadcasted_iota(jnp.int32, (128, 1024), 1)
    head = lax.broadcasted_iota(jnp.int32, (128, 1024), 0)
    expand[...] = jnp.where((lane >= head * 64) & (lane < head * 64 + 64), 1.0, 0.0).astype(f32)
    row_at = lax.broadcasted_iota(jnp.int32, (128, 128), 0)
    col_at = lax.broadcasted_iota(jnp.int32, (128, 128), 1)
    lower = row_at >= col_at
    ones_lower = jnp.where(lower, 1.0, 0.0).astype(f32)
    init_t[...] = jnp.transpose(init_ref[pl.ds(pl.multiple_of(x * 256, 256), 256), :])
    for copy in local:
        copy.wait()
    pl.semaphore_wait(barrier, COUNT - 1 + len(OTHERS))

    def z_copy(j, k, d):
        sign = 1 if d == 0 else -1
        piece = z_rows(-sign * k) if k < 3 else z_rows(-sign * k, 64 * d, 64)
        ref = wbuf[j].at[piece]
        sem = z_recv.at[d, j, k] if k < 3 else z_last.at[j]
        return remote(ref, ref, sent_sem.at[S_Z + j], sem, at(dz=sign))

    def z_step(j, k):
        for d in range(2):
            if k > 0:
                sign = 1 if d == 0 else -1
                take(wbuf[j].at[z_rows(-sign * k)], z_recv.at[d, j, k - 1])
            go(z_copy(j, k, d))

    def hx_copy(r):
        dest = lax.rem(x + NX - r, NX)
        src = hid_ref.at[:, pl.ds(pl.multiple_of(dest * X_ROWS, X_ROWS), X_ROWS)]
        return remote(src, rows.at[x, c, y], sent_sem.at[S_HX], hx_recv.at[r], at(dx=-r))

    def hy_first(r):
        ref = rows.at[x_of(r), c, y]
        if r > 0:
            take(ref, hx_recv.at[r])
        for dy in (1, 3, 2):
            go(remote(ref, ref, sent_sem.at[S_HY], hy_recv.at[r], at(dy=dy)))

    def hy_pass(r):
        take(rows.at[x_of(r), c, pl.ds(0, 3)], hy_recv.at[r])
        ref = rows.at[x_of(r), c]
        go(remote(ref, ref, sent_sem.at[S_SIB], sib_recv.at[r], at(dc=1)))

    largest = jnp.zeros((8, 128), jnp.float32)
    amax = jnp.full((8, 128), amax_ref[0], jnp.float32)
    factor = (quant_range / amax)[0:1, 0:1]
    in_scale = (amax / quant_range)[0:1, 0:1]
    top[...] = largest

    def quantized(r):
        where = x_of(r)
        take(rows.at[where, lax.rem(c + 1, NC)], sib_recv.at[r])

        def tile(i, carry):
            core, place = (i // NY, lax.rem(i, NY))
            part = pl.ds(pl.multiple_of((place * NC + core) * 32, 32), 32)
            value = rows[where, core, place].astype(jnp.float32)
            quant[where, part, :] = jnp.clip(
                value * factor, -quant_range, quant_range
            ).astype(jnp.bfloat16)
            most = jnp.max(jnp.abs(value).reshape(4, 8, 1024), axis=0)
            best = most[:, 0:128]
            for lane in range(128, 1024, 128):
                best = jnp.maximum(best, most[:, lane : lane + 128])
            top[...] = jnp.maximum(top[...], best)
            return carry

        lax.fori_loop(0, 8, tile, 0)

    def ext_cols(j):
        return slice(1024, 1280) if j == 0 else slice(256 * (j - 1), 256 * j)

    def halo_copy(j):
        next_z = lax.rem(z + 1, NZ)
        next_x = lax.rem(x + (z + 1) // NZ, NX)
        where = (next_x, next_z, y, c)
        part = pl.ds(ext_cols(j).start, 256)
        return remote(
            tail_out.at[:, part], tail_in.at[:, part], sent_sem.at[S_HALO], halo_recv.at[j], where
        )

    def cols(j):
        return pl.ds(STARTS[j], CHUNKS[j])

    def rs_copy(j, name):
        slot, low, dst, dst_low, sign = {
            TWO_UP: (0, 0, r1, 0, 1),
            TWO_DOWN: (0, 128, r1, 128, -1),
            ONE_UP_B: (1, 128, r2, 128, 1),
            ONE_DOWN_A: (2, 0, r2, 256, -1),
            ONE_UP_A: (1, 0, r2, 0, 1),
            ONE_DOWN_B: (2, 128, r2, 384, -1),
        }[name]
        return remote(
            stage.at[slot, pl.ds(low, 128), cols(j)],
            dst.at[pl.ds(dst_low, 128), cols(j)],
            sent_sem.at[S_RS],
            rs_recv.at[j, name] if name < 2 else rs_last.at[j],
            at(dx=sign),
        )

    def product(j, r):
        return jnp.dot(quant[x_of(r)], wbuf[j][...], preferred_element_type=jnp.float32)

    def rs_multiply(j):
        take(wbuf[j].at[pl.ds(0, 128)], z_last.at[j])
        stage[0, :, cols(j)] = product(j, 2).astype(jnp.bfloat16)
        value = product(j, 1)
        plus[:, cols(j)] = value[0:128]
        stage[1, 128:256, cols(j)] = value[128:256].astype(jnp.bfloat16)
        go(rs_copy(j, TWO_UP))
        go(rs_copy(j, TWO_DOWN))
        value = product(j, 3)
        minus[:, cols(j)] = value[128:256]
        stage[2, 0:128, cols(j)] = value[0:128].astype(jnp.bfloat16)
        go(rs_copy(j, ONE_UP_B))
        own[:, cols(j)] = product(j, 0)
        go(rs_copy(j, ONE_DOWN_A))

    def rs_add(j):
        rs_copy(j, TWO_UP).wait_recv()
        stage[1, 0:128, cols(j)] = (
            plus[:, cols(j)] + r1[0:128, cols(j)].astype(jnp.float32)
        ).astype(jnp.bfloat16)
        rs_copy(j, TWO_DOWN).wait_recv()
        stage[2, 128:256, cols(j)] = (
            minus[:, cols(j)] + r1[128:256, cols(j)].astype(jnp.float32)
        ).astype(jnp.bfloat16)
        go(rs_copy(j, ONE_UP_A))
        go(rs_copy(j, ONE_DOWN_B))

    def rs_final(j):
        take(r2.at[:, cols(j)], rs_last.at[j])
        total = (
            own[:, cols(j)]
            + r2[0:256, cols(j)].astype(jnp.float32)
            + r2[256:512, cols(j)].astype(jnp.float32)
        ) * in_scale
        value = total[:, 0:256].astype(bf16)
        ext[8:264, ext_cols(j)] = value.astype(f32)
        tail_out[:, ext_cols(j)] = value[240:256]
        if j == 0:
            dt_s[...] = total[:, 256:384]
        go(halo_copy(j))

    def tile_copy(rel):
        return remote(
            tiles.at[here], tiles.at[here], sent_sem.at[S_TILE], tile_recv.at[0], at_rel(rel)
        )

    def steps():
        raw = dt_s[...] + par_ref[0:1, :]
        step = jnp.maximum(raw, 0.0) + jnp.log1p(jnp.exp(-jnp.abs(raw)))
        lasts = []
        for b in range(2):
            part = step[128 * b : 128 * b + 128]
            cum = exact_dot(ones_lower, -part * par_ref[1:2, :])
            cum_s[128 * b : 128 * b + 128, :] = cum
            cum_t[b] = jnp.transpose(cum)[0:16]
            step_t[b] = jnp.transpose(part)[0:16]
            last = cum[127:128]
            lasts.append(last)
            share_s[128 * b : 128 * b + 128, :] = part * jnp.exp(last - cum)
        most = jnp.max(top[...], axis=0, keepdims=True)
        row8 = lax.broadcasted_iota(jnp.int32, (8, 128), 0)
        tiles[here] = jnp.where(row8 == 0, lasts[0] + lasts[1], most)
        rates[...] = jnp.where(
            row8 == 0, jnp.exp(lasts[0]), jnp.where(row8 == 1, jnp.exp(lasts[1]), par_ref[2:3, :])
        )

        def send_tile(rel, carry):
            tile_copy(rel).start()
            return carry

        lax.fori_loop(1, COUNT, send_tile, 0)

    def convolve(j):
        halo_copy(j).wait_recv()
        part = ext_cols(j)
        before = state_bc_ref[...] if j == 0 else state_x_ref[:, part]
        ext[5:8, part] = jnp.where(
            here == 0, before.astype(f32), tail_in[:, part].astype(f32)[13:16]
        )
        taps = conv_bc_ref[...] if j == 0 else conv_x_ref[:, part]
        for b in range(2):
            total = taps[0:1] * ext[5 + 128 * b : 133 + 128 * b, part]
            for k in range(1, KERNEL):
                total = total + taps[k : k + 1] * ext[5 + k + 128 * b : 133 + k + 128 * b, part]
            value = (total / (1.0 + jnp.exp(-total))).astype(bf16)
            if j == 0:
                bc_act[128 * b : 128 * b + 128, :] = value
                meet[b] = lax.dot_general(
                    value[:, 128:256],
                    value[:, 0:128],
                    (((1,), (1,)), ((), ())),
                    preferred_element_type=f32,
                )
            else:
                x_act[128 * b : 128 * b + 128, part] = value

    def slice_of(xs, zs):
        return (
            pl.ds(pl.multiple_of(zs * 16, 16), 16),
            pl.ds(pl.multiple_of(xs * 256, 256), 256),
        )

    def state_copy(g, dz):
        tz = lax.rem(z + dz, NZ)
        return remote(
            device_state.at[pl.ds(pl.multiple_of(tz * 16, 16), 16), pl.ds(256 * g, 256)],
            arrived.at[here],
            sent_sem.at[S_ST],
            st_recv.at[0],
            (g, tz, y, c),
        )

    def add_states(g):
        part = slice(256 * g, 256 * g + 256)
        spread = expand[:, part]
        rate = exact_dot(rates[...], spread)
        grown[g] = rate
        for b in range(2):
            rows_b = slice(128 * b, 128 * b + 128)
            weighted = (
                x_act[rows_b, part].astype(f32) * exact_dot(share_s[rows_b, :], spread)
            ).astype(bf16)
            added = lax.dot_general(
                bc_act[rows_b, 0:128], weighted, (((0,), (0,)), ((), ())), preferred_element_type=f32
            )
            if b == 0:
                added0[:, part] = added
            else:
                device_state[:, part] = (rate[1:2] * added0[:, part] + added).astype(bf16)

        @pl.when(x == g)
        def _():
            arrived[here] = device_state[pl.ds(pl.multiple_of(z * 16, 16), 16), part]

        @pl.when(x != g)
        def _():
            state_copy(g, 0).start()

        for dz in range(1, NZ):
            state_copy(g, dz).start()

    half_lane = lax.broadcasted_iota(jnp.int32, (128, 128), 1) < 64

    def inside(g):
        def block(b, carry):
            rows_b = pl.ds(pl.multiple_of(b * 128, 128), 128)
            for pair in (2 * g, 2 * g + 1):
                part = slice(128 * pair, 128 * pair + 128)
                both_weights = []
                for h in (2 * pair, 2 * pair + 1):
                    gap = cum_s[rows_b, h : h + 1] - cum_t[b, h : h + 1, :]
                    decay = jnp.exp(jnp.where(lower, gap, -1e30))
                    both_weights.append((meet[b] * decay * step_t[b, h : h + 1, :]).astype(bf16))
                values = x_act[rows_b, part].astype(f32)
                both = jnp.concatenate(
                    [jnp.where(half_lane, values, 0.0), jnp.where(half_lane, 0.0, values)], axis=0
                ).astype(bf16)
                result = jnp.dot(
                    jnp.concatenate(both_weights, axis=1), both, preferred_element_type=f32
                )
                low = 128 * (pair - 2 * g)
                acc[rows_b, part] = result + grown[g, 2:3, low : low + 128] * values
            return carry

        lax.fori_loop(0, 2, block, 0)

    def back_copy(rel):
        tx, tz, _, _ = at_rel(rel)
        return remote(
            carried.at[tx * NZ + tz],
            incoming.at[slice_of(x, z)],
            sent_sem.at[S_BACK],
            back_recv.at[x],
            at_rel(rel),
        )

    def chain(g):
        @pl.when(x == g)
        def _():
            take(tiles.at[pl.ds(0, COUNT - 1)], tile_recv.at[0])
            everything = tiles[...]
            best = jnp.max(everything[:, 1, :], axis=0, keepdims=True)
            max_out[...] = jnp.broadcast_to(jnp.max(best, axis=1, keepdims=True), (8, 128))
            decays = exact_dot(jnp.exp(everything[:, 0, :]), expand[:, 256 * g : 256 * g + 256])

            take(arrived.at[pl.ds(0, COUNT - 1)], st_recv.at[0])
            state = init_t[pl.ds(pl.multiple_of(z * 16, 16), 16), :]
            for n in range(COUNT):
                carried[n] = state.astype(bf16)
                if n < COUNT - 1:
                    state = decays[n : n + 1] * state + arrived[n].astype(f32)

            def send_back(rel, carry):
                back_copy(rel).start()
                return carry

            lax.fori_loop(1, COUNT, send_back, 0)
            incoming[slice_of(x, z)] = carried[here]

    def u_copy(g, b, kind, origin, where):
        ref = tokens.at[x_of(origin), pl.ds(128 * b, 128), pl.ds(256 * g, 256)]
        sem = u_recv.at[g, b] if kind == b else u_last.at[kind]
        return remote(ref, ref, sent_sem.at[S_U], sem, where)

    def finish(g):
        part = slice(256 * g, 256 * g + 256)

        @pl.when(x != g)
        def _():
            take(incoming.at[:, part], back_recv.at[g])

        @pl.when(x == g)
        def _():
            take(incoming.at[pl.ds(0, 112), part], back_recv.at[g])

        for b in range(2):
            rows_b = slice(128 * b, 128 * b + 128)
            entering = incoming[:, part]
            if b == 1:
                entering = (grown[g, 0:1, :] * entering.astype(f32) + added0[:, part]).astype(bf16)
            seen = jnp.dot(bc_act[rows_b, 128:256], entering, preferred_element_type=f32)
            total = acc[rows_b, part] + exact_dot(jnp.exp(cum_s[rows_b, :]), expand[:, part]) * seen
            tokens[x, rows_b, part] = (total * gain_ref[:, part]).astype(bf16)
            squared = total * total
            squared = squared[:, 0:128] + squared[:, 128:256]
            sq[rows_b, :] = squared if g == 0 else sq[rows_b, :] + squared
        go(u_copy(g, 0, 0, 0, at(dx=1)))
        go(u_copy(g, 1, 1, 0, at(dx=-1)))
        go(u_copy(g, 1, 0, 0, at(dx=1)))
        go(u_copy(g, 0, 1, 0, at(dx=-1)))

    def u_relay(g):
        take(tokens.at[0, pl.ds(0, 128), pl.ds(0, 256)], u_recv.at[g, 0])
        go(u_copy(g, 0, 2, -1, at(dx=1)))
        take(tokens.at[0, pl.ds(0, 128), pl.ds(0, 256)], u_recv.at[g, 1])
        go(u_copy(g, 1, 2, 1, at(dx=-1)))

    def o_copy(j, k, d):
        sign = 1 if d == 0 else -1
        rows_j = pl.ds(256 * j, 256)
        arrives = 4 if k == 3 else -sign * (k + 1)
        return remote(
            weights.at[rows_j, z_cols(-sign * k)],
            weights.at[rows_j, z_cols(arrives)],
            sent_sem.at[S_O],
            o_recv.at[d, j, k] if k < 3 else o_last.at[0],
            at(dz=sign),
        )

    def o_wave(k, pieces=(0, 1, 2, 3)):
        for j in pieces:
            for d in range(2):
                if k > 0:
                    o_copy(j, k - 1, d).wait_recv()
                if k < 3 or j // 2 == d:
                    go(o_copy(j, k, d))

    def sq_copy(n):
        dy, dc = OTHERS[n]
        there = pl.ds(pl.multiple_of(t_index(dy, dc) * 32, 32), 32)
        return remote(sq.at[there], squares.at[n], sent_sem.at[S_SQ], sq_recv.at[0], at(dy=dy, dc=dc))

    def multiply(r):
        slot = x_of(r)

        def one(n, carry):
            part = pl.ds(pl.multiple_of(n * 256, 256), 256)
            value = jnp.dot(
                tokens[slot], weights[:, part], preferred_element_type=jnp.float32
            ).astype(jnp.bfloat16)
            value = value.reshape(NY, NC, 32, 256)
            for core in range(NC):
                partial[r, core, :, :, part] = value[:, core]
            return carry

        lax.fori_loop(0, 4, one, 0)
        go(c_copy(r))

    def c_copy(r):
        other = lax.rem(c + 1, NC)
        return remote(
            partial.at[r, other], from_core.at[r], sent_sem.at[S_C], c_recv.at[r], at(dc=1)
        )

    def y_copy(r, name):
        slot, low, dst, sign = {
            TWO_UP: (2, 0, ry1.at[r], 1),
            TWO_DOWN: (2, 16, ry1.at[r], -1),
            ONE_UP_B: (1, 16, ry2.at[r, 0], 1),
            ONE_DOWN_A: (3, 0, ry2.at[r, 1], -1),
            ONE_UP_A: (1, 0, ry2.at[r, 0], 1),
            ONE_DOWN_B: (3, 16, ry2.at[r, 1], -1),
        }[name]
        return remote(
            ystage.at[r, slot, pl.ds(low, 16)],
            dst.at[pl.ds(low, 16)],
            sent_sem.at[S_Y],
            y_recv.at[r, name] if name < 2 else y_last.at[r],
            at(dy=sign),
        )

    def both_cores(r, dy):
        where = y_of(dy)
        return partial[r, c, where].astype(jnp.float32) + from_core[r, where].astype(jnp.float32)

    def y_first(r):
        take(from_core.at[r], c_recv.at[r])
        ystage[r, 2] = both_cores(r, 2).astype(jnp.bfloat16)
        value = both_cores(r, 1)
        yup[r] = value[0:16]
        ystage[r, 1, 16:32] = value[16:32].astype(jnp.bfloat16)
        go(y_copy(r, TWO_UP))
        go(y_copy(r, TWO_DOWN))
        value = both_cores(r, 3)
        ydown[r] = value[16:32]
        ystage[r, 3, 0:16] = value[0:16].astype(jnp.bfloat16)
        go(y_copy(r, ONE_UP_B))
        yown[r] = both_cores(r, 0)
        go(y_copy(r, ONE_DOWN_A))

    def y_add(r):
        y_copy(r, TWO_UP).wait_recv()
        ystage[r, 1, 0:16] = (yup[r] + ry1[r, 0:16].astype(jnp.float32)).astype(jnp.bfloat16)
        y_copy(r, TWO_DOWN).wait_recv()
        ystage[r, 3, 16:32] = (ydown[r] + ry1[r, 16:32].astype(jnp.float32)).astype(jnp.bfloat16)
        go(y_copy(r, ONE_UP_A))
        go(y_copy(r, ONE_DOWN_B))

    def y_final(r):
        take(ry2.at[r], y_last.at[r])
        value = (
            yown[r] + ry2[r, 0].astype(jnp.float32) + ry2[r, 1].astype(jnp.float32)
        ).astype(jnp.bfloat16)
        if r == 0:
            landed[x] = value
        else:
            fstage[r] = value
            go(remote(fstage.at[r], landed.at[x], sent_sem.at[S_F], f_recv.at[0], at(dx=r)))

    for r in (1, 3, 2):
        go(hx_copy(r))
    hy_first(0)
    z_step(0, 0)
    z_step(1, 0)
    hy_first(1)
    hy_first(3)
    z_step(0, 1)
    hy_first(2)
    z_step(1, 1)
    hy_pass(0)
    z_step(0, 2)
    z_step(1, 2)
    z_step(2, 0)
    hy_pass(1)
    z_step(0, 3)
    z_step(3, 0)
    hy_pass(3)
    z_step(1, 3)
    z_step(2, 1)
    z_step(4, 0)
    hy_pass(2)
    for r in (0, 1, 3, 2):
        quantized(r)
    rs_multiply(0)
    z_step(3, 1)
    rs_multiply(1)
    z_step(2, 2)
    z_step(3, 2)
    rs_add(0)
    z_step(4, 1)
    z_step(2, 3)
    z_step(3, 3)
    rs_add(1)
    z_step(4, 2)
    rs_multiply(2)
    rs_final(0)
    rs_multiply(3)
    z_step(4, 3)
    o_wave(0)
    steps()
    rs_add(2)
    rs_multiply(4)
    rs_final(1)
    convolve(0)
    rs_add(3)
    convolve(1)
    add_states(0)
    o_wave(1, (0, 1))
    rs_add(4)
    rs_final(2)
    convolve(2)
    add_states(1)
    o_wave(1, (2, 3))
    inside(0)
    rs_final(3)
    chain(0)
    convolve(3)
    add_states(2)
    inside(1)
    o_wave(2)
    rs_final(4)
    chain(1)
    convolve(4)
    add_states(3)
    inside(2)
    inside(3)
    finish(0)
    chain(2)
    o_wave(3)
    finish(1)
    u_relay(0)
    chain(3)
    finish(2)
    u_relay(1)
    finish(3)
    for n in range(7):
        go(sq_copy(n))
    take(weights.at[:, pl.ds(0, 128)], o_last.at[0])
    u_relay(2)
    multiply(0)
    u_relay(3)
    y_first(0)
    take(tokens.at[0, pl.ds(0, 128)], u_last.at[0])
    multiply(3)
    take(tokens.at[0, pl.ds(0, 128)], u_last.at[1])
    y_add(0)
    multiply(1)
    y_first(3)
    take(tokens.at[0], u_last.at[2])
    multiply(2)
    y_first(1)
    y_add(3)
    y_final(0)
    y_first(2)
    y_add(1)
    y_final(3)
    y_add(2)
    y_final(1)

    take(squares, sq_recv.at[0])
    index = t_index(0, 0)
    total = sq[pl.ds(pl.multiple_of(index * 32, 32), 32), :]
    for n in range(7):
        total = total + squares[n]
    mean_sq = jnp.sum(total, axis=1, keepdims=True) / (HEADS * HEAD_DIM)
    scale = lax.rsqrt(mean_sq + epsilon)

    y_final(2)
    drain(rows.at[0, 0, pl.ds(0, 3)], S_HX)
    drain(rows.at[pl.ds(0, 3), 0], S_HY)
    drain(rows.at[:, 0], S_SIB)
    for j in range(5):
        drain(wbuf[j].at[pl.ds(0, 896)], S_Z + j)
    drain(stage, S_RS)
    drain(tail_out, S_HALO)
    drain(tiles.at[pl.ds(0, COUNT - 1)], S_TILE)
    drain(arrived.at[pl.ds(0, COUNT - 1)], S_ST)
    drain(arrived.at[pl.ds(0, COUNT - 1)], S_BACK)
    drain(tokens.at[pl.ds(0, 3)], S_U)
    drain(weights.at[pl.ds(0, 896)], S_O)
    drain(squares, S_SQ)
    drain(from_core, S_C)
    drain(ystage.at[:, pl.ds(0, 3)], S_Y)
    drain(fstage.at[pl.ds(0, 3)], S_F)
    take(landed.at[pl.ds(0, 3)], f_recv.at[0])
    for block in range(NX):
        for n, slot in enumerate(SLOTS):
            place = lax.rem(z + slot + NZ, NZ)
            part = pl.ds(pl.multiple_of(1024 * block + place * 128, 128), 128)
            value = landed[block, :, 128 * n : 128 * n + 128].astype(f32)
            out_ref[:, part] = (value * scale).astype(bf16)


def run_layer(*arrays):
    vmem = pl.BlockSpec(memory_space=pltpu.VMEM)
    any_place = pl.BlockSpec(memory_space=pl.ANY)
    return pl.pallas_call(
        layer,
        name="layer",
        out_shape=(
            jax.ShapeDtypeStruct((32, 4096), jnp.bfloat16),
            jax.ShapeDtypeStruct((8, 128), jnp.float32),
        ),
        in_specs=[pl.BlockSpec(memory_space=pltpu.SMEM)]
        + [any_place] * 3
        + [vmem] * 7
        + [any_place],
        out_specs=(vmem, vmem),
        scratch_shapes=scratch(),
        compiler_params=pltpu.CompilerParams(
            collective_id=0, has_side_effects=True, vmem_limit_bytes=60 * 2**20
        ),
    )(*arrays)


def local(
    hidden_in,
    prev_amax,
    w_x,
    w_bc,
    w_dt,
    conv_x,
    conv_bc,
    conv_state_x,
    conv_state_bc,
    dt_bias,
    decay_rate,
    skip,
    init_state,
    norm_gain,
    w_out,
):
    bc_width = w_bc.shape[1] * w_bc.shape[2] * w_bc.shape[3]
    heads = w_dt.shape[1]
    w_bc_dt = jnp.concatenate(
        [
            jnp.reshape(w_bc, (w_bc.shape[0], bc_width)),
            w_dt,
            jnp.zeros((w_dt.shape[0], 128 - heads), w_dt.dtype),
        ],
        axis=1,
    )
    layer_out, largest = run_layer(
        jnp.reshape(prev_amax, (1,)),
        hidden_in,
        w_x,
        w_bc_dt,
        conv_x,
        jnp.reshape(conv_bc, (KERNEL, bc_width)),
        conv_state_x,
        jnp.reshape(conv_state_bc, (KERNEL - 1, bc_width)),
        jnp.pad(jnp.stack([dt_bias, decay_rate, skip]), ((0, 5), (0, 128 - heads))),
        jnp.reshape(init_state, (heads * HEAD_DIM, STATE)),
        jnp.reshape(norm_gain, (1, -1)),
        w_out,
    )
    return (layer_out, largest[0, 0])


def solution(mesh):
    finer = Mesh(mesh.devices.reshape(NX, NZ, NY, NC), SEQ_TENSOR)
    return jax.shard_map(
        local,
        mesh=finer,
        in_specs=(
            P(SEQ_TENSOR, None),
            P(),
            P(SEQ, TENSOR),
            P(SEQ, TENSOR, None, None),
            P(SEQ, TENSOR),
            P(None, TENSOR),
            P(None, TENSOR, None, None),
            P(None, TENSOR),
            P(None, TENSOR, None, None),
            P(TENSOR),
            P(TENSOR),
            P(TENSOR),
            P(TENSOR, None, None),
            P(TENSOR),
            P(TENSOR, SEQ),
        ),
        out_specs=(P(SEQ_TENSOR, None), P()),
        check_vma=False,
    )
```

```python
import jax
import jax.numpy as jnp
from jax import lax
from jax.experimental import pallas as pl
from jax.experimental.pallas import tpu as pltpu
from jax.sharding import Mesh
from jax.sharding import PartitionSpec as P

HEADS = 128
HEAD_DIM = 64
STATE = 128
GROUPS = 8
KERNEL = 4
SPAN = 128
SEQ = ("x", "z")
TENSOR = ("y", "c")
SEQ_TENSOR = SEQ + TENSOR


epsilon = 1e-05
quant_range = 448.0


MESH_ID = pl.DeviceIdType.MESH
NX, NZ, NY, NC = (4, 8, 4, 2)
COUNT = NX * NZ
CHUNKS = (384, 256, 256, 256, 256)
STARTS = (0, 384, 640, 896, 1152)
WIDE = 1408
X_ROWS = 1024
TWO_UP, TWO_DOWN, ONE_UP_B, ONE_DOWN_A, ONE_UP_A, ONE_DOWN_B = range(6)
SLOTS = (0, 4, -1, 1, -2, 2, -3, 3)
(S_HX, S_HY, S_SIB, S_RS, S_HALO, S_TILE, S_ST, S_BACK, S_U, S_O, S_SQ, S_C, S_Y, S_F) = range(14)
S_Z = 14
OTHERS = tuple((dy, dc) for dy in range(NY) for dc in range(NC) if (dy, dc) != (0, 0))


def scratch():
    bf16, f32 = (jnp.bfloat16, jnp.float32)
    v, dma = (pltpu.VMEM, pltpu.SemaphoreType.DMA)
    return [
        v((8, 128), f32),
        v((4, NC, NY, 32, X_ROWS), bf16),
        v((4, 256, X_ROWS), bf16),
        v((X_ROWS, CHUNKS[0]), bf16),
        v((X_ROWS, CHUNKS[1]), bf16),
        v((X_ROWS, CHUNKS[2]), bf16),
        v((X_ROWS, CHUNKS[3]), bf16),
        v((X_ROWS, CHUNKS[4]), bf16),
        v((3, 256, WIDE), bf16),
        v((256, WIDE), bf16),
        v((512, WIDE), bf16),
        v((256, WIDE), f32),
        v((128, WIDE), f32),
        v((128, WIDE), f32),
        v((8, 128), f32),
        v((16, 1280), bf16),
        v((16, 1280), bf16),
        v((264, 1280), f32),
        v((256, 1024), bf16),
        v((256, 256), bf16),
        v((256, 128), f32),
        v((256, 128), f32),
        v((256, 128), f32),
        v((2, 16, 128), f32),
        v((2, 16, 128), f32),
        v((2, 128, 128), f32),
        v((8, 128), f32),
        v((4, 8, 256), f32),
        v((128, 1024), f32),
        v((128, 1024), f32),
        v((128, 1024), bf16),
        v((COUNT, 8, 128), f32),
        v((COUNT, 16, 256), bf16),
        v((COUNT, 16, 256), bf16),
        v((128, 1024), bf16),
        v((128, 256), f32),
        v((256, 1024), f32),
        v((256, 128), f32),
        v((4, 256, 1024), bf16),
        v((1024, 1024), bf16),
        v((4, NC, NY, 32, 1024), bf16),
        v((4, NY, 32, 1024), bf16),
        v((4, NY, 32, 1024), bf16),
        v((4, 32, 1024), bf16),
        v((4, 2, 32, 1024), bf16),
        v((4, 32, 1024), f32),
        v((4, 16, 1024), f32),
        v((4, 16, 1024), f32),
        v((4, 32, 1024), bf16),
        v((4, 32, 1024), bf16),
        v((7, 32, 128), f32),
        dma((8,)),
        dma((19,)),
        dma((4,)),
        dma((4,)),
        dma((4,)),
        dma((2, 5, 3)),
        dma((5,)),
        dma((5, 2)),
        dma((5,)),
        dma((5,)),
        dma((1,)),
        dma((1,)),
        dma((4,)),
        dma((4, 2)),
        dma((3,)),
        dma((2, 4, 3)),
        dma((1,)),
        dma((1,)),
        dma((4,)),
        dma((4, 2)),
        dma((4,)),
        dma((1,)),
    ]


def remote(src, dst, send_sem, recv_sem, where):
    return pltpu.make_async_remote_copy(
        src_ref=src,
        dst_ref=dst,
        send_sem=send_sem,
        recv_sem=recv_sem,
        device_id=where,
        device_id_type=MESH_ID,
    )


def layer(
    amax_ref,
    hid_ref,
    wx_ref,
    wbc_ref,
    wdt_ref,
    conv_x_ref,
    conv_bc_ref,
    state_x_ref,
    state_bc_ref,
    bias_ref,
    decay_ref,
    skip_ref,
    init_ref,
    gain_ref,
    w_ref,
    out_ref,
    max_out,
    par_ref,
    rows,
    quant,
    w0,
    w1,
    w2,
    w3,
    w4,
    stage,
    r1,
    r2,
    own,
    plus,
    minus,
    top,
    tail_out,
    tail_in,
    ext,
    x_act,
    bc_act,
    dt_s,
    cum_s,
    share_s,
    cum_t,
    step_t,
    meet,
    rates,
    grown,
    expand,
    added0,
    device_state,
    tiles,
    arrived,
    carried,
    incoming,
    init_t,
    acc,
    sq,
    tokens,
    weights,
    partial,
    from_core,
    ystage,
    ry1,
    ry2,
    yown,
    yup,
    ydown,
    fstage,
    landed,
    squares,
    local_sem,
    sent_sem,
    hx_recv,
    hy_recv,
    sib_recv,
    z_recv,
    z_last,
    rs_recv,
    rs_last,
    halo_recv,
    tile_recv,
    st_recv,
    back_recv,
    u_recv,
    u_last,
    o_recv,
    o_last,
    sq_recv,
    c_recv,
    y_recv,
    y_last,
    f_recv,
):
    x, z, y, c = (lax.axis_index(name) for name in ("x", "z", "y", "c"))
    here = x * NZ + z
    f32, bf16 = (jnp.float32, jnp.bfloat16)
    wbuf = (w0, w1, w2, w3, w4)

    def at(dx=0, dz=0, dy=0, dc=0):
        return (
            lax.rem(x + dx + NX, NX),
            lax.rem(z + dz + NZ, NZ),
            lax.rem(y + dy + NY, NY),
            lax.rem(c + dc, NC),
        )

    def at_rel(rel):
        return (lax.rem(x + rel // NZ, NX), lax.rem(z + rel % NZ, NZ), y, c)

    def x_of(r):
        return lax.rem(x + r + NX, NX)

    def y_of(dy):
        return lax.rem(y + dy + NY, NY)

    def t_index(dy, dc):
        return y_of(dy) * NC + lax.rem(c + dc, NC)

    def exact_dot(a, b):
        return jnp.dot(a, b, precision=lax.Precision.HIGHEST, preferred_element_type=f32)

    def go(copy):
        copy.start()

    def take(ref, sem):
        remote(ref, ref, sent_sem.at[0], sem, at(dz=1)).wait_recv()

    def drain(ref, index):
        remote(ref, ref, sent_sem.at[index], hx_recv.at[0], at(dz=1)).wait_send()

    def z_rows(dz, low=0, count=128):
        block = lax.rem(z + dz + NZ, NZ)
        return pl.ds(pl.multiple_of(block * 128 + low, count), count)

    def z_cols(slot):
        return pl.ds(128 * SLOTS.index(slot), 128)

    barrier = pltpu.get_barrier_semaphore()

    def greet(rel, carry):
        pl.semaphore_signal(barrier, inc=1, device_id=at_rel(rel), device_id_type=MESH_ID)
        return carry

    lax.fori_loop(1, COUNT, greet, 0)
    for dy, dc in OTHERS:
        pl.semaphore_signal(barrier, inc=1, device_id=at(dy=dy, dc=dc), device_id_type=MESH_ID)

    local = [
        pltpu.make_async_copy(
            wx_ref.at[:, pl.ds(256 * (j - 1), 256)], wbuf[j].at[z_rows(0)], local_sem.at[j]
        )
        for j in range(1, 5)
    ]
    local.append(
        pltpu.make_async_copy(
            hid_ref.at[:, pl.ds(pl.multiple_of(x * X_ROWS, X_ROWS), X_ROWS)],
            rows.at[x, c, y],
            local_sem.at[5],
        )
    )
    local.append(pltpu.make_async_copy(w_ref, weights.at[:, z_cols(0)], local_sem.at[6]))
    for copy in local:
        copy.start()

    maps = wbc_ref[...].astype(f32)
    wbuf[0][z_rows(0), 0:128] = maps[:, 0, 0, :].astype(bf16)
    wbuf[0][z_rows(0), 128:256] = maps[:, 0, 1, :].astype(bf16)
    for_steps = jnp.concatenate([wdt_ref[...].astype(f32), jnp.zeros((112, 128), f32)], axis=0)
    wbuf[0][z_rows(0), 256:384] = jnp.transpose(for_steps).astype(bf16)
    par_ref[...] = jnp.zeros((8, 128), f32)
    par_ref[0:1, 0:16] = bias_ref[...]
    par_ref[1:2, 0:16] = decay_ref[...]
    par_ref[2:3, 0:16] = skip_ref[...]

    def side_by_side(ref, k):
        pair = ref[k, 0].astype(f32)
        return jnp.concatenate([pair[0:1], pair[1:2]], axis=1)

    lane = lax.broadcasted_iota(jnp.int32, (128, 1024), 1)
    head = lax.broadcasted_iota(jnp.int32, (128, 1024), 0)
    expand[...] = jnp.where((lane >= head * 64) & (lane < head * 64 + 64), 1.0, 0.0).astype(f32)
    row_at = lax.broadcasted_iota(jnp.int32, (128, 128), 0)
    col_at = lax.broadcasted_iota(jnp.int32, (128, 128), 1)
    lower = row_at >= col_at
    ones_lower = jnp.where(lower, 1.0, 0.0).astype(f32)
    init_t[...] = jnp.transpose(init_ref[pl.ds(pl.multiple_of(x * 256, 256), 256), :])
    for copy in local:
        copy.wait()
    pl.semaphore_wait(barrier, COUNT - 1 + len(OTHERS))

    def z_copy(j, k, d):
        sign = 1 if d == 0 else -1
        piece = z_rows(-sign * k) if k < 3 else z_rows(-sign * k, 64 * d, 64)
        ref = wbuf[j].at[piece]
        sem = z_recv.at[d, j, k] if k < 3 else z_last.at[j]
        return remote(ref, ref, sent_sem.at[S_Z + j], sem, at(dz=sign))

    def z_step(j, k):
        for d in range(2):
            if k > 0:
                sign = 1 if d == 0 else -1
                take(wbuf[j].at[z_rows(-sign * k)], z_recv.at[d, j, k - 1])
            go(z_copy(j, k, d))

    def hx_copy(r):
        dest = lax.rem(x + NX - r, NX)
        src = hid_ref.at[:, pl.ds(pl.multiple_of(dest * X_ROWS, X_ROWS), X_ROWS)]
        return remote(src, rows.at[x, c, y], sent_sem.at[S_HX], hx_recv.at[r], at(dx=-r))

    def hy_first(r):
        ref = rows.at[x_of(r), c, y]
        if r > 0:
            take(ref, hx_recv.at[r])
        for dy in (1, 3, 2):
            go(remote(ref, ref, sent_sem.at[S_HY], hy_recv.at[r], at(dy=dy)))

    def hy_pass(r):
        take(rows.at[x_of(r), c, pl.ds(0, 3)], hy_recv.at[r])
        ref = rows.at[x_of(r), c]
        go(remote(ref, ref, sent_sem.at[S_SIB], sib_recv.at[r], at(dc=1)))

    largest = jnp.zeros((8, 128), jnp.float32)
    amax = jnp.full((8, 128), amax_ref[0], jnp.float32)
    factor = (quant_range / amax)[0:1, 0:1]
    in_scale = (amax / quant_range)[0:1, 0:1]
    top[...] = largest

    def quantized(r):
        where = x_of(r)
        take(rows.at[where, lax.rem(c + 1, NC)], sib_recv.at[r])

        def tile(i, carry):
            core, place = (i // NY, lax.rem(i, NY))
            part = pl.ds(pl.multiple_of((place * NC + core) * 32, 32), 32)
            value = rows[where, core, place].astype(jnp.float32)
            quant[where, part, :] = jnp.clip(
                value * factor, -quant_range, quant_range
            ).astype(jnp.bfloat16)
            most = jnp.max(jnp.abs(value).reshape(4, 8, 1024), axis=0)
            best = most[:, 0:128]
            for lane in range(128, 1024, 128):
                best = jnp.maximum(best, most[:, lane : lane + 128])
            top[...] = jnp.maximum(top[...], best)
            return carry

        lax.fori_loop(0, 8, tile, 0)

    def ext_cols(j):
        return slice(1024, 1280) if j == 0 else slice(256 * (j - 1), 256 * j)

    def halo_copy(j):
        next_z = lax.rem(z + 1, NZ)
        next_x = lax.rem(x + (z + 1) // NZ, NX)
        where = (next_x, next_z, y, c)
        part = pl.ds(ext_cols(j).start, 256)
        return remote(
            tail_out.at[:, part], tail_in.at[:, part], sent_sem.at[S_HALO], halo_recv.at[j], where
        )

    def cols(j):
        return pl.ds(STARTS[j], CHUNKS[j])

    def rs_copy(j, name):
        slot, low, dst, dst_low, sign = {
            TWO_UP: (0, 0, r1, 0, 1),
            TWO_DOWN: (0, 128, r1, 128, -1),
            ONE_UP_B: (1, 128, r2, 128, 1),
            ONE_DOWN_A: (2, 0, r2, 256, -1),
            ONE_UP_A: (1, 0, r2, 0, 1),
            ONE_DOWN_B: (2, 128, r2, 384, -1),
        }[name]
        return remote(
            stage.at[slot, pl.ds(low, 128), cols(j)],
            dst.at[pl.ds(dst_low, 128), cols(j)],
            sent_sem.at[S_RS],
            rs_recv.at[j, name] if name < 2 else rs_last.at[j],
            at(dx=sign),
        )

    def product(j, r):
        return jnp.dot(quant[x_of(r)], wbuf[j][...], preferred_element_type=jnp.float32)

    def rs_multiply(j):
        take(wbuf[j].at[pl.ds(0, 128)], z_last.at[j])
        stage[0, :, cols(j)] = product(j, 2).astype(jnp.bfloat16)
        value = product(j, 1)
        plus[:, cols(j)] = value[0:128]
        stage[1, 128:256, cols(j)] = value[128:256].astype(jnp.bfloat16)
        go(rs_copy(j, TWO_UP))
        go(rs_copy(j, TWO_DOWN))
        value = product(j, 3)
        minus[:, cols(j)] = value[128:256]
        stage[2, 0:128, cols(j)] = value[0:128].astype(jnp.bfloat16)
        go(rs_copy(j, ONE_UP_B))
        own[:, cols(j)] = product(j, 0)
        go(rs_copy(j, ONE_DOWN_A))

    def rs_add(j):
        rs_copy(j, TWO_UP).wait_recv()
        stage[1, 0:128, cols(j)] = (
            plus[:, cols(j)] + r1[0:128, cols(j)].astype(jnp.float32)
        ).astype(jnp.bfloat16)
        rs_copy(j, TWO_DOWN).wait_recv()
        stage[2, 128:256, cols(j)] = (
            minus[:, cols(j)] + r1[128:256, cols(j)].astype(jnp.float32)
        ).astype(jnp.bfloat16)
        go(rs_copy(j, ONE_UP_A))
        go(rs_copy(j, ONE_DOWN_B))

    def rs_final(j):
        take(r2.at[:, cols(j)], rs_last.at[j])
        total = (
            own[:, cols(j)]
            + r2[0:256, cols(j)].astype(jnp.float32)
            + r2[256:512, cols(j)].astype(jnp.float32)
        ) * in_scale
        value = total[:, 0:256].astype(bf16)
        ext[8:264, ext_cols(j)] = value.astype(f32)
        tail_out[:, ext_cols(j)] = value[240:256]
        if j == 0:
            dt_s[...] = total[:, 256:384]
        go(halo_copy(j))

    def tile_copy(rel):
        return remote(
            tiles.at[here], tiles.at[here], sent_sem.at[S_TILE], tile_recv.at[0], at_rel(rel)
        )

    def steps():
        raw = dt_s[...] + par_ref[0:1, :]
        step = jnp.maximum(raw, 0.0) + jnp.log1p(jnp.exp(-jnp.abs(raw)))
        lasts = []
        for b in range(2):
            part = step[128 * b : 128 * b + 128]
            cum = exact_dot(ones_lower, -part * par_ref[1:2, :])
            cum_s[128 * b : 128 * b + 128, :] = cum
            cum_t[b] = jnp.transpose(cum)[0:16]
            step_t[b] = jnp.transpose(part)[0:16]
            last = cum[127:128]
            lasts.append(last)
            share_s[128 * b : 128 * b + 128, :] = part * jnp.exp(last - cum)
        most = jnp.max(top[...], axis=0, keepdims=True)
        row8 = lax.broadcasted_iota(jnp.int32, (8, 128), 0)
        tiles[here] = jnp.where(row8 == 0, lasts[0] + lasts[1], most)
        rates[...] = jnp.where(
            row8 == 0, jnp.exp(lasts[0]), jnp.where(row8 == 1, jnp.exp(lasts[1]), par_ref[2:3, :])
        )

        def send_tile(rel, carry):
            tile_copy(rel).start()
            return carry

        lax.fori_loop(1, COUNT, send_tile, 0)

    def convolve(j):
        halo_copy(j).wait_recv()
        part = ext_cols(j)
        if j == 0:
            before = jnp.concatenate([side_by_side(state_bc_ref, k) for k in range(3)], axis=0)
            taps = jnp.concatenate([side_by_side(conv_bc_ref, k) for k in range(KERNEL)], axis=0)
        else:
            before, taps = (state_x_ref[:, part].astype(f32), conv_x_ref[:, part])
        ext[5:8, part] = jnp.where(
            here == 0, before, tail_in[:, part].astype(f32)[13:16]
        )
        for b in range(2):
            total = taps[0:1] * ext[5 + 128 * b : 133 + 128 * b, part]
            for k in range(1, KERNEL):
                total = total + taps[k : k + 1] * ext[5 + k + 128 * b : 133 + k + 128 * b, part]
            value = (total / (1.0 + jnp.exp(-total))).astype(bf16)
            if j == 0:
                bc_act[128 * b : 128 * b + 128, :] = value
                meet[b] = lax.dot_general(
                    value[:, 128:256],
                    value[:, 0:128],
                    (((1,), (1,)), ((), ())),
                    preferred_element_type=f32,
                )
            else:
                x_act[128 * b : 128 * b + 128, part] = value

    def slice_of(xs, zs):
        return (
            pl.ds(pl.multiple_of(zs * 16, 16), 16),
            pl.ds(pl.multiple_of(xs * 256, 256), 256),
        )

    def state_copy(g, dz):
        tz = lax.rem(z + dz, NZ)
        return remote(
            device_state.at[pl.ds(pl.multiple_of(tz * 16, 16), 16), pl.ds(256 * g, 256)],
            arrived.at[here],
            sent_sem.at[S_ST],
            st_recv.at[0],
            (g, tz, y, c),
        )

    def add_states(g):
        part = slice(256 * g, 256 * g + 256)
        spread = expand[:, part]
        rate = exact_dot(rates[...], spread)
        grown[g] = rate
        for b in range(2):
            rows_b = slice(128 * b, 128 * b + 128)
            weighted = (
                x_act[rows_b, part].astype(f32) * exact_dot(share_s[rows_b, :], spread)
            ).astype(bf16)
            added = lax.dot_general(
                bc_act[rows_b, 0:128], weighted, (((0,), (0,)), ((), ())), preferred_element_type=f32
            )
            if b == 0:
                added0[:, part] = added
            else:
                device_state[:, part] = (rate[1:2] * added0[:, part] + added).astype(bf16)

        @pl.when(x == g)
        def _():
            arrived[here] = device_state[pl.ds(pl.multiple_of(z * 16, 16), 16), part]

        @pl.when(x != g)
        def _():
            state_copy(g, 0).start()

        for dz in range(1, NZ):
            state_copy(g, dz).start()

    half_lane = lax.broadcasted_iota(jnp.int32, (128, 128), 1) < 64

    def inside(g):
        def block(b, carry):
            rows_b = pl.ds(pl.multiple_of(b * 128, 128), 128)
            for pair in (2 * g, 2 * g + 1):
                part = slice(128 * pair, 128 * pair + 128)
                both_weights = []
                for h in (2 * pair, 2 * pair + 1):
                    gap = cum_s[rows_b, h : h + 1] - cum_t[b, h : h + 1, :]
                    decay = jnp.exp(jnp.where(lower, gap, -1e30))
                    both_weights.append((meet[b] * decay * step_t[b, h : h + 1, :]).astype(bf16))
                values = x_act[rows_b, part].astype(f32)
                both = jnp.concatenate(
                    [jnp.where(half_lane, values, 0.0), jnp.where(half_lane, 0.0, values)], axis=0
                ).astype(bf16)
                result = jnp.dot(
                    jnp.concatenate(both_weights, axis=1), both, preferred_element_type=f32
                )
                low = 128 * (pair - 2 * g)
                acc[rows_b, part] = result + grown[g, 2:3, low : low + 128] * values
            return carry

        lax.fori_loop(0, 2, block, 0)

    def back_copy(rel):
        tx, tz, _, _ = at_rel(rel)
        return remote(
            carried.at[tx * NZ + tz],
            incoming.at[slice_of(x, z)],
            sent_sem.at[S_BACK],
            back_recv.at[x],
            at_rel(rel),
        )

    def chain(g):
        @pl.when(x == g)
        def _():
            take(tiles.at[pl.ds(0, COUNT - 1)], tile_recv.at[0])
            everything = tiles[...]
            best = jnp.max(everything[:, 1, :], axis=0, keepdims=True)
            max_out[...] = jnp.max(best, axis=1, keepdims=True)
            decays = exact_dot(jnp.exp(everything[:, 0, :]), expand[:, 256 * g : 256 * g + 256])

            take(arrived.at[pl.ds(0, COUNT - 1)], st_recv.at[0])
            state = init_t[pl.ds(pl.multiple_of(z * 16, 16), 16), :]
            for n in range(COUNT):
                carried[n] = state.astype(bf16)
                if n < COUNT - 1:
                    state = decays[n : n + 1] * state + arrived[n].astype(f32)

            def send_back(rel, carry):
                back_copy(rel).start()
                return carry

            lax.fori_loop(1, COUNT, send_back, 0)
            incoming[slice_of(x, z)] = carried[here]

    def u_copy(g, b, kind, origin, where):
        ref = tokens.at[x_of(origin), pl.ds(128 * b, 128), pl.ds(256 * g, 256)]
        sem = u_recv.at[g, b] if kind == b else u_last.at[kind]
        return remote(ref, ref, sent_sem.at[S_U], sem, where)

    def finish(g):
        part = slice(256 * g, 256 * g + 256)

        @pl.when(x != g)
        def _():
            take(incoming.at[:, part], back_recv.at[g])

        @pl.when(x == g)
        def _():
            take(incoming.at[pl.ds(0, 112), part], back_recv.at[g])

        for b in range(2):
            rows_b = slice(128 * b, 128 * b + 128)
            entering = incoming[:, part]
            if b == 1:
                entering = (grown[g, 0:1, :] * entering.astype(f32) + added0[:, part]).astype(bf16)
            seen = jnp.dot(bc_act[rows_b, 128:256], entering, preferred_element_type=f32)
            total = acc[rows_b, part] + exact_dot(jnp.exp(cum_s[rows_b, :]), expand[:, part]) * seen
            tokens[x, rows_b, part] = (total * gain_ref[:, part]).astype(bf16)
            squared = total * total
            squared = squared[:, 0:128] + squared[:, 128:256]
            sq[rows_b, :] = squared if g == 0 else sq[rows_b, :] + squared
        go(u_copy(g, 0, 0, 0, at(dx=1)))
        go(u_copy(g, 1, 1, 0, at(dx=-1)))
        go(u_copy(g, 1, 0, 0, at(dx=1)))
        go(u_copy(g, 0, 1, 0, at(dx=-1)))

    def u_relay(g):
        take(tokens.at[0, pl.ds(0, 128), pl.ds(0, 256)], u_recv.at[g, 0])
        go(u_copy(g, 0, 2, -1, at(dx=1)))
        take(tokens.at[0, pl.ds(0, 128), pl.ds(0, 256)], u_recv.at[g, 1])
        go(u_copy(g, 1, 2, 1, at(dx=-1)))

    def o_copy(j, k, d):
        sign = 1 if d == 0 else -1
        rows_j = pl.ds(256 * j, 256)
        arrives = 4 if k == 3 else -sign * (k + 1)
        return remote(
            weights.at[rows_j, z_cols(-sign * k)],
            weights.at[rows_j, z_cols(arrives)],
            sent_sem.at[S_O],
            o_recv.at[d, j, k] if k < 3 else o_last.at[0],
            at(dz=sign),
        )

    def o_wave(k, pieces=(0, 1, 2, 3)):
        for j in pieces:
            for d in range(2):
                if k > 0:
                    o_copy(j, k - 1, d).wait_recv()
                if k < 3 or j // 2 == d:
                    go(o_copy(j, k, d))

    def sq_copy(n):
        dy, dc = OTHERS[n]
        there = pl.ds(pl.multiple_of(t_index(dy, dc) * 32, 32), 32)
        return remote(sq.at[there], squares.at[n], sent_sem.at[S_SQ], sq_recv.at[0], at(dy=dy, dc=dc))

    def multiply(r):
        slot = x_of(r)

        def one(n, carry):
            part = pl.ds(pl.multiple_of(n * 256, 256), 256)
            value = jnp.dot(
                tokens[slot], weights[:, part], preferred_element_type=jnp.float32
            ).astype(jnp.bfloat16)
            value = value.reshape(NY, NC, 32, 256)
            for core in range(NC):
                partial[r, core, :, :, part] = value[:, core]
            return carry

        lax.fori_loop(0, 4, one, 0)
        go(c_copy(r))

    def c_copy(r):
        other = lax.rem(c + 1, NC)
        return remote(
            partial.at[r, other], from_core.at[r], sent_sem.at[S_C], c_recv.at[r], at(dc=1)
        )

    def y_copy(r, name):
        slot, low, dst, sign = {
            TWO_UP: (2, 0, ry1.at[r], 1),
            TWO_DOWN: (2, 16, ry1.at[r], -1),
            ONE_UP_B: (1, 16, ry2.at[r, 0], 1),
            ONE_DOWN_A: (3, 0, ry2.at[r, 1], -1),
            ONE_UP_A: (1, 0, ry2.at[r, 0], 1),
            ONE_DOWN_B: (3, 16, ry2.at[r, 1], -1),
        }[name]
        return remote(
            ystage.at[r, slot, pl.ds(low, 16)],
            dst.at[pl.ds(low, 16)],
            sent_sem.at[S_Y],
            y_recv.at[r, name] if name < 2 else y_last.at[r],
            at(dy=sign),
        )

    def both_cores(r, dy):
        where = y_of(dy)
        return partial[r, c, where].astype(jnp.float32) + from_core[r, where].astype(jnp.float32)

    def y_first(r):
        take(from_core.at[r], c_recv.at[r])
        ystage[r, 2] = both_cores(r, 2).astype(jnp.bfloat16)
        value = both_cores(r, 1)
        yup[r] = value[0:16]
        ystage[r, 1, 16:32] = value[16:32].astype(jnp.bfloat16)
        go(y_copy(r, TWO_UP))
        go(y_copy(r, TWO_DOWN))
        value = both_cores(r, 3)
        ydown[r] = value[16:32]
        ystage[r, 3, 0:16] = value[0:16].astype(jnp.bfloat16)
        go(y_copy(r, ONE_UP_B))
        yown[r] = both_cores(r, 0)
        go(y_copy(r, ONE_DOWN_A))

    def y_add(r):
        y_copy(r, TWO_UP).wait_recv()
        ystage[r, 1, 0:16] = (yup[r] + ry1[r, 0:16].astype(jnp.float32)).astype(jnp.bfloat16)
        y_copy(r, TWO_DOWN).wait_recv()
        ystage[r, 3, 16:32] = (ydown[r] + ry1[r, 16:32].astype(jnp.float32)).astype(jnp.bfloat16)
        go(y_copy(r, ONE_UP_A))
        go(y_copy(r, ONE_DOWN_B))

    def y_final(r):
        take(ry2.at[r], y_last.at[r])
        value = (
            yown[r] + ry2[r, 0].astype(jnp.float32) + ry2[r, 1].astype(jnp.float32)
        ).astype(jnp.bfloat16)
        if r == 0:
            landed[x] = value
        else:
            fstage[r] = value
            go(remote(fstage.at[r], landed.at[x], sent_sem.at[S_F], f_recv.at[0], at(dx=r)))

    for r in (1, 3, 2):
        go(hx_copy(r))
    hy_first(0)
    z_step(0, 0)
    z_step(1, 0)
    hy_first(1)
    hy_first(3)
    z_step(0, 1)
    hy_first(2)
    z_step(1, 1)
    hy_pass(0)
    z_step(0, 2)
    hy_pass(1)
    z_step(1, 2)
    z_step(2, 0)
    hy_pass(3)
    z_step(0, 3)
    z_step(3, 0)
    hy_pass(2)
    z_step(1, 3)
    z_step(2, 1)
    z_step(4, 0)
    quantized(0)
    quantized(1)
    quantized(3)
    quantized(2)
    rs_multiply(0)
    z_step(3, 1)
    rs_multiply(1)
    z_step(2, 2)
    z_step(3, 2)
    rs_add(0)
    z_step(4, 1)
    z_step(2, 3)
    z_step(3, 3)
    rs_add(1)
    z_step(4, 2)
    rs_multiply(2)
    rs_multiply(3)
    z_step(4, 3)
    o_wave(0)
    rs_final(0)
    rs_add(2)
    rs_multiply(4)
    steps()
    rs_final(1)
    rs_add(3)
    convolve(0)
    rs_final(2)
    rs_add(4)
    convolve(1)
    add_states(0)
    o_wave(1, (0, 1))
    rs_final(3)
    convolve(2)
    add_states(1)
    o_wave(1, (2, 3))
    rs_final(4)
    convolve(3)
    add_states(2)
    inside(0)
    convolve(4)
    add_states(3)
    o_wave(2, (0, 1))
    chain(0)
    inside(1)
    chain(1)
    inside(2)
    inside(3)
    o_wave(2, (2, 3))
    chain(2)
    chain(3)
    o_wave(3, (0, 1))
    finish(0)
    finish(1)
    u_relay(0)
    o_wave(3, (2, 3))
    finish(2)
    u_relay(1)
    finish(3)
    u_relay(2)
    for n in range(7):
        go(sq_copy(n))
    take(weights.at[:, pl.ds(0, 128)], o_last.at[0])
    multiply(0)
    y_first(0)
    u_relay(3)
    take(tokens.at[0, pl.ds(0, 128)], u_last.at[0])
    multiply(3)
    y_add(0)
    take(tokens.at[0, pl.ds(0, 128)], u_last.at[1])
    multiply(1)
    y_first(3)
    take(tokens.at[0], u_last.at[2])
    multiply(2)
    y_first(1)
    y_add(3)
    y_first(2)
    y_add(1)
    y_final(0)
    y_add(2)
    y_final(3)
    y_final(1)

    take(squares, sq_recv.at[0])
    index = t_index(0, 0)
    total = sq[pl.ds(pl.multiple_of(index * 32, 32), 32), :]
    for n in range(7):
        total = total + squares[n]
    mean_sq = jnp.sum(total, axis=1, keepdims=True) / (HEADS * HEAD_DIM)
    scale = lax.rsqrt(mean_sq + epsilon)

    y_final(2)
    drain(rows.at[0, 0, pl.ds(0, 3)], S_HX)
    drain(rows.at[pl.ds(0, 3), 0], S_HY)
    drain(rows.at[:, 0], S_SIB)
    for j in range(5):
        drain(wbuf[j].at[pl.ds(0, 896)], S_Z + j)
    drain(stage, S_RS)
    drain(tail_out, S_HALO)
    drain(tiles.at[pl.ds(0, COUNT - 1)], S_TILE)
    drain(arrived.at[pl.ds(0, COUNT - 1)], S_ST)
    drain(arrived.at[pl.ds(0, COUNT - 1)], S_BACK)
    drain(tokens.at[pl.ds(0, 3)], S_U)
    drain(weights.at[pl.ds(0, 896)], S_O)
    drain(squares, S_SQ)
    drain(from_core, S_C)
    drain(ystage.at[:, pl.ds(0, 3)], S_Y)
    drain(fstage.at[pl.ds(0, 3)], S_F)
    take(landed.at[pl.ds(0, 3)], f_recv.at[0])
    for block in range(NX):
        for n, slot in enumerate(SLOTS):
            place = lax.rem(z + slot + NZ, NZ)
            part = pl.ds(pl.multiple_of(1024 * block + place * 128, 128), 128)
            value = landed[block, :, 128 * n : 128 * n + 128].astype(f32)
            out_ref[:, part] = (value * scale).astype(bf16)


def run_layer(*arrays):
    vmem = pl.BlockSpec(memory_space=pltpu.VMEM)
    any_place = pl.BlockSpec(memory_space=pl.ANY)
    return pl.pallas_call(
        layer,
        name="layer",
        out_shape=(
            jax.ShapeDtypeStruct((32, 4096), jnp.bfloat16),
            jax.ShapeDtypeStruct((1, 1), jnp.float32),
        ),
        in_specs=[pl.BlockSpec(memory_space=pltpu.SMEM)]
        + [any_place] * 2
        + [vmem] * 11
        + [any_place],
        out_specs=(vmem, vmem),
        scratch_shapes=scratch(),
        compiler_params=pltpu.CompilerParams(
            collective_id=0, has_side_effects=True, vmem_limit_bytes=60 * 2**20
        ),
    )(*arrays)


def local(
    hidden_in,
    prev_amax,
    w_x,
    w_bc,
    w_dt,
    conv_x,
    conv_bc,
    conv_state_x,
    conv_state_bc,
    dt_bias,
    decay_rate,
    skip,
    init_state,
    norm_gain,
    w_out,
):
    heads = w_dt.shape[1]
    layer_out, largest = run_layer(
        jnp.reshape(prev_amax, (1,)),
        hidden_in,
        w_x,
        w_bc,
        jnp.transpose(w_dt),
        conv_x,
        conv_bc,
        conv_state_x,
        conv_state_bc,
        jnp.reshape(dt_bias, (1, heads)),
        jnp.reshape(decay_rate, (1, heads)),
        jnp.reshape(skip, (1, heads)),
        jnp.reshape(init_state, (heads * HEAD_DIM, STATE)),
        jnp.reshape(norm_gain, (1, -1)),
        w_out,
    )
    return (layer_out, largest[0, 0])


def solution(mesh):
    finer = Mesh(mesh.devices.reshape(NX, NZ, NY, NC), SEQ_TENSOR)
    return jax.shard_map(
        local,
        mesh=finer,
        in_specs=(
            P(SEQ_TENSOR, None),
            P(),
            P(SEQ, TENSOR),
            P(SEQ, TENSOR, None, None),
            P(SEQ, TENSOR),
            P(None, TENSOR),
            P(None, TENSOR, None, None),
            P(None, TENSOR),
            P(None, TENSOR, None, None),
            P(TENSOR),
            P(TENSOR),
            P(TENSOR),
            P(TENSOR, None, None),
            P(TENSOR),
            P(TENSOR, SEQ),
        ),
        out_specs=(P(SEQ_TENSOR, None), P()),
        check_vma=False,
    )
```

```python
import jax
import jax.numpy as jnp
from jax import lax
from jax.experimental import pallas as pl
from jax.experimental.pallas import tpu as pltpu
from jax.sharding import Mesh
from jax.sharding import PartitionSpec as P

HEADS = 128
HEAD_DIM = 64
STATE = 128
GROUPS = 8
KERNEL = 4
SPAN = 128
SEQ = ("x", "z")
TENSOR = ("y", "c")
SEQ_TENSOR = SEQ + TENSOR


epsilon = 1e-05
quant_range = 448.0


MESH_ID = pl.DeviceIdType.MESH
NX, NZ, NY, NC = (4, 8, 4, 2)
COUNT = NX * NZ
CHUNKS = (384, 256, 256, 256, 256)
STARTS = (0, 384, 640, 896, 1152)
WIDE = 1408
X_ROWS = 1024
TWO_UP, TWO_DOWN, ONE_UP_B, ONE_DOWN_A, ONE_UP_A, ONE_DOWN_B = range(6)
SLOTS = (0, 4, -1, 1, -2, 2, -3, 3)
(S_HX, S_HY, S_SIB, S_RS, S_HALO, S_TILE, S_ST, S_BACK, S_U, S_O, S_SQ, S_C, S_Y, S_F) = range(14)
S_Z = 14
OTHERS = tuple((dy, dc) for dy in range(NY) for dc in range(NC) if (dy, dc) != (0, 0))


def scratch():
    bf16, f32 = (jnp.bfloat16, jnp.float32)
    v, dma = (pltpu.VMEM, pltpu.SemaphoreType.DMA)
    return [
        v((8, 128), f32),
        v((4, NC, NY, 32, X_ROWS), bf16),
        v((4, 256, X_ROWS), bf16),
        v((X_ROWS, CHUNKS[0]), bf16),
        v((X_ROWS, CHUNKS[1]), bf16),
        v((X_ROWS, CHUNKS[2]), bf16),
        v((X_ROWS, CHUNKS[3]), bf16),
        v((X_ROWS, CHUNKS[4]), bf16),
        v((3, 256, WIDE), bf16),
        v((256, WIDE), bf16),
        v((512, WIDE), bf16),
        v((256, WIDE), f32),
        v((128, WIDE), f32),
        v((128, WIDE), f32),
        v((8, 128), f32),
        v((16, 1280), bf16),
        v((16, 1280), bf16),
        v((264, 1280), f32),
        v((256, 1024), bf16),
        v((256, 256), bf16),
        v((256, 128), f32),
        v((256, 128), f32),
        v((256, 128), f32),
        v((2, 16, 128), f32),
        v((2, 16, 128), f32),
        v((2, 128, 128), f32),
        v((8, 128), f32),
        v((4, 8, 256), f32),
        v((128, 1024), f32),
        v((128, 1024), f32),
        v((128, 1024), bf16),
        v((COUNT, 8, 128), f32),
        v((COUNT, 16, 256), bf16),
        v((COUNT, 16, 256), bf16),
        v((128, 1024), bf16),
        v((128, 256), f32),
        v((256, 1024), f32),
        v((256, 128), f32),
        v((4, 256, 1024), bf16),
        v((1024, 1024), bf16),
        v((4, NC, NY, 32, 1024), bf16),
        v((4, NY, 32, 1024), bf16),
        v((4, NY, 32, 1024), bf16),
        v((4, 32, 1024), bf16),
        v((4, 2, 32, 1024), bf16),
        v((4, 32, 1024), f32),
        v((4, 16, 1024), f32),
        v((4, 16, 1024), f32),
        v((4, 32, 1024), bf16),
        v((4, 32, 1024), bf16),
        v((7, 32, 128), f32),
        dma((8,)),
        dma((19,)),
        dma((4,)),
        dma((4,)),
        dma((4,)),
        dma((2, 5, 3)),
        dma((5,)),
        dma((5, 2)),
        dma((5,)),
        dma((5,)),
        dma((1,)),
        dma((1,)),
        dma((4,)),
        dma((4, 2)),
        dma((3,)),
        dma((2, 4, 3)),
        dma((1,)),
        dma((1,)),
        dma((4,)),
        dma((4, 2)),
        dma((4,)),
        dma((1,)),
    ]


def remote(src, dst, send_sem, recv_sem, where):
    return pltpu.make_async_remote_copy(
        src_ref=src,
        dst_ref=dst,
        send_sem=send_sem,
        recv_sem=recv_sem,
        device_id=where,
        device_id_type=MESH_ID,
    )


def layer(
    amax_ref,
    hid_ref,
    wx_ref,
    wbc_ref,
    wdt_ref,
    conv_x_ref,
    conv_bc_ref,
    state_x_ref,
    state_bc_ref,
    bias_ref,
    decay_ref,
    skip_ref,
    init_ref,
    gain_ref,
    w_ref,
    out_ref,
    max_out,
    par_ref,
    rows,
    quant,
    w0,
    w1,
    w2,
    w3,
    w4,
    stage,
    r1,
    r2,
    own,
    plus,
    minus,
    top,
    tail_out,
    tail_in,
    ext,
    x_act,
    bc_act,
    dt_s,
    cum_s,
    share_s,
    cum_t,
    step_t,
    meet,
    rates,
    grown,
    expand,
    added0,
    device_state,
    tiles,
    arrived,
    carried,
    incoming,
    init_t,
    acc,
    sq,
    tokens,
    weights,
    partial,
    from_core,
    ystage,
    ry1,
    ry2,
    yown,
    yup,
    ydown,
    fstage,
    landed,
    squares,
    local_sem,
    sent_sem,
    hx_recv,
    hy_recv,
    sib_recv,
    z_recv,
    z_last,
    rs_recv,
    rs_last,
    halo_recv,
    tile_recv,
    st_recv,
    back_recv,
    u_recv,
    u_last,
    o_recv,
    o_last,
    sq_recv,
    c_recv,
    y_recv,
    y_last,
    f_recv,
):
    x, z, y, c = (lax.axis_index(name) for name in ("x", "z", "y", "c"))
    here = x * NZ + z
    f32, bf16 = (jnp.float32, jnp.bfloat16)
    wbuf = (w0, w1, w2, w3, w4)

    def at(dx=0, dz=0, dy=0, dc=0):
        return (
            lax.rem(x + dx + NX, NX),
            lax.rem(z + dz + NZ, NZ),
            lax.rem(y + dy + NY, NY),
            lax.rem(c + dc, NC),
        )

    def at_rel(rel):
        return (lax.rem(x + rel // NZ, NX), lax.rem(z + rel % NZ, NZ), y, c)

    def x_of(r):
        return lax.rem(x + r + NX, NX)

    def y_of(dy):
        return lax.rem(y + dy + NY, NY)

    def t_index(dy, dc):
        return y_of(dy) * NC + lax.rem(c + dc, NC)

    def exact_dot(a, b):
        return jnp.dot(a, b, precision=lax.Precision.HIGHEST, preferred_element_type=f32)

    def go(copy):
        copy.start()

    def take(ref, sem):
        remote(ref, ref, sent_sem.at[0], sem, at(dz=1)).wait_recv()

    def drain(ref, index):
        remote(ref, ref, sent_sem.at[index], hx_recv.at[0], at(dz=1)).wait_send()

    def z_rows(dz, low=0, count=128):
        block = lax.rem(z + dz + NZ, NZ)
        return pl.ds(pl.multiple_of(block * 128 + low, count), count)

    def z_cols(slot):
        return pl.ds(128 * SLOTS.index(slot), 128)

    barrier = pltpu.get_barrier_semaphore()

    beside = (at(dx=1), at(dx=-1), at(dx=2), at(dz=1), at(dz=-1))
    for peer in beside:
        pl.semaphore_signal(barrier, inc=1, device_id=peer, device_id_type=MESH_ID)
    for dy, dc in OTHERS:
        pl.semaphore_signal(barrier, inc=1, device_id=at(dy=dy, dc=dc), device_id_type=MESH_ID)

    local = [
        pltpu.make_async_copy(
            wx_ref.at[:, pl.ds(256 * (j - 1), 256)], wbuf[j].at[z_rows(0)], local_sem.at[j]
        )
        for j in range(1, 5)
    ]
    local.append(
        pltpu.make_async_copy(
            hid_ref.at[:, pl.ds(pl.multiple_of(x * X_ROWS, X_ROWS), X_ROWS)],
            rows.at[x, c, y],
            local_sem.at[5],
        )
    )
    local.append(pltpu.make_async_copy(w_ref, weights.at[:, z_cols(0)], local_sem.at[6]))
    for copy in local:
        copy.start()

    maps = wbc_ref[...].astype(f32)
    wbuf[0][z_rows(0), 0:128] = maps[:, 0, 0, :].astype(bf16)
    wbuf[0][z_rows(0), 128:256] = maps[:, 0, 1, :].astype(bf16)
    for_steps = jnp.concatenate([wdt_ref[...].astype(f32), jnp.zeros((112, 128), f32)], axis=0)
    wbuf[0][z_rows(0), 256:384] = jnp.transpose(for_steps).astype(bf16)
    par_ref[...] = jnp.zeros((8, 128), f32)
    par_ref[0:1, 0:16] = bias_ref[...]
    par_ref[1:2, 0:16] = decay_ref[...]
    par_ref[2:3, 0:16] = skip_ref[...]

    def side_by_side(ref, k):
        pair = ref[k, 0].astype(f32)
        return jnp.concatenate([pair[0:1], pair[1:2]], axis=1)

    lane = lax.broadcasted_iota(jnp.int32, (128, 1024), 1)
    head = lax.broadcasted_iota(jnp.int32, (128, 1024), 0)
    expand[...] = jnp.where((lane >= head * 64) & (lane < head * 64 + 64), 1.0, 0.0).astype(f32)
    row_at = lax.broadcasted_iota(jnp.int32, (128, 128), 0)
    col_at = lax.broadcasted_iota(jnp.int32, (128, 128), 1)
    lower = row_at >= col_at
    ones_lower = jnp.where(lower, 1.0, 0.0).astype(f32)
    init_t[...] = jnp.transpose(init_ref[pl.ds(pl.multiple_of(x * 256, 256), 256), :])
    for copy in local:
        copy.wait()
    pl.semaphore_wait(barrier, len(beside) + len(OTHERS))

    def z_copy(j, k, d):
        sign = 1 if d == 0 else -1
        piece = z_rows(-sign * k) if k < 3 else z_rows(-sign * k, 64 * d, 64)
        ref = wbuf[j].at[piece]
        sem = z_recv.at[d, j, k] if k < 3 else z_last.at[j]
        return remote(ref, ref, sent_sem.at[S_Z + j], sem, at(dz=sign))

    def z_step(j, k):
        for d in range(2):
            if k > 0:
                sign = 1 if d == 0 else -1
                take(wbuf[j].at[z_rows(-sign * k)], z_recv.at[d, j, k - 1])
            go(z_copy(j, k, d))

    def hx_copy(r):
        dest = lax.rem(x + NX - r, NX)
        src = hid_ref.at[:, pl.ds(pl.multiple_of(dest * X_ROWS, X_ROWS), X_ROWS)]
        return remote(src, rows.at[x, c, y], sent_sem.at[S_HX], hx_recv.at[r], at(dx=-r))

    def hy_first(r):
        ref = rows.at[x_of(r), c, y]
        if r > 0:
            take(ref, hx_recv.at[r])
        for dy in (1, 3, 2):
            go(remote(ref, ref, sent_sem.at[S_HY], hy_recv.at[r], at(dy=dy)))

    def hy_pass(r):
        take(rows.at[x_of(r), c, pl.ds(0, 3)], hy_recv.at[r])
        ref = rows.at[x_of(r), c]
        go(remote(ref, ref, sent_sem.at[S_SIB], sib_recv.at[r], at(dc=1)))

    largest = jnp.zeros((8, 128), jnp.float32)
    amax = jnp.full((8, 128), amax_ref[0], jnp.float32)
    factor = (quant_range / amax)[0:1, 0:1]
    in_scale = (amax / quant_range)[0:1, 0:1]
    top[...] = largest

    def quantized(r):
        where = x_of(r)
        take(rows.at[where, lax.rem(c + 1, NC)], sib_recv.at[r])

        def tile(i, carry):
            core, place = (i // NY, lax.rem(i, NY))
            part = pl.ds(pl.multiple_of((place * NC + core) * 32, 32), 32)
            value = rows[where, core, place].astype(jnp.float32)
            quant[where, part, :] = jnp.clip(
                value * factor, -quant_range, quant_range
            ).astype(jnp.bfloat16)
            most = jnp.max(jnp.abs(value).reshape(4, 8, 1024), axis=0)
            best = most[:, 0:128]
            for lane in range(128, 1024, 128):
                best = jnp.maximum(best, most[:, lane : lane + 128])
            top[...] = jnp.maximum(top[...], best)
            return carry

        lax.fori_loop(0, 8, tile, 0)

    def ext_cols(j):
        return slice(1024, 1280) if j == 0 else slice(256 * (j - 1), 256 * j)

    def halo_copy(j):
        next_z = lax.rem(z + 1, NZ)
        next_x = lax.rem(x + (z + 1) // NZ, NX)
        where = (next_x, next_z, y, c)
        part = pl.ds(ext_cols(j).start, 256)
        return remote(
            tail_out.at[:, part], tail_in.at[:, part], sent_sem.at[S_HALO], halo_recv.at[j], where
        )

    def cols(j):
        return pl.ds(STARTS[j], CHUNKS[j])

    def rs_copy(j, name):
        slot, low, dst, dst_low, sign = {
            TWO_UP: (0, 0, r1, 0, 1),
            TWO_DOWN: (0, 128, r1, 128, -1),
            ONE_UP_B: (1, 128, r2, 128, 1),
            ONE_DOWN_A: (2, 0, r2, 256, -1),
            ONE_UP_A: (1, 0, r2, 0, 1),
            ONE_DOWN_B: (2, 128, r2, 384, -1),
        }[name]
        return remote(
            stage.at[slot, pl.ds(low, 128), cols(j)],
            dst.at[pl.ds(dst_low, 128), cols(j)],
            sent_sem.at[S_RS],
            rs_recv.at[j, name] if name < 2 else rs_last.at[j],
            at(dx=sign),
        )

    def product(j, r):
        return jnp.dot(quant[x_of(r)], wbuf[j][...], preferred_element_type=jnp.float32)

    def rs_multiply(j):
        take(wbuf[j].at[pl.ds(0, 128)], z_last.at[j])
        stage[0, :, cols(j)] = product(j, 2).astype(jnp.bfloat16)
        value = product(j, 1)
        plus[:, cols(j)] = value[0:128]
        stage[1, 128:256, cols(j)] = value[128:256].astype(jnp.bfloat16)
        go(rs_copy(j, TWO_UP))
        go(rs_copy(j, TWO_DOWN))
        value = product(j, 3)
        minus[:, cols(j)] = value[128:256]
        stage[2, 0:128, cols(j)] = value[0:128].astype(jnp.bfloat16)
        go(rs_copy(j, ONE_UP_B))
        own[:, cols(j)] = product(j, 0)
        go(rs_copy(j, ONE_DOWN_A))

    def rs_add(j):
        rs_copy(j, TWO_UP).wait_recv()
        stage[1, 0:128, cols(j)] = (
            plus[:, cols(j)] + r1[0:128, cols(j)].astype(jnp.float32)
        ).astype(jnp.bfloat16)
        rs_copy(j, TWO_DOWN).wait_recv()
        stage[2, 128:256, cols(j)] = (
            minus[:, cols(j)] + r1[128:256, cols(j)].astype(jnp.float32)
        ).astype(jnp.bfloat16)
        go(rs_copy(j, ONE_UP_A))
        go(rs_copy(j, ONE_DOWN_B))

    def rs_final(j):
        take(r2.at[:, cols(j)], rs_last.at[j])
        total = (
            own[:, cols(j)]
            + r2[0:256, cols(j)].astype(jnp.float32)
            + r2[256:512, cols(j)].astype(jnp.float32)
        ) * in_scale
        value = total[:, 0:256].astype(bf16)
        ext[8:264, ext_cols(j)] = value.astype(f32)
        tail_out[:, ext_cols(j)] = value[240:256]
        if j == 0:
            dt_s[...] = total[:, 256:384]
        go(halo_copy(j))

    def tile_copy(rel):
        return remote(
            tiles.at[here], tiles.at[here], sent_sem.at[S_TILE], tile_recv.at[0], at_rel(rel)
        )

    def steps():
        raw = dt_s[...] + par_ref[0:1, :]
        step = jnp.maximum(raw, 0.0) + jnp.log1p(jnp.exp(-jnp.abs(raw)))
        lasts = []
        for b in range(2):
            part = step[128 * b : 128 * b + 128]
            cum = exact_dot(ones_lower, -part * par_ref[1:2, :])
            cum_s[128 * b : 128 * b + 128, :] = cum
            cum_t[b] = jnp.transpose(cum)[0:16]
            step_t[b] = jnp.transpose(part)[0:16]
            last = cum[127:128]
            lasts.append(last)
            share_s[128 * b : 128 * b + 128, :] = part * jnp.exp(last - cum)
        most = jnp.max(top[...], axis=0, keepdims=True)
        row8 = lax.broadcasted_iota(jnp.int32, (8, 128), 0)
        tiles[here] = jnp.where(row8 == 0, lasts[0] + lasts[1], most)
        rates[...] = jnp.where(
            row8 == 0, jnp.exp(lasts[0]), jnp.where(row8 == 1, jnp.exp(lasts[1]), par_ref[2:3, :])
        )

        def send_tile(rel, carry):
            tile_copy(rel).start()
            return carry

        lax.fori_loop(1, COUNT, send_tile, 0)

    def convolve(j):
        halo_copy(j).wait_recv()
        part = ext_cols(j)
        if j == 0:
            before = jnp.concatenate([side_by_side(state_bc_ref, k) for k in range(3)], axis=0)
            taps = jnp.concatenate([side_by_side(conv_bc_ref, k) for k in range(KERNEL)], axis=0)
        else:
            before, taps = (state_x_ref[:, part].astype(f32), conv_x_ref[:, part])
        ext[5:8, part] = jnp.where(
            here == 0, before, tail_in[:, part].astype(f32)[13:16]
        )
        for b in range(2):
            total = taps[0:1] * ext[5 + 128 * b : 133 + 128 * b, part]
            for k in range(1, KERNEL):
                total = total + taps[k : k + 1] * ext[5 + k + 128 * b : 133 + k + 128 * b, part]
            value = (total / (1.0 + jnp.exp(-total))).astype(bf16)
            if j == 0:
                bc_act[128 * b : 128 * b + 128, :] = value
                meet[b] = lax.dot_general(
                    value[:, 128:256],
                    value[:, 0:128],
                    (((1,), (1,)), ((), ())),
                    preferred_element_type=f32,
                )
            else:
                x_act[128 * b : 128 * b + 128, part] = value

    def slice_of(xs, zs):
        return (
            pl.ds(pl.multiple_of(zs * 16, 16), 16),
            pl.ds(pl.multiple_of(xs * 256, 256), 256),
        )

    def state_copy(g, dz):
        tz = lax.rem(z + dz, NZ)
        return remote(
            device_state.at[pl.ds(pl.multiple_of(tz * 16, 16), 16), pl.ds(256 * g, 256)],
            arrived.at[here],
            sent_sem.at[S_ST],
            st_recv.at[0],
            (g, tz, y, c),
        )

    def add_states(g):
        part = slice(256 * g, 256 * g + 256)
        spread = expand[:, part]
        rate = exact_dot(rates[...], spread)
        grown[g] = rate
        for b in range(2):
            rows_b = slice(128 * b, 128 * b + 128)
            weighted = (
                x_act[rows_b, part].astype(f32) * exact_dot(share_s[rows_b, :], spread)
            ).astype(bf16)
            added = lax.dot_general(
                bc_act[rows_b, 0:128], weighted, (((0,), (0,)), ((), ())), preferred_element_type=f32
            )
            if b == 0:
                added0[:, part] = added
            else:
                device_state[:, part] = (rate[1:2] * added0[:, part] + added).astype(bf16)

        @pl.when(x == g)
        def _():
            arrived[here] = device_state[pl.ds(pl.multiple_of(z * 16, 16), 16), part]

        @pl.when(x != g)
        def _():
            state_copy(g, 0).start()

        for dz in range(1, NZ):
            state_copy(g, dz).start()

    half_lane = lax.broadcasted_iota(jnp.int32, (128, 128), 1) < 64

    def inside(g):
        def block(b, carry):
            rows_b = pl.ds(pl.multiple_of(b * 128, 128), 128)
            for pair in (2 * g, 2 * g + 1):
                part = slice(128 * pair, 128 * pair + 128)
                both_weights = []
                for h in (2 * pair, 2 * pair + 1):
                    gap = cum_s[rows_b, h : h + 1] - cum_t[b, h : h + 1, :]
                    decay = jnp.exp(jnp.where(lower, gap, -1e30))
                    both_weights.append((meet[b] * decay * step_t[b, h : h + 1, :]).astype(bf16))
                values = x_act[rows_b, part].astype(f32)
                both = jnp.concatenate(
                    [jnp.where(half_lane, values, 0.0), jnp.where(half_lane, 0.0, values)], axis=0
                ).astype(bf16)
                result = jnp.dot(
                    jnp.concatenate(both_weights, axis=1), both, preferred_element_type=f32
                )
                low = 128 * (pair - 2 * g)
                acc[rows_b, part] = result + grown[g, 2:3, low : low + 128] * values
            return carry

        lax.fori_loop(0, 2, block, 0)

    def back_copy(rel):
        tx, tz, _, _ = at_rel(rel)
        return remote(
            carried.at[tx * NZ + tz],
            incoming.at[slice_of(x, z)],
            sent_sem.at[S_BACK],
            back_recv.at[x],
            at_rel(rel),
        )

    def chain(g):
        @pl.when(x == g)
        def _():
            take(tiles.at[pl.ds(0, COUNT - 1)], tile_recv.at[0])
            everything = tiles[...]
            best = jnp.max(everything[:, 1, :], axis=0, keepdims=True)
            max_out[...] = jnp.max(best, axis=1, keepdims=True)
            decays = exact_dot(jnp.exp(everything[:, 0, :]), expand[:, 256 * g : 256 * g + 256])

            take(arrived.at[pl.ds(0, COUNT - 1)], st_recv.at[0])
            state = init_t[pl.ds(pl.multiple_of(z * 16, 16), 16), :]
            for n in range(COUNT):
                carried[n] = state.astype(bf16)
                if n < COUNT - 1:
                    state = decays[n : n + 1] * state + arrived[n].astype(f32)

            def send_back(rel, carry):
                back_copy(rel).start()
                return carry

            lax.fori_loop(1, COUNT, send_back, 0)
            incoming[slice_of(x, z)] = carried[here]

    def u_copy(g, b, kind, origin, where):
        ref = tokens.at[x_of(origin), pl.ds(128 * b, 128), pl.ds(256 * g, 256)]
        sem = u_recv.at[g, b] if kind == b else u_last.at[kind]
        return remote(ref, ref, sent_sem.at[S_U], sem, where)

    def finish(g):
        part = slice(256 * g, 256 * g + 256)

        @pl.when(x != g)
        def _():
            take(incoming.at[:, part], back_recv.at[g])

        @pl.when(x == g)
        def _():
            take(incoming.at[pl.ds(0, 112), part], back_recv.at[g])

        for b in range(2):
            rows_b = slice(128 * b, 128 * b + 128)
            entering = incoming[:, part]
            if b == 1:
                entering = (grown[g, 0:1, :] * entering.astype(f32) + added0[:, part]).astype(bf16)
            seen = jnp.dot(bc_act[rows_b, 128:256], entering, preferred_element_type=f32)
            total = acc[rows_b, part] + exact_dot(jnp.exp(cum_s[rows_b, :]), expand[:, part]) * seen
            tokens[x, rows_b, part] = (total * gain_ref[:, part]).astype(bf16)
            squared = total * total
            squared = squared[:, 0:128] + squared[:, 128:256]
            sq[rows_b, :] = squared if g == 0 else sq[rows_b, :] + squared
        go(u_copy(g, 0, 0, 0, at(dx=1)))
        go(u_copy(g, 1, 1, 0, at(dx=-1)))
        go(u_copy(g, 1, 0, 0, at(dx=1)))
        go(u_copy(g, 0, 1, 0, at(dx=-1)))

    def u_relay(g):
        take(tokens.at[0, pl.ds(0, 128), pl.ds(0, 256)], u_recv.at[g, 0])
        go(u_copy(g, 0, 2, -1, at(dx=1)))
        take(tokens.at[0, pl.ds(0, 128), pl.ds(0, 256)], u_recv.at[g, 1])
        go(u_copy(g, 1, 2, 1, at(dx=-1)))

    def o_copy(j, k, d):
        sign = 1 if d == 0 else -1
        rows_j = pl.ds(256 * j, 256)
        arrives = 4 if k == 3 else -sign * (k + 1)
        return remote(
            weights.at[rows_j, z_cols(-sign * k)],
            weights.at[rows_j, z_cols(arrives)],
            sent_sem.at[S_O],
            o_recv.at[d, j, k] if k < 3 else o_last.at[0],
            at(dz=sign),
        )

    def o_wave(k, pieces=(0, 1, 2, 3)):
        for j in pieces:
            for d in range(2):
                if k > 0:
                    o_copy(j, k - 1, d).wait_recv()
                if k < 3 or j // 2 == d:
                    go(o_copy(j, k, d))

    def sq_copy(n):
        dy, dc = OTHERS[n]
        there = pl.ds(pl.multiple_of(t_index(dy, dc) * 32, 32), 32)
        return remote(sq.at[there], squares.at[n], sent_sem.at[S_SQ], sq_recv.at[0], at(dy=dy, dc=dc))

    def multiply(r):
        slot = x_of(r)

        def one(n, carry):
            part = pl.ds(pl.multiple_of(n * 256, 256), 256)
            value = jnp.dot(
                tokens[slot], weights[:, part], preferred_element_type=jnp.float32
            ).astype(jnp.bfloat16)
            value = value.reshape(NY, NC, 32, 256)
            for core in range(NC):
                partial[r, core, :, :, part] = value[:, core]
            return carry

        lax.fori_loop(0, 4, one, 0)
        go(c_copy(r))

    def c_copy(r):
        other = lax.rem(c + 1, NC)
        return remote(
            partial.at[r, other], from_core.at[r], sent_sem.at[S_C], c_recv.at[r], at(dc=1)
        )

    def y_copy(r, name):
        slot, low, dst, sign = {
            TWO_UP: (2, 0, ry1.at[r], 1),
            TWO_DOWN: (2, 16, ry1.at[r], -1),
            ONE_UP_B: (1, 16, ry2.at[r, 0], 1),
            ONE_DOWN_A: (3, 0, ry2.at[r, 1], -1),
            ONE_UP_A: (1, 0, ry2.at[r, 0], 1),
            ONE_DOWN_B: (3, 16, ry2.at[r, 1], -1),
        }[name]
        return remote(
            ystage.at[r, slot, pl.ds(low, 16)],
            dst.at[pl.ds(low, 16)],
            sent_sem.at[S_Y],
            y_recv.at[r, name] if name < 2 else y_last.at[r],
            at(dy=sign),
        )

    def both_cores(r, dy):
        where = y_of(dy)
        return partial[r, c, where].astype(jnp.float32) + from_core[r, where].astype(jnp.float32)

    def y_first(r):
        take(from_core.at[r], c_recv.at[r])
        ystage[r, 2] = both_cores(r, 2).astype(jnp.bfloat16)
        value = both_cores(r, 1)
        yup[r] = value[0:16]
        ystage[r, 1, 16:32] = value[16:32].astype(jnp.bfloat16)
        go(y_copy(r, TWO_UP))
        go(y_copy(r, TWO_DOWN))
        value = both_cores(r, 3)
        ydown[r] = value[16:32]
        ystage[r, 3, 0:16] = value[0:16].astype(jnp.bfloat16)
        go(y_copy(r, ONE_UP_B))
        yown[r] = both_cores(r, 0)
        go(y_copy(r, ONE_DOWN_A))

    def y_add(r):
        y_copy(r, TWO_UP).wait_recv()
        ystage[r, 1, 0:16] = (yup[r] + ry1[r, 0:16].astype(jnp.float32)).astype(jnp.bfloat16)
        y_copy(r, TWO_DOWN).wait_recv()
        ystage[r, 3, 16:32] = (ydown[r] + ry1[r, 16:32].astype(jnp.float32)).astype(jnp.bfloat16)
        go(y_copy(r, ONE_UP_A))
        go(y_copy(r, ONE_DOWN_B))

    def y_final(r):
        take(ry2.at[r], y_last.at[r])
        value = (
            yown[r] + ry2[r, 0].astype(jnp.float32) + ry2[r, 1].astype(jnp.float32)
        ).astype(jnp.bfloat16)
        if r == 0:
            landed[x] = value
        else:
            fstage[r] = value
            go(remote(fstage.at[r], landed.at[x], sent_sem.at[S_F], f_recv.at[0], at(dx=r)))

    for r in (1, 3, 2):
        go(hx_copy(r))
    hy_first(0)
    z_step(0, 0)
    z_step(1, 0)
    hy_first(1)
    hy_first(3)
    z_step(0, 1)
    hy_first(2)
    z_step(1, 1)
    hy_pass(0)
    z_step(0, 2)
    hy_pass(1)
    z_step(1, 2)
    z_step(2, 0)
    hy_pass(3)
    z_step(0, 3)
    z_step(3, 0)
    hy_pass(2)
    z_step(1, 3)
    z_step(2, 1)
    z_step(4, 0)
    quantized(0)
    quantized(1)
    quantized(3)
    quantized(2)
    rs_multiply(0)
    z_step(3, 1)
    rs_multiply(1)
    z_step(2, 2)
    z_step(3, 2)
    rs_add(0)
    z_step(4, 1)
    z_step(2, 3)
    z_step(3, 3)
    rs_add(1)
    z_step(4, 2)
    rs_multiply(2)
    rs_multiply(3)
    z_step(4, 3)
    o_wave(0)
    rs_final(0)
    rs_add(2)
    rs_multiply(4)
    steps()
    rs_final(1)
    rs_add(3)
    o_wave(1, (0, 1))
    convolve(0)
    rs_final(2)
    rs_add(4)
    convolve(1)
    add_states(0)
    rs_final(3)
    convolve(2)
    add_states(1)
    rs_final(4)
    convolve(3)
    add_states(2)
    inside(0)
    convolve(4)
    add_states(3)
    o_wave(1, (2, 3))
    chain(0)
    inside(1)
    chain(1)
    inside(2)
    inside(3)
    chain(2)
    chain(3)
    o_wave(2)
    finish(0)
    finish(1)
    u_relay(0)
    o_wave(3)
    finish(2)
    u_relay(1)
    finish(3)
    u_relay(2)
    for n in range(7):
        go(sq_copy(n))
    take(weights.at[:, pl.ds(0, 128)], o_last.at[0])
    multiply(0)
    y_first(0)
    u_relay(3)
    take(tokens.at[0, pl.ds(0, 128)], u_last.at[0])
    multiply(3)
    y_add(0)
    take(tokens.at[0, pl.ds(0, 128)], u_last.at[1])
    multiply(1)
    y_first(3)
    take(tokens.at[0], u_last.at[2])
    multiply(2)
    y_first(1)
    y_add(3)
    y_first(2)
    y_add(1)
    y_final(0)
    y_add(2)
    y_final(3)
    y_final(1)

    take(squares, sq_recv.at[0])
    index = t_index(0, 0)
    total = sq[pl.ds(pl.multiple_of(index * 32, 32), 32), :]
    for n in range(7):
        total = total + squares[n]
    mean_sq = jnp.sum(total, axis=1, keepdims=True) / (HEADS * HEAD_DIM)
    scale = lax.rsqrt(mean_sq + epsilon)

    y_final(2)
    drain(rows.at[0, 0, pl.ds(0, 3)], S_HX)
    drain(rows.at[pl.ds(0, 3), 0], S_HY)
    drain(rows.at[:, 0], S_SIB)
    for j in range(5):
        drain(wbuf[j].at[pl.ds(0, 896)], S_Z + j)
    drain(stage, S_RS)
    drain(tail_out, S_HALO)
    drain(tiles.at[pl.ds(0, COUNT - 1)], S_TILE)
    drain(arrived.at[pl.ds(0, COUNT - 1)], S_ST)
    drain(arrived.at[pl.ds(0, COUNT - 1)], S_BACK)
    drain(tokens.at[pl.ds(0, 3)], S_U)
    drain(weights.at[pl.ds(0, 896)], S_O)
    drain(squares, S_SQ)
    drain(from_core, S_C)
    drain(ystage.at[:, pl.ds(0, 3)], S_Y)
    drain(fstage.at[pl.ds(0, 3)], S_F)
    take(landed.at[pl.ds(0, 3)], f_recv.at[0])
    for block in range(NX):
        for n, slot in enumerate(SLOTS):
            place = lax.rem(z + slot + NZ, NZ)
            part = pl.ds(pl.multiple_of(1024 * block + place * 128, 128), 128)
            value = landed[block, :, 128 * n : 128 * n + 128].astype(f32)
            out_ref[:, part] = (value * scale).astype(bf16)


def run_layer(*arrays):
    vmem = pl.BlockSpec(memory_space=pltpu.VMEM)
    any_place = pl.BlockSpec(memory_space=pl.ANY)
    return pl.pallas_call(
        layer,
        name="layer",
        out_shape=(
            jax.ShapeDtypeStruct((32, 4096), jnp.bfloat16),
            jax.ShapeDtypeStruct((1, 1), jnp.float32),
        ),
        in_specs=[pl.BlockSpec(memory_space=pltpu.SMEM)]
        + [any_place] * 2
        + [vmem] * 11
        + [any_place],
        out_specs=(vmem, vmem),
        scratch_shapes=scratch(),
        compiler_params=pltpu.CompilerParams(
            collective_id=0, has_side_effects=True, vmem_limit_bytes=60 * 2**20
        ),
    )(*arrays)


def local(
    hidden_in,
    prev_amax,
    w_x,
    w_bc,
    w_dt,
    conv_x,
    conv_bc,
    conv_state_x,
    conv_state_bc,
    dt_bias,
    decay_rate,
    skip,
    init_state,
    norm_gain,
    w_out,
):
    heads = w_dt.shape[1]
    layer_out, largest = run_layer(
        jnp.reshape(prev_amax, (1,)),
        hidden_in,
        w_x,
        w_bc,
        jnp.transpose(w_dt),
        conv_x,
        conv_bc,
        conv_state_x,
        conv_state_bc,
        jnp.reshape(dt_bias, (1, heads)),
        jnp.reshape(decay_rate, (1, heads)),
        jnp.reshape(skip, (1, heads)),
        jnp.reshape(init_state, (heads * HEAD_DIM, STATE)),
        jnp.reshape(norm_gain, (1, -1)),
        w_out,
    )
    return (layer_out, largest[0, 0])


def solution(mesh):
    finer = Mesh(mesh.devices.reshape(NX, NZ, NY, NC), SEQ_TENSOR)
    return jax.shard_map(
        local,
        mesh=finer,
        in_specs=(
            P(SEQ_TENSOR, None),
            P(),
            P(SEQ, TENSOR),
            P(SEQ, TENSOR, None, None),
            P(SEQ, TENSOR),
            P(None, TENSOR),
            P(None, TENSOR, None, None),
            P(None, TENSOR),
            P(None, TENSOR, None, None),
            P(TENSOR),
            P(TENSOR),
            P(TENSOR),
            P(TENSOR, None, None),
            P(TENSOR),
            P(TENSOR, SEQ),
        ),
        out_specs=(P(SEQ_TENSOR, None), P()),
        check_vma=False,
    )
```

```python
import jax
import jax.numpy as jnp
from jax import lax
from jax.experimental import pallas as pl
from jax.experimental.pallas import tpu as pltpu
from jax.sharding import Mesh
from jax.sharding import PartitionSpec as P

HEADS = 128
HEAD_DIM = 64
STATE = 128
GROUPS = 8
KERNEL = 4
SPAN = 128
SEQ = ("x", "z")
TENSOR = ("y", "c")
SEQ_TENSOR = SEQ + TENSOR


epsilon = 1e-05
quant_range = 448.0


MESH_ID = pl.DeviceIdType.MESH
NX, NZ, NY, NC = (4, 8, 4, 2)
COUNT = NX * NZ
CHUNKS = (384, 256, 256, 256, 256)
STARTS = (0, 384, 640, 896, 1152)
WIDE = 1408
X_ROWS = 1024
TWO_UP, TWO_DOWN, ONE_UP_B, ONE_DOWN_A, ONE_UP_A, ONE_DOWN_B = range(6)
SLOTS = (0, 4, -1, 1, -2, 2, -3, 3)
(S_HX, S_HY, S_SIB, S_RS, S_HALO, S_TILE, S_ST, S_BACK, S_U, S_O, S_SQ, S_C, S_Y, S_F) = range(14)
S_Z = 14
OTHERS = tuple((dy, dc) for dy in range(NY) for dc in range(NC) if (dy, dc) != (0, 0))


def scratch():
    bf16, f32 = (jnp.bfloat16, jnp.float32)
    v, dma = (pltpu.VMEM, pltpu.SemaphoreType.DMA)
    return [
        v((8, 128), f32),
        v((4, NC, NY, 32, X_ROWS), bf16),
        v((4, 256, X_ROWS), bf16),
        v((X_ROWS, CHUNKS[0]), bf16),
        v((X_ROWS, CHUNKS[1]), bf16),
        v((X_ROWS, CHUNKS[2]), bf16),
        v((X_ROWS, CHUNKS[3]), bf16),
        v((X_ROWS, CHUNKS[4]), bf16),
        v((3, 256, WIDE), bf16),
        v((256, WIDE), bf16),
        v((512, WIDE), bf16),
        v((256, WIDE), f32),
        v((128, WIDE), f32),
        v((128, WIDE), f32),
        v((8, 128), f32),
        v((16, 1280), bf16),
        v((16, 1280), bf16),
        v((264, 1280), f32),
        v((256, 1024), bf16),
        v((256, 256), bf16),
        v((256, 128), f32),
        v((256, 128), f32),
        v((256, 128), f32),
        v((2, 16, 128), f32),
        v((2, 16, 128), f32),
        v((2, 128, 128), f32),
        v((8, 128), f32),
        v((4, 8, 256), f32),
        v((128, 1024), f32),
        v((128, 1024), f32),
        v((128, 1024), bf16),
        v((COUNT, 8, 128), f32),
        v((COUNT, 16, 256), bf16),
        v((COUNT, 16, 256), bf16),
        v((128, 1024), bf16),
        v((128, 256), f32),
        v((256, 1024), f32),
        v((256, 128), f32),
        v((4, 256, 1024), bf16),
        v((1024, 1024), bf16),
        v((4, NC, NY, 32, 1024), bf16),
        v((4, NY, 32, 1024), bf16),
        v((4, NY, 32, 1024), bf16),
        v((4, 32, 1024), bf16),
        v((4, 2, 32, 1024), bf16),
        v((4, 32, 1024), f32),
        v((4, 16, 1024), f32),
        v((4, 16, 1024), f32),
        v((4, 32, 1024), bf16),
        v((4, 32, 1024), bf16),
        v((7, 32, 128), f32),
        dma((8,)),
        dma((19,)),
        dma((4,)),
        dma((4,)),
        dma((4,)),
        dma((2, 5, 3)),
        dma((5,)),
        dma((5, 2)),
        dma((5,)),
        dma((5,)),
        dma((1,)),
        dma((1,)),
        dma((4,)),
        dma((4, 2)),
        dma((3,)),
        dma((2, 4, 3)),
        dma((1,)),
        dma((1,)),
        dma((4,)),
        dma((4, 2)),
        dma((4,)),
        dma((1,)),
    ]


def remote(src, dst, send_sem, recv_sem, where):
    return pltpu.make_async_remote_copy(
        src_ref=src,
        dst_ref=dst,
        send_sem=send_sem,
        recv_sem=recv_sem,
        device_id=where,
        device_id_type=MESH_ID,
    )


def layer(
    amax_ref,
    hid_ref,
    wx_ref,
    wbc_ref,
    wdt_ref,
    conv_x_ref,
    conv_bc_ref,
    state_x_ref,
    state_bc_ref,
    bias_ref,
    decay_ref,
    skip_ref,
    init_ref,
    gain_ref,
    w_ref,
    out_ref,
    max_out,
    par_ref,
    rows,
    quant,
    w0,
    w1,
    w2,
    w3,
    w4,
    stage,
    r1,
    r2,
    own,
    plus,
    minus,
    top,
    tail_out,
    tail_in,
    ext,
    x_act,
    bc_act,
    dt_s,
    cum_s,
    share_s,
    cum_t,
    step_t,
    meet,
    rates,
    grown,
    expand,
    added0,
    device_state,
    tiles,
    arrived,
    carried,
    incoming,
    init_t,
    acc,
    sq,
    tokens,
    weights,
    partial,
    from_core,
    ystage,
    ry1,
    ry2,
    yown,
    yup,
    ydown,
    fstage,
    landed,
    squares,
    local_sem,
    sent_sem,
    hx_recv,
    hy_recv,
    sib_recv,
    z_recv,
    z_last,
    rs_recv,
    rs_last,
    halo_recv,
    tile_recv,
    st_recv,
    back_recv,
    u_recv,
    u_last,
    o_recv,
    o_last,
    sq_recv,
    c_recv,
    y_recv,
    y_last,
    f_recv,
):
    x, z, y, c = (lax.axis_index(name) for name in ("x", "z", "y", "c"))
    here = x * NZ + z
    f32, bf16 = (jnp.float32, jnp.bfloat16)
    wbuf = (w0, w1, w2, w3, w4)

    def at(dx=0, dz=0, dy=0, dc=0):
        return (
            lax.rem(x + dx + NX, NX),
            lax.rem(z + dz + NZ, NZ),
            lax.rem(y + dy + NY, NY),
            lax.rem(c + dc, NC),
        )

    def at_rel(rel):
        return (lax.rem(x + rel // NZ, NX), lax.rem(z + rel % NZ, NZ), y, c)

    def x_of(r):
        return lax.rem(x + r + NX, NX)

    def y_of(dy):
        return lax.rem(y + dy + NY, NY)

    def t_index(dy, dc):
        return y_of(dy) * NC + lax.rem(c + dc, NC)

    def exact_dot(a, b):
        return jnp.dot(a, b, precision=lax.Precision.HIGHEST, preferred_element_type=f32)

    def go(copy):
        copy.start()

    def take(ref, sem):
        remote(ref, ref, sent_sem.at[0], sem, at(dz=1)).wait_recv()

    def drain(ref, index):
        remote(ref, ref, sent_sem.at[index], hx_recv.at[0], at(dz=1)).wait_send()

    def z_rows(dz, low=0, count=128):
        block = lax.rem(z + dz + NZ, NZ)
        return pl.ds(pl.multiple_of(block * 128 + low, count), count)

    def z_cols(slot):
        return pl.ds(128 * SLOTS.index(slot), 128)

    barrier = pltpu.get_barrier_semaphore()

    beside = (at(dx=1), at(dx=-1), at(dx=2), at(dz=1), at(dz=-1))
    for peer in beside:
        pl.semaphore_signal(barrier, inc=1, device_id=peer, device_id_type=MESH_ID)
    for dy, dc in OTHERS:
        pl.semaphore_signal(barrier, inc=1, device_id=at(dy=dy, dc=dc), device_id_type=MESH_ID)

    local = [
        pltpu.make_async_copy(
            wx_ref.at[:, pl.ds(256 * (j - 1), 256)], wbuf[j].at[z_rows(0)], local_sem.at[j]
        )
        for j in range(1, 5)
    ]
    local.append(
        pltpu.make_async_copy(
            hid_ref.at[:, pl.ds(pl.multiple_of(x * X_ROWS, X_ROWS), X_ROWS)],
            rows.at[x, c, y],
            local_sem.at[5],
        )
    )
    local.append(pltpu.make_async_copy(w_ref, weights.at[:, z_cols(0)], local_sem.at[6]))
    for copy in local:
        copy.start()

    def side_by_side(ref, k):
        pair = ref[k, 0].astype(f32)
        return jnp.concatenate([pair[0:1], pair[1:2]], axis=1)

    lane = lax.broadcasted_iota(jnp.int32, (128, 1024), 1)
    head = lax.broadcasted_iota(jnp.int32, (128, 1024), 0)
    row_at = lax.broadcasted_iota(jnp.int32, (128, 128), 0)
    col_at = lax.broadcasted_iota(jnp.int32, (128, 128), 1)
    lower = row_at >= col_at
    ones_lower = jnp.where(lower, 1.0, 0.0).astype(f32)
    pl.semaphore_wait(barrier, len(beside) + len(OTHERS))

    def z_copy(j, k, d):
        sign = 1 if d == 0 else -1
        piece = z_rows(-sign * k) if k < 3 else z_rows(-sign * k, 64 * d, 64)
        ref = wbuf[j].at[piece]
        sem = z_recv.at[d, j, k] if k < 3 else z_last.at[j]
        return remote(ref, ref, sent_sem.at[S_Z + j], sem, at(dz=sign))

    def z_step(j, k):
        for d in range(2):
            if k > 0:
                sign = 1 if d == 0 else -1
                take(wbuf[j].at[z_rows(-sign * k)], z_recv.at[d, j, k - 1])
            go(z_copy(j, k, d))

    def hx_copy(r):
        dest = lax.rem(x + NX - r, NX)
        src = hid_ref.at[:, pl.ds(pl.multiple_of(dest * X_ROWS, X_ROWS), X_ROWS)]
        return remote(src, rows.at[x, c, y], sent_sem.at[S_HX], hx_recv.at[r], at(dx=-r))

    def hy_first(r):
        ref = rows.at[x_of(r), c, y]
        if r > 0:
            take(ref, hx_recv.at[r])
        for dy in (1, 3, 2):
            go(remote(ref, ref, sent_sem.at[S_HY], hy_recv.at[r], at(dy=dy)))

    def hy_pass(r):
        take(rows.at[x_of(r), c, pl.ds(0, 3)], hy_recv.at[r])
        ref = rows.at[x_of(r), c]
        go(remote(ref, ref, sent_sem.at[S_SIB], sib_recv.at[r], at(dc=1)))

    largest = jnp.zeros((8, 128), jnp.float32)
    amax = jnp.full((8, 128), amax_ref[0], jnp.float32)
    factor = (quant_range / amax)[0:1, 0:1]
    in_scale = (amax / quant_range)[0:1, 0:1]
    top[...] = largest

    def quantized(r):
        where = x_of(r)
        take(rows.at[where, lax.rem(c + 1, NC)], sib_recv.at[r])

        def tile(i, carry):
            core, place = (i // NY, lax.rem(i, NY))
            part = pl.ds(pl.multiple_of((place * NC + core) * 32, 32), 32)
            value = rows[where, core, place].astype(jnp.float32)
            quant[where, part, :] = jnp.clip(
                value * factor, -quant_range, quant_range
            ).astype(jnp.bfloat16)
            most = jnp.max(jnp.abs(value).reshape(4, 8, 1024), axis=0)
            best = most[:, 0:128]
            for lane in range(128, 1024, 128):
                best = jnp.maximum(best, most[:, lane : lane + 128])
            top[...] = jnp.maximum(top[...], best)
            return carry

        lax.fori_loop(0, 8, tile, 0)

    def ext_cols(j):
        return slice(1024, 1280) if j == 0 else slice(256 * (j - 1), 256 * j)

    def halo_copy(j):
        next_z = lax.rem(z + 1, NZ)
        next_x = lax.rem(x + (z + 1) // NZ, NX)
        where = (next_x, next_z, y, c)
        part = pl.ds(ext_cols(j).start, 256)
        return remote(
            tail_out.at[:, part], tail_in.at[:, part], sent_sem.at[S_HALO], halo_recv.at[j], where
        )

    def cols(j):
        return pl.ds(STARTS[j], CHUNKS[j])

    def rs_copy(j, name):
        slot, low, dst, dst_low, sign = {
            TWO_UP: (0, 0, r1, 0, 1),
            TWO_DOWN: (0, 128, r1, 128, -1),
            ONE_UP_B: (1, 128, r2, 128, 1),
            ONE_DOWN_A: (2, 0, r2, 256, -1),
            ONE_UP_A: (1, 0, r2, 0, 1),
            ONE_DOWN_B: (2, 128, r2, 384, -1),
        }[name]
        return remote(
            stage.at[slot, pl.ds(low, 128), cols(j)],
            dst.at[pl.ds(dst_low, 128), cols(j)],
            sent_sem.at[S_RS],
            rs_recv.at[j, name] if name < 2 else rs_last.at[j],
            at(dx=sign),
        )

    def product(j, r):
        return jnp.dot(quant[x_of(r)], wbuf[j][...], preferred_element_type=jnp.float32)

    def rs_multiply(j):
        take(wbuf[j].at[pl.ds(0, 128)], z_last.at[j])
        stage[0, :, cols(j)] = product(j, 2).astype(jnp.bfloat16)
        value = product(j, 1)
        plus[:, cols(j)] = value[0:128]
        stage[1, 128:256, cols(j)] = value[128:256].astype(jnp.bfloat16)
        go(rs_copy(j, TWO_UP))
        go(rs_copy(j, TWO_DOWN))
        value = product(j, 3)
        minus[:, cols(j)] = value[128:256]
        stage[2, 0:128, cols(j)] = value[0:128].astype(jnp.bfloat16)
        go(rs_copy(j, ONE_UP_B))
        own[:, cols(j)] = product(j, 0)
        go(rs_copy(j, ONE_DOWN_A))

    def rs_add(j):
        rs_copy(j, TWO_UP).wait_recv()
        stage[1, 0:128, cols(j)] = (
            plus[:, cols(j)] + r1[0:128, cols(j)].astype(jnp.float32)
        ).astype(jnp.bfloat16)
        rs_copy(j, TWO_DOWN).wait_recv()
        stage[2, 128:256, cols(j)] = (
            minus[:, cols(j)] + r1[128:256, cols(j)].astype(jnp.float32)
        ).astype(jnp.bfloat16)
        go(rs_copy(j, ONE_UP_A))
        go(rs_copy(j, ONE_DOWN_B))

    def rs_final(j):
        take(r2.at[:, cols(j)], rs_last.at[j])
        total = (
            own[:, cols(j)]
            + r2[0:256, cols(j)].astype(jnp.float32)
            + r2[256:512, cols(j)].astype(jnp.float32)
        ) * in_scale
        value = total[:, 0:256].astype(bf16)
        ext[8:264, ext_cols(j)] = value.astype(f32)
        tail_out[:, ext_cols(j)] = value[240:256]
        if j == 0:
            dt_s[...] = total[:, 256:384]
        go(halo_copy(j))

    def tile_copy(rel):
        return remote(
            tiles.at[here], tiles.at[here], sent_sem.at[S_TILE], tile_recv.at[0], at_rel(rel)
        )

    def steps():
        raw = dt_s[...] + par_ref[0:1, :]
        step = jnp.maximum(raw, 0.0) + jnp.log1p(jnp.exp(-jnp.abs(raw)))
        lasts = []
        for b in range(2):
            part = step[128 * b : 128 * b + 128]
            cum = exact_dot(ones_lower, -part * par_ref[1:2, :])
            cum_s[128 * b : 128 * b + 128, :] = cum
            cum_t[b] = jnp.transpose(cum)[0:16]
            step_t[b] = jnp.transpose(part)[0:16]
            last = cum[127:128]
            lasts.append(last)
            share_s[128 * b : 128 * b + 128, :] = part * jnp.exp(last - cum)
        most = jnp.max(top[...], axis=0, keepdims=True)
        row8 = lax.broadcasted_iota(jnp.int32, (8, 128), 0)
        tiles[here] = jnp.where(row8 == 0, lasts[0] + lasts[1], most)
        rates[...] = jnp.where(
            row8 == 0, jnp.exp(lasts[0]), jnp.where(row8 == 1, jnp.exp(lasts[1]), par_ref[2:3, :])
        )

        def send_tile(rel, carry):
            tile_copy(rel).start()
            return carry

        lax.fori_loop(1, COUNT, send_tile, 0)

    def convolve(j):
        halo_copy(j).wait_recv()
        part = ext_cols(j)
        if j == 0:
            before = jnp.concatenate([side_by_side(state_bc_ref, k) for k in range(3)], axis=0)
            taps = jnp.concatenate([side_by_side(conv_bc_ref, k) for k in range(KERNEL)], axis=0)
        else:
            before, taps = (state_x_ref[:, part].astype(f32), conv_x_ref[:, part])
        ext[5:8, part] = jnp.where(
            here == 0, before, tail_in[:, part].astype(f32)[13:16]
        )
        for b in range(2):
            total = taps[0:1] * ext[5 + 128 * b : 133 + 128 * b, part]
            for k in range(1, KERNEL):
                total = total + taps[k : k + 1] * ext[5 + k + 128 * b : 133 + k + 128 * b, part]
            value = (total / (1.0 + jnp.exp(-total))).astype(bf16)
            if j == 0:
                bc_act[128 * b : 128 * b + 128, :] = value
                meet[b] = lax.dot_general(
                    value[:, 128:256],
                    value[:, 0:128],
                    (((1,), (1,)), ((), ())),
                    preferred_element_type=f32,
                )
            else:
                x_act[128 * b : 128 * b + 128, part] = value

    def slice_of(xs, zs):
        return (
            pl.ds(pl.multiple_of(zs * 16, 16), 16),
            pl.ds(pl.multiple_of(xs * 256, 256), 256),
        )

    def state_copy(g, dz):
        tz = lax.rem(z + dz, NZ)
        return remote(
            device_state.at[pl.ds(pl.multiple_of(tz * 16, 16), 16), pl.ds(256 * g, 256)],
            arrived.at[here],
            sent_sem.at[S_ST],
            st_recv.at[0],
            (g, tz, y, c),
        )

    def add_states(g):
        part = slice(256 * g, 256 * g + 256)
        spread = expand[:, part]
        rate = exact_dot(rates[...], spread)
        grown[g] = rate
        for b in range(2):
            rows_b = slice(128 * b, 128 * b + 128)
            weighted = (
                x_act[rows_b, part].astype(f32) * exact_dot(share_s[rows_b, :], spread)
            ).astype(bf16)
            added = lax.dot_general(
                bc_act[rows_b, 0:128], weighted, (((0,), (0,)), ((), ())), preferred_element_type=f32
            )
            if b == 0:
                added0[:, part] = added
            else:
                device_state[:, part] = (rate[1:2] * added0[:, part] + added).astype(bf16)

        @pl.when(x == g)
        def _():
            arrived[here] = device_state[pl.ds(pl.multiple_of(z * 16, 16), 16), part]

        @pl.when(x != g)
        def _():
            state_copy(g, 0).start()

        for dz in range(1, NZ):
            state_copy(g, dz).start()

    half_lane = lax.broadcasted_iota(jnp.int32, (128, 128), 1) < 64

    def inside(g):
        def block(b, carry):
            rows_b = pl.ds(pl.multiple_of(b * 128, 128), 128)
            for pair in (2 * g, 2 * g + 1):
                part = slice(128 * pair, 128 * pair + 128)
                both_weights = []
                for h in (2 * pair, 2 * pair + 1):
                    gap = cum_s[rows_b, h : h + 1] - cum_t[b, h : h + 1, :]
                    decay = jnp.exp(jnp.where(lower, gap, -1e30))
                    both_weights.append((meet[b] * decay * step_t[b, h : h + 1, :]).astype(bf16))
                values = x_act[rows_b, part].astype(f32)
                both = jnp.concatenate(
                    [jnp.where(half_lane, values, 0.0), jnp.where(half_lane, 0.0, values)], axis=0
                ).astype(bf16)
                result = jnp.dot(
                    jnp.concatenate(both_weights, axis=1), both, preferred_element_type=f32
                )
                low = 128 * (pair - 2 * g)
                acc[rows_b, part] = result + grown[g, 2:3, low : low + 128] * values
            return carry

        lax.fori_loop(0, 2, block, 0)

    def back_copy(rel):
        tx, tz, _, _ = at_rel(rel)
        return remote(
            carried.at[tx * NZ + tz],
            incoming.at[slice_of(x, z)],
            sent_sem.at[S_BACK],
            back_recv.at[x],
            at_rel(rel),
        )

    def chain(g):
        @pl.when(x == g)
        def _():
            take(tiles.at[pl.ds(0, COUNT - 1)], tile_recv.at[0])
            everything = tiles[...]
            best = jnp.max(everything[:, 1, :], axis=0, keepdims=True)
            max_out[...] = jnp.max(best, axis=1, keepdims=True)
            decays = exact_dot(jnp.exp(everything[:, 0, :]), expand[:, 256 * g : 256 * g + 256])

            take(arrived.at[pl.ds(0, COUNT - 1)], st_recv.at[0])
            state = init_t[pl.ds(pl.multiple_of(z * 16, 16), 16), :]
            for n in range(COUNT):
                carried[n] = state.astype(bf16)
                if n < COUNT - 1:
                    state = decays[n : n + 1] * state + arrived[n].astype(f32)

            def send_back(rel, carry):
                back_copy(rel).start()
                return carry

            lax.fori_loop(1, COUNT, send_back, 0)
            incoming[slice_of(x, z)] = carried[here]

    def u_copy(g, b, kind, origin, where):
        ref = tokens.at[x_of(origin), pl.ds(128 * b, 128), pl.ds(256 * g, 256)]
        sem = u_recv.at[g, b] if kind == b else u_last.at[kind]
        return remote(ref, ref, sent_sem.at[S_U], sem, where)

    def finish(g):
        part = slice(256 * g, 256 * g + 256)

        @pl.when(x != g)
        def _():
            take(incoming.at[:, part], back_recv.at[g])

        @pl.when(x == g)
        def _():
            take(incoming.at[pl.ds(0, 112), part], back_recv.at[g])

        for b in range(2):
            rows_b = slice(128 * b, 128 * b + 128)
            entering = incoming[:, part]
            if b == 1:
                entering = (grown[g, 0:1, :] * entering.astype(f32) + added0[:, part]).astype(bf16)
            seen = jnp.dot(bc_act[rows_b, 128:256], entering, preferred_element_type=f32)
            total = acc[rows_b, part] + exact_dot(jnp.exp(cum_s[rows_b, :]), expand[:, part]) * seen
            tokens[x, rows_b, part] = (total * gain_ref[:, part]).astype(bf16)
            squared = total * total
            squared = squared[:, 0:128] + squared[:, 128:256]
            sq[rows_b, :] = squared if g == 0 else sq[rows_b, :] + squared
        go(u_copy(g, 0, 0, 0, at(dx=1)))
        go(u_copy(g, 1, 1, 0, at(dx=-1)))
        go(u_copy(g, 1, 0, 0, at(dx=1)))
        go(u_copy(g, 0, 1, 0, at(dx=-1)))

    def u_relay(g):
        take(tokens.at[0, pl.ds(0, 128), pl.ds(0, 256)], u_recv.at[g, 0])
        go(u_copy(g, 0, 2, -1, at(dx=1)))
        take(tokens.at[0, pl.ds(0, 128), pl.ds(0, 256)], u_recv.at[g, 1])
        go(u_copy(g, 1, 2, 1, at(dx=-1)))

    def o_copy(j, k, d):
        sign = 1 if d == 0 else -1
        rows_j = pl.ds(256 * j, 256)
        arrives = 4 if k == 3 else -sign * (k + 1)
        return remote(
            weights.at[rows_j, z_cols(-sign * k)],
            weights.at[rows_j, z_cols(arrives)],
            sent_sem.at[S_O],
            o_recv.at[d, j, k] if k < 3 else o_last.at[0],
            at(dz=sign),
        )

    def o_wave(k, pieces=(0, 1, 2, 3)):
        for j in pieces:
            for d in range(2):
                if k > 0:
                    o_copy(j, k - 1, d).wait_recv()
                if k < 3 or j // 2 == d:
                    go(o_copy(j, k, d))

    def sq_copy(n):
        dy, dc = OTHERS[n]
        there = pl.ds(pl.multiple_of(t_index(dy, dc) * 32, 32), 32)
        return remote(sq.at[there], squares.at[n], sent_sem.at[S_SQ], sq_recv.at[0], at(dy=dy, dc=dc))

    def multiply(r):
        slot = x_of(r)

        def one(n, carry):
            part = pl.ds(pl.multiple_of(n * 256, 256), 256)
            value = jnp.dot(
                tokens[slot], weights[:, part], preferred_element_type=jnp.float32
            ).astype(jnp.bfloat16)
            value = value.reshape(NY, NC, 32, 256)
            for core in range(NC):
                partial[r, core, :, :, part] = value[:, core]
            return carry

        lax.fori_loop(0, 4, one, 0)
        go(c_copy(r))

    def c_copy(r):
        other = lax.rem(c + 1, NC)
        return remote(
            partial.at[r, other], from_core.at[r], sent_sem.at[S_C], c_recv.at[r], at(dc=1)
        )

    def y_copy(r, name):
        slot, low, dst, sign = {
            TWO_UP: (2, 0, ry1.at[r], 1),
            TWO_DOWN: (2, 16, ry1.at[r], -1),
            ONE_UP_B: (1, 16, ry2.at[r, 0], 1),
            ONE_DOWN_A: (3, 0, ry2.at[r, 1], -1),
            ONE_UP_A: (1, 0, ry2.at[r, 0], 1),
            ONE_DOWN_B: (3, 16, ry2.at[r, 1], -1),
        }[name]
        return remote(
            ystage.at[r, slot, pl.ds(low, 16)],
            dst.at[pl.ds(low, 16)],
            sent_sem.at[S_Y],
            y_recv.at[r, name] if name < 2 else y_last.at[r],
            at(dy=sign),
        )

    def both_cores(r, dy):
        where = y_of(dy)
        return partial[r, c, where].astype(jnp.float32) + from_core[r, where].astype(jnp.float32)

    def y_first(r):
        take(from_core.at[r], c_recv.at[r])
        ystage[r, 2] = both_cores(r, 2).astype(jnp.bfloat16)
        value = both_cores(r, 1)
        yup[r] = value[0:16]
        ystage[r, 1, 16:32] = value[16:32].astype(jnp.bfloat16)
        go(y_copy(r, TWO_UP))
        go(y_copy(r, TWO_DOWN))
        value = both_cores(r, 3)
        ydown[r] = value[16:32]
        ystage[r, 3, 0:16] = value[0:16].astype(jnp.bfloat16)
        go(y_copy(r, ONE_UP_B))
        yown[r] = both_cores(r, 0)
        go(y_copy(r, ONE_DOWN_A))

    def y_add(r):
        y_copy(r, TWO_UP).wait_recv()
        ystage[r, 1, 0:16] = (yup[r] + ry1[r, 0:16].astype(jnp.float32)).astype(jnp.bfloat16)
        y_copy(r, TWO_DOWN).wait_recv()
        ystage[r, 3, 16:32] = (ydown[r] + ry1[r, 16:32].astype(jnp.float32)).astype(jnp.bfloat16)
        go(y_copy(r, ONE_UP_A))
        go(y_copy(r, ONE_DOWN_B))

    def y_final(r):
        take(ry2.at[r], y_last.at[r])
        value = (
            yown[r] + ry2[r, 0].astype(jnp.float32) + ry2[r, 1].astype(jnp.float32)
        ).astype(jnp.bfloat16)
        if r == 0:
            landed[x] = value
        else:
            fstage[r] = value
            go(remote(fstage.at[r], landed.at[x], sent_sem.at[S_F], f_recv.at[0], at(dx=r)))

    for r in (1, 3, 2):
        go(hx_copy(r))
    local[4].wait()
    hy_first(0)
    maps = wbc_ref[...].astype(f32)
    wbuf[0][z_rows(0), 0:128] = maps[:, 0, 0, :].astype(bf16)
    wbuf[0][z_rows(0), 128:256] = maps[:, 0, 1, :].astype(bf16)
    for_steps = jnp.concatenate([wdt_ref[...].astype(f32), jnp.zeros((112, 128), f32)], axis=0)
    wbuf[0][z_rows(0), 256:384] = jnp.transpose(for_steps).astype(bf16)
    z_step(0, 0)
    for copy in local[:4] + local[5:]:
        copy.wait()
    z_step(1, 0)
    par_ref[...] = jnp.zeros((8, 128), f32)
    par_ref[0:1, 0:16] = bias_ref[...]
    par_ref[1:2, 0:16] = decay_ref[...]
    par_ref[2:3, 0:16] = skip_ref[...]
    expand[...] = jnp.where((lane >= head * 64) & (lane < head * 64 + 64), 1.0, 0.0).astype(f32)
    init_t[...] = jnp.transpose(init_ref[pl.ds(pl.multiple_of(x * 256, 256), 256), :])
    hy_first(1)
    hy_first(3)
    z_step(0, 1)
    hy_first(2)
    z_step(1, 1)
    hy_pass(0)
    z_step(0, 2)
    hy_pass(1)
    z_step(1, 2)
    z_step(2, 0)
    hy_pass(3)
    z_step(3, 0)
    hy_pass(2)
    z_step(0, 3)
    z_step(1, 3)
    z_step(2, 1)
    z_step(4, 0)
    quantized(0)
    quantized(1)
    quantized(3)
    quantized(2)
    rs_multiply(0)
    z_step(3, 1)
    rs_multiply(1)
    z_step(2, 2)
    z_step(3, 2)
    rs_add(0)
    z_step(4, 1)
    z_step(2, 3)
    z_step(3, 3)
    rs_add(1)
    z_step(4, 2)
    rs_multiply(2)
    rs_multiply(3)
    z_step(4, 3)
    o_wave(0)
    rs_final(0)
    rs_add(2)
    rs_multiply(4)
    steps()
    rs_final(1)
    rs_add(3)
    o_wave(1, (0, 1))
    convolve(0)
    rs_final(2)
    rs_add(4)
    convolve(1)
    add_states(0)
    rs_final(3)
    convolve(2)
    add_states(1)
    rs_final(4)
    convolve(3)
    add_states(2)
    inside(0)
    convolve(4)
    add_states(3)
    o_wave(1, (2, 3))
    chain(0)
    inside(1)
    chain(1)
    inside(2)
    inside(3)
    chain(2)
    chain(3)
    o_wave(2)
    finish(0)
    finish(1)
    u_relay(0)
    o_wave(3)
    finish(2)
    u_relay(1)
    finish(3)
    take(weights.at[:, pl.ds(0, 128)], o_last.at[0])
    multiply(0)
    u_relay(2)
    y_first(0)
    u_relay(3)
    for n in range(7):
        go(sq_copy(n))
    take(tokens.at[0, pl.ds(0, 128)], u_last.at[0])
    multiply(3)
    y_add(0)
    take(tokens.at[0, pl.ds(0, 128)], u_last.at[1])
    multiply(1)
    y_first(3)
    take(tokens.at[0], u_last.at[2])
    multiply(2)
    y_first(1)
    y_add(3)
    y_first(2)
    y_add(1)
    y_final(0)
    y_add(2)
    y_final(3)
    y_final(1)

    take(squares, sq_recv.at[0])
    index = t_index(0, 0)
    total = sq[pl.ds(pl.multiple_of(index * 32, 32), 32), :]
    for n in range(7):
        total = total + squares[n]
    mean_sq = jnp.sum(total, axis=1, keepdims=True) / (HEADS * HEAD_DIM)
    scale = lax.rsqrt(mean_sq + epsilon)

    y_final(2)
    drain(rows.at[0, 0, pl.ds(0, 3)], S_HX)
    drain(rows.at[pl.ds(0, 3), 0], S_HY)
    drain(rows.at[:, 0], S_SIB)
    for j in range(5):
        drain(wbuf[j].at[pl.ds(0, 896)], S_Z + j)
    drain(stage, S_RS)
    drain(tail_out, S_HALO)
    drain(tiles.at[pl.ds(0, COUNT - 1)], S_TILE)
    drain(arrived.at[pl.ds(0, COUNT - 1)], S_ST)
    drain(arrived.at[pl.ds(0, COUNT - 1)], S_BACK)
    drain(tokens.at[pl.ds(0, 3)], S_U)
    drain(weights.at[pl.ds(0, 896)], S_O)
    drain(squares, S_SQ)
    drain(from_core, S_C)
    drain(ystage.at[:, pl.ds(0, 3)], S_Y)
    drain(fstage.at[pl.ds(0, 3)], S_F)
    take(landed.at[pl.ds(0, 3)], f_recv.at[0])
    for block in range(NX):
        for n, slot in enumerate(SLOTS):
            place = lax.rem(z + slot + NZ, NZ)
            part = pl.ds(pl.multiple_of(1024 * block + place * 128, 128), 128)
            value = landed[block, :, 128 * n : 128 * n + 128].astype(f32)
            out_ref[:, part] = (value * scale).astype(bf16)


def run_layer(*arrays):
    vmem = pl.BlockSpec(memory_space=pltpu.VMEM)
    any_place = pl.BlockSpec(memory_space=pl.ANY)
    return pl.pallas_call(
        layer,
        name="layer",
        out_shape=(
            jax.ShapeDtypeStruct((32, 4096), jnp.bfloat16),
            jax.ShapeDtypeStruct((1, 1), jnp.float32),
        ),
        in_specs=[pl.BlockSpec(memory_space=pltpu.SMEM)]
        + [any_place] * 2
        + [vmem] * 11
        + [any_place],
        out_specs=(vmem, vmem),
        scratch_shapes=scratch(),
        compiler_params=pltpu.CompilerParams(
            collective_id=0, has_side_effects=True, vmem_limit_bytes=60 * 2**20
        ),
    )(*arrays)


def local(
    hidden_in,
    prev_amax,
    w_x,
    w_bc,
    w_dt,
    conv_x,
    conv_bc,
    conv_state_x,
    conv_state_bc,
    dt_bias,
    decay_rate,
    skip,
    init_state,
    norm_gain,
    w_out,
):
    heads = w_dt.shape[1]
    layer_out, largest = run_layer(
        jnp.reshape(prev_amax, (1,)),
        hidden_in,
        w_x,
        w_bc,
        jnp.transpose(w_dt),
        conv_x,
        conv_bc,
        conv_state_x,
        conv_state_bc,
        jnp.reshape(dt_bias, (1, heads)),
        jnp.reshape(decay_rate, (1, heads)),
        jnp.reshape(skip, (1, heads)),
        jnp.reshape(init_state, (heads * HEAD_DIM, STATE)),
        jnp.reshape(norm_gain, (1, -1)),
        w_out,
    )
    return (layer_out, largest[0, 0])


def solution(mesh):
    finer = Mesh(mesh.devices.reshape(NX, NZ, NY, NC), SEQ_TENSOR)
    return jax.shard_map(
        local,
        mesh=finer,
        in_specs=(
            P(SEQ_TENSOR, None),
            P(),
            P(SEQ, TENSOR),
            P(SEQ, TENSOR, None, None),
            P(SEQ, TENSOR),
            P(None, TENSOR),
            P(None, TENSOR, None, None),
            P(None, TENSOR),
            P(None, TENSOR, None, None),
            P(TENSOR),
            P(TENSOR),
            P(TENSOR),
            P(TENSOR, None, None),
            P(TENSOR),
            P(TENSOR, SEQ),
        ),
        out_specs=(P(SEQ_TENSOR, None), P()),
        check_vma=False,
    )
```
